32 devices in a mesh: mem: 4 (over x, core), gx: 4 (over z), gy: 2 (over y).
Axes of the slice: x: 2, y: 2, z: 4, core: 2. Of those that a mesh axis runs over, the one named last changes fastest.
Arguments:
- prior_sample_set: float32 [256, 2, 32, 256], P('mem', None, 'gx', 'gy'), may hold values from -6 to 6
- flow_speeds: float32 [2, 2, 32, 256], P(None, None, 'gx', 'gy'), may hold values from -0.6 to 0.6
- observed_cells: int32 [4, 2, 4, 1, 128], P('gx', 'gy', 'mem'), may hold values from 0 to 511
- observed_values: float32 [4, 2, 4, 1, 128], P('gx', 'gy', 'mem'), may hold values from -6 to 6
- error_variance: float32 [4, 2, 4, 1, 128], P('gx', 'gy', 'mem'), may hold values from 0.5 to 4
Outputs:
- analysis: bfloat16 [256, 2, 32, 256], P('mem', None, 'gx', 'gy')
The draws below stay inside these ranges and needn't reach their ends.
All inputs are finite; a program needn't handle non-finite values.
Results may differ from the reference program's by a relative error of at most 0.001.
The reference program's roundings to bfloat16 on the way count: a program that leaves them out, or rounds other values in their place, can miss the bound.
Values may be sent and summed in bfloat16 or wider, within the bound.
No kernel may reach another device: no remote copies, remote signals or barrier semaphores. Data moves between devices by JAX's collectives and lax.ppermute only.
A program may use at most 64 MiB of HBM per device.

```python
import math
import jax
import jax.numpy as jnp
from jax import lax

MEMBERS = 256
LAYERS = 2
RK_STEPS = 1
ROOT_STEPS = 4
PATCH = 256
OBS_PATCH = 128
STRIP = 1
NX = 32
NY = 256
PATCHES = 1
N_MEM = 4
N_GX = 4
N_GY = 2


def plant(drawn, own_key, least, largest):
    extent = drawn.shape
    place = [jax.random.randint(jax.random.fold_in(own_key, axis), (), 0, extent[axis]) for axis in range(len(extent))]
    drawn = drawn.at[tuple(place)].set(least)
    longest = extent.index(max(extent))
    place[longest] = (place[longest] + 1) % extent[longest]
    return drawn.at[tuple(place)].set(largest)


def shard_levels(key, dims, shards, low, high):
    level, own = 1.0, jax.random.fold_in(key, 6)
    for axis_at, parts in shards:
        draws = jnp.exp(jax.random.uniform(jax.random.fold_in(own, axis_at), (parts,), jnp.float32, low / len(shards), high / len(shards)))
        level = level * jnp.repeat(draws, dims[axis_at] // parts).reshape([-1 if axis == axis_at else 1 for axis in range(len(dims))])
    return level


def scatter_about(key, extent, scale, bound, pieces=(), kind=jnp.bfloat16):
    factor_of = shard_levels(key, extent, pieces, -0.22, 0.18) if pieces else 1.0
    drawn = jax.random.normal(key, extent, jnp.float32) * scale * factor_of
    return jnp.minimum(jnp.maximum(drawn, -bound), bound).astype(kind)


def setup_inputs(seed: int = 0) -> dict:
    keys = jax.random.split(jax.random.key(seed), 6)
    return {
        "prior_sample_set": scatter_about(keys[0], (MEMBERS, LAYERS, NX, NY), 1.0, 6.0, ((0, 4), (2, 4), (3, 2)), jnp.float32),
        "flow_speeds": jnp.clip(jax.random.uniform(keys[1], (2, LAYERS, NX, NY), jnp.float32, -0.6, 0.6) * shard_levels(keys[1], (2, LAYERS, NX, NY), ((2, 4), (3, 2)), -0.4, 0.0), -0.6, 0.6),
        "observed_cells": plant(jax.random.randint(keys[2], (N_GX, N_GY, N_MEM, PATCHES, OBS_PATCH), 0, LAYERS * STRIP * PATCH), jax.random.fold_in(keys[2], 1), 0, (LAYERS * STRIP * PATCH) - 1).astype(jnp.int32),
        "observed_values": scatter_about(keys[3], (N_GX, N_GY, N_MEM, PATCHES, OBS_PATCH), 1.0, 6.0, ((0, 4), (1, 2), (2, 4)), jnp.float32),
        "error_variance": jnp.clip(jnp.exp(math.log(4.0) - 2.0794415 * jax.random.uniform(keys[4], (N_GX, N_GY, N_MEM, PATCHES, OBS_PATCH), jnp.float32) ** shard_levels(keys[4], (N_GX, N_GY, N_MEM, PATCHES, OBS_PATCH), ((0, 4), (1, 2), (2, 4)), -0.2, 0.2)), 0.5, 4.0),
    }


diffusion = 0.1
coupling = 0.2

def tendency(model_mesh_field, wind_x, wind_y):
    centre = model_mesh_field[:, :, 1:-1, 1:-1]
    north = model_mesh_field[:, :, 2:, 1:-1]
    south = model_mesh_field[:, :, :-2, 1:-1]
    east = model_mesh_field[:, :, 1:-1, 2:]
    west = model_mesh_field[:, :, 1:-1, :-2]
    layer_mean = lax.optimization_barrier(jnp.mean(centre, axis=1, keepdims=True))
    return -0.5 * wind_x * (north - south) - 0.5 * wind_y * (east - west) + diffusion * (north + south + east + west - 4.0 * centre) + coupling * (layer_mean - centre)

def wrap_section(model_mesh_field, flow_speeds):
    padded = jnp.pad(model_mesh_field, ((0, 0), (0, 0), (1, 1), (1, 1)), mode='wrap')
    return tendency(padded, flow_speeds[0], flow_speeds[1])

def wrap_step(model_mesh_field, flow_speeds):
    section_one = wrap_section(model_mesh_field, flow_speeds)
    section_two = wrap_section(model_mesh_field + 0.5 * section_one, flow_speeds)
    section_three = wrap_section(model_mesh_field + 0.5 * section_two, flow_speeds)
    section_four = wrap_section(model_mesh_field + section_three, flow_speeds)
    return model_mesh_field + (section_one + 2.0 * section_two + 2.0 * section_three + section_four) / 6.0

def advance_one_realization(realization_vector, flow_speeds):
    model_mesh_field = realization_vector[None]
    for step in range(RK_STEPS):
        model_mesh_field = wrap_step(model_mesh_field, flow_speeds)
    return model_mesh_field[0].astype(jnp.bfloat16)

def transform_exact(weights, rolled):
    return jnp.einsum('qik,ilsqc->klsqc', weights.astype(jnp.float32), rolled.astype(jnp.float32), precision=lax.Precision.HIGHEST)

def analyze(strip_block, cells, values, errors, transform):
    realization_vectors, layer_stack, rows, width = strip_block.shape
    patches, count = cells.shape
    patch = width // patches
    highest = lax.Precision.HIGHEST
    mean_field = lax.optimization_barrier(jnp.mean(strip_block, axis=0, dtype=jnp.float32))
    layer_of = cells // (rows * patch)
    row_of = cells // patch % rows
    column = cells % patch
    starts = (jnp.arange(patches, dtype=jnp.int32) * patch)[:, None]
    flat_index = (layer_of * (rows * width) + row_of * width + starts + column).astype(jnp.int32)
    picked = jnp.take(strip_block.reshape(realization_vectors, layer_stack * rows * width), flat_index.reshape(-1), axis=1)
    base = jnp.take(mean_field.reshape(-1), flat_index.reshape(-1)).reshape(patches, count)
    spread = picked.astype(jnp.float32).reshape(realization_vectors, patches, count) - base[None]
    innovation = values - base
    offset = column.astype(jnp.float32) - 0.5 * (patch - 1)
    spread_parts = []
    innovation_parts = []
    for shift in (-1, 0, 1):
        distance = (shift * patch + jnp.roll(offset, -shift, axis=0)) / patch
        scale = jnp.sqrt(jnp.exp(-0.5 * distance * distance) / jnp.roll(errors, -shift, axis=0))
        spread_parts.append(jnp.roll(spread, -shift, axis=1) * scale[None])
        innovation_parts.append(jnp.roll(innovation, -shift, axis=0) * scale)
    scaled = jnp.concatenate(spread_parts, axis=2)
    scaled_innovation = jnp.concatenate(innovation_parts, axis=1)
    identity = jnp.eye(realization_vectors, dtype=jnp.float32)
    gram = jnp.einsum('kpj,ipj->pki', scaled, scaled, precision=highest) + (realization_vectors - 1.0) * identity
    frob = jnp.sqrt(lax.optimization_barrier(jnp.sum(gram * gram, axis=(1, 2))))
    current = gram / frob[:, None, None]
    root = jnp.broadcast_to(identity, gram.shape)
    for step in range(ROOT_STEPS):
        middle = 1.5 * identity - 0.5 * jnp.einsum('pab,pbc->pac', root, current, precision=highest)
        current = jnp.einsum('pab,pbc->pac', current, middle, precision=highest)
        root = jnp.einsum('pab,pbc->pac', middle, root, precision=highest)
    projected = jnp.einsum('kpj,pj->pk', scaled, scaled_innovation, precision=highest)
    once = jnp.einsum('pab,pb->pa', root, projected, precision=highest)
    twice = jnp.einsum('pab,pb->pa', root, once, precision=highest)
    mean_weights = twice / frob[:, None]
    weights = (jnp.sqrt(realization_vectors - 1.0) * root / jnp.sqrt(frob)[:, None, None] + mean_weights[:, :, None]).astype(jnp.bfloat16)
    perturbation = (strip_block - mean_field[None]).astype(jnp.bfloat16)
    rolled = jnp.roll(perturbation, -(patch // 2), axis=3).reshape(realization_vectors, layer_stack, rows, patches, patch)
    first = transform(weights, rolled)
    second = transform(jnp.roll(weights, -1, axis=0), rolled)
    position = (jnp.arange(patch, dtype=jnp.float32) + 0.5) / patch
    increment = ((1.0 - position) * first + position * second).reshape(realization_vectors, layer_stack, rows, width)
    return (jnp.roll(increment, patch // 2, axis=3) + mean_field[None]).astype(jnp.bfloat16)

def reference(prior_sample_set, flow_speeds, observed_cells, observed_values, error_variance):
    realization_vectors = lax.map(lambda lone_element: advance_one_realization(lone_element, flow_speeds), prior_sample_set)
    strips = realization_vectors.reshape(MEMBERS, LAYERS, NX // STRIP, STRIP, NY).transpose(2, 0, 1, 3, 4)
    cells = observed_cells.reshape(NX // STRIP, PATCHES, OBS_PATCH)
    values = observed_values.reshape(NX // STRIP, PATCHES, OBS_PATCH)
    errors = error_variance.reshape(NX // STRIP, PATCHES, OBS_PATCH)

    def one_strip(items):
        return analyze(items[0], items[1], items[2], items[3], transform_exact)
    result = lax.map(one_strip, (strips, cells, values, errors))
    return result.transpose(1, 2, 0, 3, 4).reshape(MEMBERS, LAYERS, NX, NY)
```

```python
import functools
import math

import jax
import jax.numpy as jnp
from jax import lax
from jax.experimental import pallas as pl
from jax.experimental.pallas import tpu as pltpu
from jax.sharding import PartitionSpec as P

ROOT_STEPS = 4


diffusion = 0.1
coupling = 0.2


def with_halo(block, sides, width):
    for axis, dim in sides:
        count = lax.axis_size(axis)
        forward = [(i, i + 1) for i in range(count - 1)]
        forward.append((count - 1, 0))
        backward = [(target, source) for source, target in forward]
        low = lax.ppermute(
            lax.slice_in_dim(block, block.shape[dim] - width, None, axis=dim), axis, forward
        )
        high = lax.ppermute(lax.slice_in_dim(block, 0, width, axis=dim), axis, backward)
        block = jnp.concatenate([low, block, high], axis=dim)
    return block


def tendency(model_mesh_field, wind_x, wind_y):
    centre = model_mesh_field[:, :, 1:-1, 1:-1]
    north = model_mesh_field[:, :, 2:, 1:-1]
    south = model_mesh_field[:, :, :-2, 1:-1]
    east = model_mesh_field[:, :, 1:-1, 2:]
    west = model_mesh_field[:, :, 1:-1, :-2]
    layer_mean = jnp.mean(centre, axis=1, keepdims=True)
    return (
        -0.5 * wind_x * (north - south)
        - 0.5 * wind_y * (east - west)
        + diffusion * (north + south + east + west - 4.0 * centre)
        + coupling * (layer_mean - centre)
    )


def crop_margin(array, width):
    return array[:, :, width : array.shape[2] - width, width : array.shape[3] - width]


def deep_step(model_mesh_field, wind_pad):
    padded = with_halo(model_mesh_field, (("gx", 2), ("gy", 3)), 4)
    wind_three = crop_margin(wind_pad, 1)
    wind_two = crop_margin(wind_pad, 2)
    wind_one = crop_margin(wind_pad, 3)
    wind_zero = crop_margin(wind_pad, 4)
    section_one = tendency(padded, wind_three[0], wind_three[1])
    section_two = tendency(crop_margin(padded, 1) + 0.5 * section_one, wind_two[0], wind_two[1])
    section_three = tendency(crop_margin(padded, 2) + 0.5 * section_two, wind_one[0], wind_one[1])
    section_four = tendency(crop_margin(padded, 3) + section_three, wind_zero[0], wind_zero[1])
    return (
        crop_margin(padded, 4)
        + (
            crop_margin(section_one, 3)
            + 2.0 * crop_margin(section_two, 2)
            + 2.0 * crop_margin(section_three, 1)
            + section_four
        )
        / 6.0
    )


def transform_device(weights, rolled):
    return jnp.einsum("qik,ilsqc->klsqc", weights, rolled, preferred_element_type=jnp.float32)


def analyze(strip_block, cells, values, errors, transform):
    realization_vectors, layer_stack, rows, width = strip_block.shape
    patches, count = cells.shape
    patch = width // patches
    highest = lax.Precision.HIGHEST
    mean_field = jnp.mean(strip_block, axis=0, dtype=jnp.float32)
    layer_of = cells // (rows * patch)
    row_of = cells // patch % rows
    column = cells % patch
    starts = (jnp.arange(patches, dtype=jnp.int32) * patch)[:, None]
    flat_index = layer_of * (rows * width) + row_of * width + starts + column
    picked = jnp.take(
        strip_block.reshape(realization_vectors, layer_stack * rows * width),
        flat_index.reshape(-1),
        axis=1,
    )
    base = jnp.take(mean_field.reshape(-1), flat_index.reshape(-1)).reshape(patches, count)
    spread = picked.astype(jnp.float32).reshape(realization_vectors, patches, count) - base[None]
    innovation = values - base
    offset = column.astype(jnp.float32) - 0.5 * (patch - 1)
    spread_parts = []
    innovation_parts = []
    for shift in (-1, 0, 1):
        distance = (shift * patch + jnp.roll(offset, -shift, axis=0)) / patch
        scale = jnp.sqrt(jnp.exp(-0.5 * distance * distance) / jnp.roll(errors, -shift, axis=0))
        spread_parts.append(jnp.roll(spread, -shift, axis=1) * scale[None])
        innovation_parts.append(jnp.roll(innovation, -shift, axis=0) * scale)
    scaled = jnp.concatenate(spread_parts, axis=2)
    scaled_innovation = jnp.concatenate(innovation_parts, axis=1)
    identity = jnp.eye(realization_vectors, dtype=jnp.float32)
    gram = (
        jnp.einsum("kpj,ipj->pki", scaled, scaled, precision=highest)
        + (realization_vectors - 1.0) * identity
    )
    frob = jnp.sqrt(jnp.sum(gram * gram, axis=(1, 2)))
    current = gram / frob[:, None, None]
    root = jnp.broadcast_to(identity, gram.shape)
    for step in range(ROOT_STEPS):
        middle = 1.5 * identity - 0.5 * jnp.einsum("pab,pbc->pac", root, current, precision=highest)
        current = jnp.einsum("pab,pbc->pac", current, middle, precision=highest)
        root = jnp.einsum("pab,pbc->pac", middle, root, precision=highest)
    projected = jnp.einsum("kpj,pj->pk", scaled, scaled_innovation, precision=highest)
    once = jnp.einsum("pab,pb->pa", root, projected, precision=highest)
    twice = jnp.einsum("pab,pb->pa", root, once, precision=highest)
    mean_weights = twice / frob[:, None]
    weights = (
        jnp.sqrt(realization_vectors - 1.0) * root / jnp.sqrt(frob)[:, None, None]
        + mean_weights[:, :, None]
    ).astype(jnp.bfloat16)
    perturbation = (strip_block - mean_field[None]).astype(jnp.bfloat16)
    rolled = jnp.roll(perturbation, -(patch // 2), axis=3).reshape(
        realization_vectors, layer_stack, rows, patches, patch
    )
    first = transform(weights, rolled)
    second = transform(jnp.roll(weights, -1, axis=0), rolled)
    position = (jnp.arange(patch, dtype=jnp.float32) + 0.5) / patch
    increment = ((1.0 - position) * first + position * second).reshape(
        realization_vectors, layer_stack, rows, width
    )
    return (jnp.roll(increment, patch // 2, axis=3) + mean_field[None]).astype(jnp.bfloat16)


def on_device_general(prior_sample_set, flow_speeds, observed_cells, observed_values, error_variance):
    member_group_count = lax.axis_size("mem")
    northward_group_count = lax.axis_size("gy")
    local_member_states, layer_stack, rows_x, column_count_north = prior_sample_set.shape
    band_row_count = rows_x // (member_group_count * northward_group_count)
    all_members = local_member_states * member_group_count
    model_mesh_field = prior_sample_set
    wind_pad = with_halo(flow_speeds, (("gx", 2), ("gy", 3)), 4)
    model_mesh_field = deep_step(model_mesh_field, wind_pad)
    advance_sample_set = model_mesh_field.astype(jnp.bfloat16)
    flattened_realizations = advance_sample_set.reshape(
        local_member_states,
        layer_stack,
        northward_group_count,
        member_group_count,
        band_row_count,
        column_count_north,
    )
    flattened_realizations = flattened_realizations.transpose(3, 2, 0, 1, 4, 5).reshape(
        member_group_count * northward_group_count,
        local_member_states,
        layer_stack,
        band_row_count,
        column_count_north,
    )
    received = lax.all_to_all(
        flattened_realizations, ("mem", "gy"), split_axis=0, concat_axis=0, tiled=True
    )
    received = received.reshape(
        member_group_count,
        northward_group_count,
        local_member_states,
        layer_stack,
        band_row_count,
        column_count_north,
    )
    columns = received.transpose(0, 2, 3, 4, 1, 5).reshape(
        all_members, layer_stack, band_row_count, northward_group_count * column_count_north
    )
    cells = observed_cells.reshape(observed_cells.shape[-2], observed_cells.shape[-1])
    values = observed_values.reshape(observed_values.shape[-2], observed_values.shape[-1])
    errors = error_variance.reshape(error_variance.shape[-2], error_variance.shape[-1])
    analysed = analyze(columns, cells, values, errors, transform_device)
    outgoing = analysed.reshape(
        member_group_count,
        local_member_states,
        layer_stack,
        band_row_count,
        northward_group_count,
        column_count_north,
    )
    outgoing = outgoing.transpose(0, 4, 1, 2, 3, 5).reshape(
        member_group_count * northward_group_count,
        local_member_states,
        layer_stack,
        band_row_count,
        column_count_north,
    )
    returned = lax.all_to_all(outgoing, ("mem", "gy"), split_axis=0, concat_axis=0, tiled=True)
    returned = returned.reshape(
        member_group_count,
        northward_group_count,
        local_member_states,
        layer_stack,
        band_row_count,
        column_count_north,
    )
    return returned.transpose(2, 3, 1, 0, 4, 5).reshape(
        local_member_states, layer_stack, rows_x, column_count_north
    )


LANES = 128
HALO = 4
OCTET = 8
GROUP = 32
PACK = LANES // GROUP
STAGE_FACTORS = (1.0 / 4.0, 1.0 / 3.0, 1.0 / 2.0, 1.0)


def lane_iota(shape):
    return lax.broadcasted_iota(jnp.int32, shape, len(shape) - 1)


def lane_roll(x, shift):
    shift = shift % LANES
    return x if shift == 0 else pltpu.roll(x, shift, 1)


def split_two(x):
    high = x.astype(jnp.bfloat16)
    return high, (x - high.astype(jnp.float32)).astype(jnp.bfloat16)


def split_three(x):
    high, rest = x.astype(jnp.bfloat16), None
    rest = x - high.astype(jnp.float32)
    middle = rest.astype(jnp.bfloat16)
    low = (rest - middle.astype(jnp.float32)).astype(jnp.bfloat16)
    return high, middle, low


def tile_row(odd, j):
    return jnp.where(odd == 1, 11 - j, j - HALO)


class Sizes:
    def __init__(self, local, layers, rows):
        self.local = local
        self.layers = layers
        self.rows = rows
        self.members = 2 * local
        self.octets = self.members // OCTET
        self.packs = self.octets // PACK
        self.per_member = layers * rows
        self.halo_rows = layers * (HALO + 1) * self.members
        self.wind_rows = 2 * layers * HALO


def member_rows(s, odd, own_ref, sib_ref, octet, layer, j):
    half = s.octets // 2
    start = layer * s.rows + tile_row(odd, j)
    if isinstance(octet, int):
        ref = own_ref if octet < half else sib_ref
        return ref[pl.ds((octet % half) * OCTET * s.per_member + start, OCTET, stride=s.per_member), :]
    raise ValueError("octet")


def pack_halo_kernel(s, own_ref, sib_ref, wind_ref, out_ref, wind_rows_ref):
    odd = lax.rem(lax.axis_index("mem"), 2)
    for layer in range(s.layers):
        for j in range(HALO):
            base = (layer * (HALO + 1) + HALO - j) * s.members
            for pair in range(s.octets // 2):
                value = jnp.concatenate(
                    [member_rows(s, odd, own_ref, sib_ref, 2 * pair + k, layer, 2 * HALO + j) for k in range(2)], axis=0
                )
                high, low = split_two(value)
                out_ref[pl.ds(base + pair * 16, 16), :] = high
                if j == HALO - 1:
                    out_ref[pl.ds(layer * (HALO + 1) * s.members + pair * 16, 16), :] = low
    copy_wind_rows(s, odd, wind_ref, wind_rows_ref)
    for i, part in enumerate(split_three(wind_rows_ref[...])):
        out_ref[pl.ds(s.halo_rows + i * s.wind_rows, s.wind_rows), :] = part


def copy_wind_rows(s, odd, from_ref, to_ref):
    for block in range(2 * s.layers):
        for j in range(HALO):
            row = block * s.rows + tile_row(odd, 2 * HALO + j)
            to_ref[pl.ds(block * HALO + j, 1), :] = from_ref[pl.ds(row, 1), :]


def to_strip(x_of):
    total = None
    for q in range(PACK):
        x = x_of(q)
        lane = lane_iota(x.shape)
        first = lane_roll(x, HALO + GROUP * q)
        last = lane_roll(x, 16 + GROUP * q - (LANES - 12))
        at = lane - GROUP * q
        if total is None:
            total = jnp.zeros_like(x)
        total = jnp.where((at >= HALO) & (at < 16), first, total)
        total = jnp.where((at >= 16) & (at < 28), last, total)
    return total


def to_edges(strip, k, total):
    lane = jnp.bitwise_and(lane_iota(strip.shape) + HALO - 8 * k, GROUP - 1)
    low = lane_roll(strip, 8 * k - 24)
    high = lane_roll(strip, 24 + 8 * k)
    both = jnp.where(lane < HALO, high, low)
    return jnp.where(lane < 2 * HALO, both, total)


def with_edges(strip, edges, k):
    lane = jnp.bitwise_and(lane_iota(strip.shape) + HALO, GROUP - 1)
    return jnp.where(lane < 2 * HALO, lane_roll(edges, -8 * k), strip)


def pack_edges_kernel(s, own_ref, sib_ref, wind_ref, strip_ref, side_ref, corner_ref, wind_strip_ref, rows_ref):
    odd = lax.rem(lax.axis_index("mem"), 2)
    size = OCTET
    for layer in range(s.layers):
        for block in range(2):
            for p in range(s.packs):
                total = jnp.zeros((size, LANES), jnp.float32)
                for k in range(HALO):
                    j = HALO + block * HALO + k
                    strip = to_strip(lambda q: member_rows(s, odd, own_ref, sib_ref, PACK * p + q, layer, j))
                    strip_ref[pl.ds(((layer * 2 * HALO + j - HALO) * s.packs + p) * size, size), :] = strip
                    total = to_edges(strip, k, total)
                side_ref[pl.ds(((layer * 2 + block) * s.packs + p) * size, size), :] = total
    base = s.layers * 2 * s.packs * size
    for block in range(2 * s.layers):
        value = wind_ref[pl.ds(block * s.rows, s.rows), :]
        strip = to_strip(lambda q: value)
        wind_strip_ref[pl.ds(block * s.rows, s.rows), :] = strip
        side_ref[pl.ds(base + block * s.rows, s.rows), :] = to_edges(strip, 0, jnp.zeros_like(strip))
    for layer in range(s.layers):
        rows = s.packs * size
        corner_ref[pl.ds(layer * rows, rows), :] = side_ref[pl.ds((layer * 2 + 1) * rows, rows), :].astype(jnp.bfloat16)
    for block in range(2 * s.layers):
        for j in range(HALO):
            row = base + block * s.rows + tile_row(odd, 2 * HALO + j)
            rows_ref[pl.ds(block * HALO + j, 1), :] = side_ref[pl.ds(row, 1), :]
    for i, part in enumerate(split_three(rows_ref[...])):
        corner_ref[pl.ds(s.layers * s.packs * size + i * s.wind_rows, s.wind_rows), :] = part


def coefficients(store, wind_x, wind_y):
    for stage, factor in enumerate(STAGE_FACTORS):
        values = (0.1 - 0.5 * wind_x, 0.1 + 0.5 * wind_x, 0.1 - 0.5 * wind_y, 0.1 + 0.5 * wind_y)
        for kind, value in enumerate(values):
            store(stage * 4 + kind, value * factor)


def stages(s, field, row_of, shape):
    current = field
    for stage, factor in enumerate(STAGE_FACTORS):
        low, high = stage + 1, 3 * HALO - 1 - stage
        following = {}
        for j in range(low, high):
            if stage == len(STAGE_FACTORS) - 1 and not HALO <= j < 2 * HALO:
                continue
            for layer in range(s.layers):
                centre = current[layer, j]
                others = sum(current[k, j] for k in range(s.layers) if k != layer)
                north, south, east, west = (row_of(stage * 4 + kind, layer, j, shape) for kind in range(4))
                share = 0.2 / s.layers
                total = north * current[layer, j + 1] + south * current[layer, j - 1]
                total = total + east * lane_roll(centre, -1) + west * lane_roll(centre, 1)
                total = total + (factor * (share - 0.6)) * centre + (factor * share) * others
                following[layer, j] = field[layer, j] + total
        current = following
    return current


def forecast_kernel(
    s, own_ref, sib_ref, wind_ref, wind_strip_ref, strip_ref, halo_ref, side_ref, corner_ref,
    out0_ref, out1_ref, out2_ref, out3_ref,
    wide_ref, cut_ref, main_coef_ref, strip_coef_ref, halo32_ref, halo_strip_ref, edge_ref,
):
    mem = lax.axis_index("mem")
    odd = lax.rem(mem, 2)
    place = (mem // 2) * 2 + lax.axis_index("gy")
    size = OCTET
    span = 16

    def three(ref, base, rows):
        return sum(ref[pl.ds(base + i * rows, rows), :].astype(jnp.float32) for i in range(3))

    near = three(halo_ref, s.halo_rows, s.wind_rows)
    corner = three(corner_ref, s.layers * s.packs * size, s.wind_rows)
    near_strip = with_edges(to_strip(lambda q: near), corner, 0)
    base = s.layers * 2 * s.packs * size
    wide_ref[...] = jnp.zeros_like(wide_ref)
    cut_ref[...] = jnp.zeros_like(cut_ref)
    for block in range(2 * s.layers):
        at = block * span
        wide_ref[pl.ds(at, HALO), :] = near[block * HALO : (block + 1) * HALO]
        cut_ref[pl.ds(at, HALO), :] = near_strip[block * HALO : (block + 1) * HALO]
        for j in range(HALO, 3 * HALO):
            row = block * s.rows + tile_row(odd, j)
            wide_ref[pl.ds(at + j, 1), :] = wind_ref[pl.ds(row, 1), :]
            cut_ref[pl.ds(at + j, 1), :] = with_edges(
                wind_strip_ref[pl.ds(row, 1), :], side_ref[pl.ds(base + row, 1), :], 0
            )
    sign = jnp.where(odd == 1, -1.0, 1.0)
    half = s.layers * span
    for from_ref, to_ref in ((wide_ref, main_coef_ref), (cut_ref, strip_coef_ref)):
        def store(index, value):
            to_ref[pl.ds(index * half, half), :] = value

        coefficients(store, sign * from_ref[pl.ds(0, half), :], from_ref[pl.ds(half, half), :])

    for layer in range(s.layers):
        for j in range(HALO):
            at = (layer * (HALO + 1) + HALO - j) * s.members
            value = halo_ref[pl.ds(at, s.members), :].astype(jnp.float32)
            if j == HALO - 1:
                value = value + halo_ref[pl.ds(layer * (HALO + 1) * s.members, s.members), :].astype(jnp.float32)
            halo32_ref[pl.ds((layer * HALO + j) * s.members, s.members), :] = value

    def row_from(ref):
        def row_of(index, layer, j, shape):
            return jnp.broadcast_to(ref[pl.ds(index * half + layer * span + j, 1), :], shape)

        return row_of

    def halo_octet(layer, j, octet):
        return halo32_ref[pl.ds((layer * HALO + j) * s.members + octet * size, size), :]

    shape = (size, LANES)
    for layer in range(s.layers):
        for p in range(s.packs):
            edges = corner_ref[pl.ds((layer * s.packs + p) * size, size), :].astype(jnp.float32)
            for j in range(HALO):
                strip = with_edges(to_strip(lambda q: halo_octet(layer, j, PACK * p + q)), edges, j)
                halo_strip_ref[pl.ds(((layer * HALO + j) * s.packs + p) * size, size), :] = strip

    def strip_step(p, carry):
        field = {}
        for layer in range(s.layers):
            for j in range(HALO):
                at = pl.multiple_of(((layer * HALO + j) * s.packs + p) * size, size)
                field[layer, j] = halo_strip_ref[pl.ds(at, size), :]
            for block in range(2):
                at = pl.multiple_of(((layer * 2 + block) * s.packs + p) * size, size)
                edges = side_ref[pl.ds(at, size), :]
                for k in range(HALO):
                    j = HALO + block * HALO + k
                    at = pl.multiple_of(((layer * 2 * HALO + j - HALO) * s.packs + p) * size, size)
                    field[layer, j] = with_edges(strip_ref[pl.ds(at, size), :], edges, k)
        result = stages(s, field, row_from(strip_coef_ref), shape)
        for layer in range(s.layers):
            for t in range(HALO):
                at = pl.multiple_of(((layer * HALO + t) * s.packs + p) * size, size)
                edge_ref[pl.ds(at, size), :] = result[layer, HALO + t]
        return carry

    lax.fori_loop(0, s.packs, strip_step, 0)

    swap_one = jnp.bitwise_and(place, 1) == 1
    swap_two = place >= 2
    lane = lane_iota(shape)
    outs = (out0_ref, out1_ref, out2_ref, out3_ref)

    def octet_result(ref, within, octet, q):
        field = {}
        for layer in range(s.layers):
            for j in range(HALO):
                at = pl.multiple_of((layer * HALO + j) * s.members + octet * size, size)
                field[layer, j] = halo32_ref[pl.ds(at, size), :]
            for j in range(HALO, 3 * HALO):
                start = within * size * s.per_member + layer * s.rows + tile_row(odd, j)
                field[layer, j] = ref[pl.ds(start, size, stride=s.per_member), :]
        result = stages(s, field, row_from(main_coef_ref), shape)
        for layer in range(s.layers):
            for t in range(HALO):
                at = pl.multiple_of(((layer * HALO + t) * s.packs + octet // PACK) * size, size)
                edge = edge_ref[pl.ds(at, size), :]
                first = lane_roll(edge, -(GROUP * q + HALO))
                last = lane_roll(edge, LANES - HALO - 24 - GROUP * q)
                value = jnp.where(lane < HALO, first, result[layer, HALO + t])
                result[layer, HALO + t] = jnp.where(lane >= LANES - HALO, last, value)
        return result

    half_packs = s.packs // 2
    for which, ref in enumerate((own_ref, sib_ref)):
        def main_step(i, carry):
            for pair in range(PACK // 2):
                parts = []
                for k in range(2):
                    q = 2 * pair + k
                    within = i * PACK + q
                    octet = (which * half_packs + i) * PACK + q
                    parts.append(octet_result(ref, within, octet, q))
                at = pl.multiple_of(((which * half_packs + i) * PACK + 2 * pair) * size, 2 * size)
                for layer in range(s.layers):
                    rows = [
                        jnp.concatenate([part[layer, HALO + t] for part in parts], axis=0).astype(jnp.bfloat16)
                        for t in range(HALO)
                    ]
                    rows = [jnp.where(swap_one, rows[t ^ 1], rows[t]) for t in range(HALO)]
                    rows = [jnp.where(swap_two, rows[t ^ 2], rows[t]) for t in range(HALO)]
                    for d, out_ref in enumerate(outs):
                        out_ref[layer, pl.ds(at, 2 * size), :] = rows[d]
            return carry

        lax.fori_loop(0, half_packs, main_step, 0)


def dot(a, b, contract):
    return lax.dot_general(a, b, ((contract[0], contract[1]), ((), ())), preferred_element_type=jnp.float32)


def dot_three(a, b, contract=((1,), (0,))):
    (a_high, a_low), (b_high, b_low) = a, b
    return dot(a_high, b_low, contract) + dot(a_low, b_high, contract) + dot(a_high, b_high, contract)


def analysis_kernel(s, total_members, piece0_ref, piece1_ref, piece2_ref, piece3_ref, obs_ref, out_ref):
    mem, side = lax.axis_index("mem"), lax.axis_index("gy")
    me = mem * 2 + side
    pieces = (piece0_ref, piece1_ref, piece2_ref, piece3_ref)
    width = 2 * LANES
    cells_total = s.layers * width
    inverse = 1.0 / total_members
    members = jnp.concatenate(
        [
            jnp.concatenate([pieces[2 * dx + dy][layer] for layer in range(s.layers) for dy in range(2)], axis=1)
            for dx in range(2)
        ],
        axis=0,
    )
    ones = jnp.ones((OCTET, total_members), jnp.bfloat16)
    mean = dot(ones, members, ((1,), (0,)))[0:1] * inverse
    perturbation = (members.astype(jnp.float32) - mean).astype(jnp.bfloat16)

    cells = obs_ref[0:1, :].astype(jnp.int32)
    values, errors = obs_ref[1:2, :], obs_ref[2:3, :]
    column = jnp.bitwise_and(cells, width - 1)
    layer_of = cells // width
    half = jnp.bitwise_xor(column // LANES, side)
    index = layer_of * width + half * LANES + jnp.bitwise_and(column, LANES - 1)
    chosen = lax.broadcasted_iota(jnp.int32, (cells_total, cells.shape[1]), 0) == index
    picked = dot(members, chosen.astype(jnp.bfloat16), ((1,), (0,)))
    base = jnp.sum(picked, axis=0, keepdims=True) * inverse
    offset = column.astype(jnp.float32) - 0.5 * (width - 1)
    weight = jnp.zeros_like(values)
    for shift in (-1, 0, 1):
        distance = (shift * width + offset) / width
        weight = weight + jnp.exp(-0.5 * distance * distance) / errors
    scale = jnp.sqrt(weight)
    scaled = (picked - base) * scale
    innovation = (values - base) * scale
    parts = split_two(scaled)
    size = (total_members, total_members)
    diagonal = lax.broadcasted_iota(jnp.int32, size, 0) == lax.broadcasted_iota(jnp.int32, size, 1)
    identity = jnp.where(diagonal, 1.0, 0.0)
    gram = dot_three(parts, parts, ((1,), (1,))) + (total_members - 1.0) * identity
    square = jnp.sum(jnp.sum(gram * gram, axis=0, keepdims=True), axis=1, keepdims=True)
    frob = jnp.sqrt(square)
    current = gram / frob
    middle = 1.5 * identity - 0.5 * current
    root = middle
    for step in range(1, ROOT_STEPS):
        middle_parts = split_two(middle)
        current = dot_three(split_two(current), middle_parts)
        root_parts = split_two(root)
        middle = 1.5 * identity - 0.5 * dot_three(root_parts, split_two(current))
        root = dot_three(split_two(middle), root_parts)
    projected = jnp.sum(scaled * innovation, axis=1, keepdims=True)
    once = jnp.sum(root * projected, axis=0, keepdims=True)
    twice = jnp.sum(root * once, axis=1, keepdims=True)
    mean_weights = jnp.sum(jnp.where(diagonal, twice, 0.0), axis=0, keepdims=True) / frob
    weights = (math.sqrt(total_members - 1.0) * root / jnp.sqrt(frob) + mean_weights).astype(jnp.bfloat16)
    for dx in range(2):
        for part in range(2):
            rows = slice((2 * dx + part) * s.local, (2 * dx + part + 1) * s.local)
            block = dot(weights[rows], perturbation, ((1,), (0,))) + mean
            block = block.astype(jnp.bfloat16)
            for dy in range(2):
                target = jnp.bitwise_xor(me, dx * 4 + part * 2 + dy)
                for layer in range(s.layers):
                    at = (layer * 2 + dy) * LANES
                    out_ref[target, layer] = block[:, at : at + LANES]


def place_rows_kernel(s, in_ref, out_ref, rows_ref):
    for source in range(8):
        x, c, y = source // 4, (source // 2) % 2, source % 2
        t = 2 * x + y
        row = t if c == 0 else 7 - t
        for layer in range(s.layers):
            for octet in range(0, s.local // OCTET, 2):
                value = in_ref[source, layer, octet * OCTET : (octet + 2) * OCTET, :].astype(jnp.float32)
                start = octet * OCTET * s.per_member + layer * s.rows + row
                rows_ref[pl.ds(start, 2 * OCTET, stride=s.per_member), :] = value
    out_ref[...] = rows_ref[...].astype(jnp.bfloat16).reshape(out_ref.shape)


def vmem_call(kernel, outs, scratch, *args):
    spec = pl.BlockSpec(memory_space=pltpu.VMEM)
    return pl.pallas_call(
        kernel,
        out_shape=outs,
        in_specs=[spec] * len(args),
        out_specs=jax.tree.map(lambda _: spec, outs),
        scratch_shapes=[pltpu.VMEM(shape, dtype) for shape, dtype in scratch],
    )(*args)


def on_device_tile(prior_sample_set, flow_speeds, observed_cells, observed_values, error_variance):
    local, layers, rows, columns = prior_sample_set.shape
    s = Sizes(local, layers, rows)
    n_gx = lax.axis_size("gx")
    f32, bf16 = jnp.float32, jnp.bfloat16
    shaped = jax.ShapeDtypeStruct
    size = OCTET

    pair = [(m, m ^ 1) for m in range(4)]
    def step(m):
        return 1 if m % 2 == 0 else n_gx - 1
    along = [(m * n_gx + z, m * n_gx + (z + step(m)) % n_gx) for m in range(4) for z in range(n_gx)]
    across = [(0, 1), (1, 0)]
    diagonal = [
        ((m * n_gx + z) * 2 + y, (m * n_gx + (z + step(m)) % n_gx) * 2 + 1 - y)
        for m in range(4) for z in range(n_gx) for y in range(2)
    ]
    owners = []
    for x in range(2):
        for c in range(2):
            for y in range(2):
                source = (x, y, 0) if c == 0 else (1 - x, 1 - y, 1)
                owners.append(((source[0] * 2 + source[1]) * 2 + source[2], (x * 2 + c) * 2 + y))

    own = prior_sample_set.reshape(local * layers * rows, columns)
    sib = lax.ppermute(prior_sample_set, "mem", pair).reshape(own.shape)
    wind = flow_speeds.reshape(2 * layers * rows, columns)

    halo_out = vmem_call(
        functools.partial(pack_halo_kernel, s),
        shaped((s.halo_rows + 3 * s.wind_rows, LANES), bf16),
        [((s.wind_rows, LANES), f32)],
        own, sib, wind,
    )
    halo = lax.ppermute(halo_out, ("mem", "gx"), along)
    side_rows = layers * 2 * s.packs * size + 2 * layers * rows
    corner_rows = layers * s.packs * size + 3 * s.wind_rows
    strips, side_out, corner_out, wind_strip = vmem_call(
        functools.partial(pack_edges_kernel, s),
        (
            shaped((layers * 2 * HALO * s.packs * size, LANES), f32),
            shaped((side_rows, LANES), f32),
            shaped((corner_rows, LANES), bf16),
            shaped((2 * layers * rows, LANES), f32),
        ),
        [((s.wind_rows, LANES), f32)],
        own, sib, wind,
    )
    side = lax.ppermute(side_out, "gy", across)
    corner = lax.ppermute(corner_out, ("mem", "gx", "gy"), diagonal)

    count = observed_cells.shape[-1]
    obs = jnp.stack(
        [observed_cells.reshape(count).astype(f32), observed_values.reshape(count), error_variance.reshape(count)]
    )
    obs = lax.ppermute(obs, ("mem", "gy"), owners)

    span = 16
    coef_rows = 16 * layers * span
    piece = shaped((layers, s.members, LANES), bf16)
    pieces = vmem_call(
        functools.partial(forecast_kernel, s),
        (piece, piece, piece, piece),
        [
            ((2 * layers * span, LANES), f32),
            ((2 * layers * span, LANES), f32),
            ((coef_rows, LANES), f32),
            ((coef_rows, LANES), f32),
            ((layers * HALO * s.members, LANES), f32),
            ((layers * HALO * s.packs * size, LANES), f32),
            ((layers * HALO * s.packs * size, LANES), f32),
        ],
        own, sib, wind, wind_strip, strips, halo, side, corner,
    )

    def flip(dx, dy):
        return [((m * 2 + y), ((m ^ (2 * dx)) * 2 + (y ^ dy))) for m in range(4) for y in range(2)]

    arrived = [
        pieces[0],
        lax.ppermute(pieces[1], ("mem", "gy"), flip(0, 1)),
        lax.ppermute(pieces[2], ("mem", "gy"), flip(1, 0)),
        lax.ppermute(pieces[3], ("mem", "gy"), flip(1, 1)),
    ]
    outgoing = vmem_call(
        functools.partial(analysis_kernel, s, 4 * local),
        shaped((8, layers, local, LANES), bf16),
        [],
        *arrived, obs,
    )
    returned = lax.all_to_all(outgoing, ("mem", "gy"), split_axis=0, concat_axis=0, tiled=True)
    return vmem_call(
        functools.partial(place_rows_kernel, s),
        shaped((local, layers, rows, columns), bf16),
        [((local * layers * rows, LANES), f32)],
        returned,
    )


def on_device(prior_sample_set, flow_speeds, observed_cells, observed_values, error_variance):
    local, layers, rows, columns = prior_sample_set.shape
    suits = (
        lax.axis_size("mem") == 4
        and lax.axis_size("gy") == 2
        and rows == 2 * HALO
        and columns == LANES
        and observed_cells.shape[-2] == 1
        and local % (OCTET * PACK) == 0
    )
    form = on_device_tile if suits else on_device_general
    return form(prior_sample_set, flow_speeds, observed_cells, observed_values, error_variance)


def solution(mesh):
    in_specs = (
        P("mem", None, "gx", "gy"),
        P(None, None, "gx", "gy"),
        P("gx", "gy", "mem", None, None),
        P("gx", "gy", "mem", None, None),
        P("gx", "gy", "mem", None, None),
    )
    out_specs = P("mem", None, "gx", "gy")
    return jax.shard_map(
        on_device, mesh=mesh, in_specs=in_specs, out_specs=out_specs, check_vma=False
    )
```

```python
import functools
import math

import jax
import jax.numpy as jnp
from jax import lax
from jax.experimental import pallas as pl
from jax.experimental.pallas import tpu as pltpu
from jax.sharding import PartitionSpec as P

ROOT_STEPS = 4


diffusion = 0.1
coupling = 0.2


def with_halo(block, sides, width):
    for axis, dim in sides:
        count = lax.axis_size(axis)
        forward = [(i, i + 1) for i in range(count - 1)]
        forward.append((count - 1, 0))
        backward = [(target, source) for source, target in forward]
        low = lax.ppermute(
            lax.slice_in_dim(block, block.shape[dim] - width, None, axis=dim), axis, forward
        )
        high = lax.ppermute(lax.slice_in_dim(block, 0, width, axis=dim), axis, backward)
        block = jnp.concatenate([low, block, high], axis=dim)
    return block


def tendency(model_mesh_field, wind_x, wind_y):
    centre = model_mesh_field[:, :, 1:-1, 1:-1]
    north = model_mesh_field[:, :, 2:, 1:-1]
    south = model_mesh_field[:, :, :-2, 1:-1]
    east = model_mesh_field[:, :, 1:-1, 2:]
    west = model_mesh_field[:, :, 1:-1, :-2]
    layer_mean = jnp.mean(centre, axis=1, keepdims=True)
    return (
        -0.5 * wind_x * (north - south)
        - 0.5 * wind_y * (east - west)
        + diffusion * (north + south + east + west - 4.0 * centre)
        + coupling * (layer_mean - centre)
    )


def crop_margin(array, width):
    return array[:, :, width : array.shape[2] - width, width : array.shape[3] - width]


def deep_step(model_mesh_field, wind_pad):
    padded = with_halo(model_mesh_field, (("gx", 2), ("gy", 3)), 4)
    wind_three = crop_margin(wind_pad, 1)
    wind_two = crop_margin(wind_pad, 2)
    wind_one = crop_margin(wind_pad, 3)
    wind_zero = crop_margin(wind_pad, 4)
    section_one = tendency(padded, wind_three[0], wind_three[1])
    section_two = tendency(crop_margin(padded, 1) + 0.5 * section_one, wind_two[0], wind_two[1])
    section_three = tendency(crop_margin(padded, 2) + 0.5 * section_two, wind_one[0], wind_one[1])
    section_four = tendency(crop_margin(padded, 3) + section_three, wind_zero[0], wind_zero[1])
    return (
        crop_margin(padded, 4)
        + (
            crop_margin(section_one, 3)
            + 2.0 * crop_margin(section_two, 2)
            + 2.0 * crop_margin(section_three, 1)
            + section_four
        )
        / 6.0
    )


def transform_device(weights, rolled):
    return jnp.einsum("qik,ilsqc->klsqc", weights, rolled, preferred_element_type=jnp.float32)


def analyze(strip_block, cells, values, errors, transform):
    realization_vectors, layer_stack, rows, width = strip_block.shape
    patches, count = cells.shape
    patch = width // patches
    highest = lax.Precision.HIGHEST
    mean_field = jnp.mean(strip_block, axis=0, dtype=jnp.float32)
    layer_of = cells // (rows * patch)
    row_of = cells // patch % rows
    column = cells % patch
    starts = (jnp.arange(patches, dtype=jnp.int32) * patch)[:, None]
    flat_index = layer_of * (rows * width) + row_of * width + starts + column
    picked = jnp.take(
        strip_block.reshape(realization_vectors, layer_stack * rows * width),
        flat_index.reshape(-1),
        axis=1,
    )
    base = jnp.take(mean_field.reshape(-1), flat_index.reshape(-1)).reshape(patches, count)
    spread = picked.astype(jnp.float32).reshape(realization_vectors, patches, count) - base[None]
    innovation = values - base
    offset = column.astype(jnp.float32) - 0.5 * (patch - 1)
    spread_parts = []
    innovation_parts = []
    for shift in (-1, 0, 1):
        distance = (shift * patch + jnp.roll(offset, -shift, axis=0)) / patch
        scale = jnp.sqrt(jnp.exp(-0.5 * distance * distance) / jnp.roll(errors, -shift, axis=0))
        spread_parts.append(jnp.roll(spread, -shift, axis=1) * scale[None])
        innovation_parts.append(jnp.roll(innovation, -shift, axis=0) * scale)
    scaled = jnp.concatenate(spread_parts, axis=2)
    scaled_innovation = jnp.concatenate(innovation_parts, axis=1)
    identity = jnp.eye(realization_vectors, dtype=jnp.float32)
    gram = (
        jnp.einsum("kpj,ipj->pki", scaled, scaled, precision=highest)
        + (realization_vectors - 1.0) * identity
    )
    frob = jnp.sqrt(jnp.sum(gram * gram, axis=(1, 2)))
    current = gram / frob[:, None, None]
    root = jnp.broadcast_to(identity, gram.shape)
    for step in range(ROOT_STEPS):
        middle = 1.5 * identity - 0.5 * jnp.einsum("pab,pbc->pac", root, current, precision=highest)
        current = jnp.einsum("pab,pbc->pac", current, middle, precision=highest)
        root = jnp.einsum("pab,pbc->pac", middle, root, precision=highest)
    projected = jnp.einsum("kpj,pj->pk", scaled, scaled_innovation, precision=highest)
    once = jnp.einsum("pab,pb->pa", root, projected, precision=highest)
    twice = jnp.einsum("pab,pb->pa", root, once, precision=highest)
    mean_weights = twice / frob[:, None]
    weights = (
        jnp.sqrt(realization_vectors - 1.0) * root / jnp.sqrt(frob)[:, None, None]
        + mean_weights[:, :, None]
    ).astype(jnp.bfloat16)
    perturbation = (strip_block - mean_field[None]).astype(jnp.bfloat16)
    rolled = jnp.roll(perturbation, -(patch // 2), axis=3).reshape(
        realization_vectors, layer_stack, rows, patches, patch
    )
    first = transform(weights, rolled)
    second = transform(jnp.roll(weights, -1, axis=0), rolled)
    position = (jnp.arange(patch, dtype=jnp.float32) + 0.5) / patch
    increment = ((1.0 - position) * first + position * second).reshape(
        realization_vectors, layer_stack, rows, width
    )
    return (jnp.roll(increment, patch // 2, axis=3) + mean_field[None]).astype(jnp.bfloat16)


def on_device_general(prior_sample_set, flow_speeds, observed_cells, observed_values, error_variance):
    member_group_count = lax.axis_size("mem")
    northward_group_count = lax.axis_size("gy")
    local_member_states, layer_stack, rows_x, column_count_north = prior_sample_set.shape
    band_row_count = rows_x // (member_group_count * northward_group_count)
    all_members = local_member_states * member_group_count
    model_mesh_field = prior_sample_set
    wind_pad = with_halo(flow_speeds, (("gx", 2), ("gy", 3)), 4)
    model_mesh_field = deep_step(model_mesh_field, wind_pad)
    advance_sample_set = model_mesh_field.astype(jnp.bfloat16)
    flattened_realizations = advance_sample_set.reshape(
        local_member_states,
        layer_stack,
        northward_group_count,
        member_group_count,
        band_row_count,
        column_count_north,
    )
    flattened_realizations = flattened_realizations.transpose(3, 2, 0, 1, 4, 5).reshape(
        member_group_count * northward_group_count,
        local_member_states,
        layer_stack,
        band_row_count,
        column_count_north,
    )
    received = lax.all_to_all(
        flattened_realizations, ("mem", "gy"), split_axis=0, concat_axis=0, tiled=True
    )
    received = received.reshape(
        member_group_count,
        northward_group_count,
        local_member_states,
        layer_stack,
        band_row_count,
        column_count_north,
    )
    columns = received.transpose(0, 2, 3, 4, 1, 5).reshape(
        all_members, layer_stack, band_row_count, northward_group_count * column_count_north
    )
    cells = observed_cells.reshape(observed_cells.shape[-2], observed_cells.shape[-1])
    values = observed_values.reshape(observed_values.shape[-2], observed_values.shape[-1])
    errors = error_variance.reshape(error_variance.shape[-2], error_variance.shape[-1])
    analysed = analyze(columns, cells, values, errors, transform_device)
    outgoing = analysed.reshape(
        member_group_count,
        local_member_states,
        layer_stack,
        band_row_count,
        northward_group_count,
        column_count_north,
    )
    outgoing = outgoing.transpose(0, 4, 1, 2, 3, 5).reshape(
        member_group_count * northward_group_count,
        local_member_states,
        layer_stack,
        band_row_count,
        column_count_north,
    )
    returned = lax.all_to_all(outgoing, ("mem", "gy"), split_axis=0, concat_axis=0, tiled=True)
    returned = returned.reshape(
        member_group_count,
        northward_group_count,
        local_member_states,
        layer_stack,
        band_row_count,
        column_count_north,
    )
    return returned.transpose(2, 3, 1, 0, 4, 5).reshape(
        local_member_states, layer_stack, rows_x, column_count_north
    )


LANES = 128
HALO = 4
OCTET = 8
DOMAIN = 3 * HALO
EXTENT = LANES + 2 * OCTET
VMEM_GRANT = 24 << 20
STAGE_FACTORS = (1.0 / 4.0, 1.0 / 3.0, 1.0 / 2.0, 1.0)


def split_two(x):
    high = x.astype(jnp.bfloat16)
    return high, (x - high.astype(jnp.float32)).astype(jnp.bfloat16)


def split_three(x):
    high = x.astype(jnp.bfloat16)
    rest = x - high.astype(jnp.float32)
    middle = rest.astype(jnp.bfloat16)
    return high, middle, (rest - middle.astype(jnp.float32)).astype(jnp.bfloat16)


def tile_row(odd, j):
    return jnp.where(odd == 1, DOMAIN - 1 - j, j - HALO)


def domain_row(odd, row):
    return jnp.where(odd == 1, DOMAIN - 1 - row, row + HALO)


class Sizes:
    def __init__(self, local, layers, rows):
        self.local = local
        self.layers = layers
        self.rows = rows
        self.members = 2 * local
        self.per_member = layers * rows
        self.halo_rows = layers * (HALO + 1) * LANES
        self.wind_rows = 2 * layers * HALO
        self.side_rows = layers * 2 * HALO * OCTET
        self.corner_rows = layers * HALO * OCTET
        self.obs_at = self.side_rows + 2 * layers * rows

    def field_at(self, layer, j):
        return (layer * DOMAIN + j) * EXTENT

    def wind_at(self, part, layer, j):
        return ((part * self.layers + layer) * DOMAIN + j) * EXTENT


def columns_first(s, odd, own_ref, sib_ref, layer, j):
    start = layer * s.rows + tile_row(odd, j)
    parts = [ref[pl.ds(start, s.local, stride=s.per_member), :] for ref in (own_ref, sib_ref)]
    return jnp.concatenate(parts, axis=0).T


def wind_scale(s, odd, value):
    sign = jnp.where(odd == 1, -0.5, 0.5)
    row = lax.broadcasted_iota(jnp.int32, value.shape, 0)
    return value * jnp.where(row < value.shape[0] // 2, sign, 0.5)


def fetch_kernel(
    s, prior_ref, wind_ref, cells_ref, values_ref, errors_ref, own_ref, wind_out_ref, obs_ref,
    cells_vmem, values_vmem, errors_vmem, sems,
):
    copies = [
        pltpu.make_async_copy(source, target, sems.at[i])
        for i, (source, target) in enumerate(
            (
                (cells_ref, cells_vmem), (values_ref, values_vmem), (errors_ref, errors_vmem),
                (wind_ref, wind_out_ref), (prior_ref, own_ref),
            )
        )
    ]
    for copy in copies:
        copy.start()
    obs_ref[...] = jnp.zeros_like(obs_ref)
    for copy in copies[:3]:
        copy.wait()
    obs_ref[0:1, :] = cells_vmem[...].astype(jnp.float32)
    obs_ref[1:2, :] = values_vmem[...]
    obs_ref[2:3, :] = errors_vmem[...]
    for copy in copies[3:]:
        copy.wait()


def pack_halo_kernel(s, own_ref, sib_ref, wind_ref, out_ref, field_ref, rows_ref):
    odd = lax.rem(lax.axis_index("mem"), 2)
    for layer in range(s.layers):
        base = layer * (HALO + 1) * LANES
        for j in range(HALO):
            value = columns_first(s, odd, own_ref, sib_ref, layer, 2 * HALO + j)
            field_ref[pl.ds(s.field_at(layer, 2 * HALO + j) + OCTET, LANES), :] = value
            high, low = split_two(value)
            out_ref[pl.ds(base + (HALO - j) * LANES, LANES), :] = high
            if j == HALO - 1:
                out_ref[pl.ds(base, LANES), :] = low
    for block in range(2 * s.layers):
        for j in range(HALO):
            row = block * s.rows + tile_row(odd, 2 * HALO + j)
            rows_ref[pl.ds(block * HALO + j, 1), :] = wind_ref[pl.ds(row, 1), :]
    for i, part in enumerate(split_three(wind_scale(s, odd, rows_ref[...]))):
        out_ref[pl.ds(s.halo_rows + i * s.wind_rows, s.wind_rows), :] = part


def spread(parts, rows, targets, store):
    stacked = jnp.concatenate(parts, axis=0)
    turned = stacked.T
    source = lax.broadcasted_iota(jnp.int32, (stacked.shape[0], LANES), 0)
    for first, second in zip(targets[::2], targets[1::2], strict=True):
        chosen = [jnp.where(lax.rem(source, rows) == row, 1.0, 0.0) for row in (first, second)]
        both = dot(turned, jnp.concatenate(chosen, axis=1).astype(jnp.bfloat16), ((1,), (0,)))
        store(first, both[:, :LANES])
        store(second, both[:, LANES:])


def pack_edges_kernel(s, own_ref, sib_ref, wind_ref, halo_ref, obs_ref, _, field_ref, side_ref, corner_ref, winds_ref):
    odd = lax.rem(lax.axis_index("mem"), 2)
    for layer in range(s.layers):
        for j in range(HALO, 2 * HALO):
            value = columns_first(s, odd, own_ref, sib_ref, layer, j)
            field_ref[pl.ds(s.field_at(layer, j) + OCTET, LANES), :] = value
    for layer in range(s.layers):
        for j in range(HALO, DOMAIN):
            at = s.field_at(layer, j) + OCTET
            to = (layer * 2 * HALO + j - HALO) * OCTET
            side_ref[pl.ds(to, HALO), :] = field_ref[pl.ds(at + LANES - HALO, HALO), :]
            side_ref[pl.ds(to + HALO, HALO), :] = field_ref[pl.ds(at, HALO), :]
        to, at = layer * HALO * OCTET, (layer * 2 * HALO + HALO) * OCTET
        corner_ref[pl.ds(to, HALO * OCTET), :] = side_ref[pl.ds(at, HALO * OCTET), :].astype(jnp.bfloat16)
    corner_ref[pl.ds(s.corner_rows, 3 * s.wind_rows), :] = halo_ref[pl.ds(s.halo_rows, 3 * s.wind_rows), :]
    scaled = wind_scale(s, odd, wind_ref[...])
    side_ref[pl.ds(s.side_rows, 2 * s.layers * s.rows), :] = scaled
    side_ref[pl.ds(s.obs_at, OCTET), :] = obs_ref[...]

    def store(row, value):
        at = s.wind_at(row // s.rows // s.layers, row // s.rows % s.layers, domain_row(odd, row % s.rows))
        winds_ref[pl.ds(pl.multiple_of(at, OCTET) + OCTET, LANES), :] = value

    rows = 2 * s.layers * s.rows
    spread(split_three(scaled), rows, list(range(rows)), store)


def set_wind_edges(winds_ref, turned, row, at):
    edge = jnp.concatenate([turned[LANES - OCTET :], turned[:OCTET]], axis=0)
    value = jnp.broadcast_to(edge[:, row : row + 1], (2 * OCTET, LANES))
    winds_ref[pl.ds(at + HALO, HALO), :] = value[HALO : 2 * HALO]
    winds_ref[pl.ds(at + OCTET + LANES, HALO), :] = value[OCTET : OCTET + HALO]


def padded_rows(x):
    return jnp.concatenate([x, jnp.zeros((LANES - x.shape[0], LANES), x.dtype)], axis=0)


def set_field_edges(s, field_ref, layer, j, edge):
    at = s.field_at(layer, j)
    field_ref[pl.ds(at + HALO, HALO), :] = edge[:HALO]
    field_ref[pl.ds(at + OCTET + LANES, HALO), :] = edge[HALO:]


def evaluate(s, field_ref, winds_ref, from_ref, stage, start, wanted, emit):
    factor, share = STAGE_FACTORS[stage], 0.2 / s.layers
    centre = {}
    for j in range(wanted[0] - 1, wanted[1] + 1):
        for layer in range(s.layers):
            centre[layer, j] = from_ref[pl.ds(s.field_at(layer, j) + start, OCTET), :]
    for j in range(*wanted):
        for layer in range(s.layers):
            at = s.field_at(layer, j) + start
            others = sum(centre[k, j] for k in range(s.layers) if k != layer)
            north, south = centre[layer, j + 1], centre[layer, j - 1]
            east, west = from_ref[pl.ds(at + 1, OCTET), :], from_ref[pl.ds(at - 1, OCTET), :]
            along = winds_ref[pl.ds(s.wind_at(0, layer, j) + start, OCTET), :]
            across = winds_ref[pl.ds(s.wind_at(1, layer, j) + start, OCTET), :]
            total = along * (south - north) + across * (west - east)
            total = total + 0.1 * ((north + south) + (east + west))
            total = total + ((share - 0.6) * centre[layer, j] + share * others)
            base = field_ref[pl.ds(at, OCTET), :]
            emit(layer, j, base + (total if factor == 1.0 else factor * total))


def run_stage(s, field_ref, winds_ref, from_ref, to_ref, stage, wanted):
    def step(i, carry):
        start = HALO + OCTET * i

        def emit(layer, j, value):
            to_ref[pl.ds(s.field_at(layer, j) + start, OCTET), :] = value

        evaluate(s, field_ref, winds_ref, from_ref, stage, start, wanted, emit)
        return carry

    lax.fori_loop(0, (LANES + 2 * HALO) // OCTET, step, 0)


def inner_kernel(s, _, __, side_ref, field_ref, winds_ref, first_ref, second_ref):
    odd = lax.rem(lax.axis_index("mem"), 2)
    for layer in range(s.layers):
        for j in range(HALO, DOMAIN):
            edge = side_ref[pl.ds((layer * 2 * HALO + j - HALO) * OCTET, OCTET), :]
            set_field_edges(s, field_ref, layer, j, edge)
    beside = padded_rows(side_ref[pl.ds(s.side_rows, 2 * s.layers * s.rows), :]).T
    for block in range(2 * s.layers):
        for row in range(s.rows):
            at = s.wind_at(block // s.layers, block % s.layers, domain_row(odd, row))
            set_wind_edges(winds_ref, beside, block * s.rows + row, pl.multiple_of(at, OCTET))
    refs = (field_ref, first_ref, second_ref, first_ref)
    for stage in range(3):
        wanted = (HALO + 1 + stage, DOMAIN - 1 - stage)
        run_stage(s, field_ref, winds_ref, refs[stage], refs[stage + 1], stage, wanted)


def forecast_kernel(
    s, _, __, ___, ____, halo_ref, corner_ref,
    out0_ref, out1_ref, out2_ref, out3_ref, field_ref, winds_ref, first_ref, second_ref,
):
    mem = lax.axis_index("mem")
    odd = lax.rem(mem, 2)
    place = (mem // 2) * 2 + lax.axis_index("gy")

    for layer in range(s.layers):
        corner = corner_ref[pl.ds(layer * HALO * OCTET, HALO * OCTET), :].astype(jnp.float32)
        for j in range(HALO):
            base = layer * (HALO + 1) * LANES
            value = halo_ref[pl.ds(base + (HALO - j) * LANES, LANES), :].astype(jnp.float32)
            if j == HALO - 1:
                value = value + halo_ref[pl.ds(base, LANES), :].astype(jnp.float32)
            field_ref[pl.ds(s.field_at(layer, j) + OCTET, LANES), :] = value
            set_field_edges(s, field_ref, layer, j, corner[j * OCTET : (j + 1) * OCTET])
    far = [corner_ref[pl.ds(s.corner_rows + i * s.wind_rows, s.wind_rows), :].astype(jnp.float32) for i in range(3)]
    beyond = padded_rows(far[0] + far[1] + far[2]).T
    targets = [block * HALO + j for block in range(2 * s.layers) for j in range(1, HALO)]

    def wind_at(row):
        return s.wind_at(row // HALO // s.layers, row // HALO % s.layers, row % HALO)

    for row in targets:
        set_wind_edges(winds_ref, beyond, row, wind_at(row))

    def store(row, value):
        winds_ref[pl.ds(wind_at(row) + OCTET, LANES), :] = value

    near = [halo_ref[pl.ds(s.halo_rows + i * s.wind_rows, s.wind_rows), :] for i in range(3)]
    spread(near, s.wind_rows, targets, store)

    refs = (field_ref, first_ref, second_ref, first_ref)
    for stage in range(3):
        wanted = (1 + stage, HALO + 1 + stage)
        run_stage(s, field_ref, winds_ref, refs[stage], refs[stage + 1], stage, wanted)

    swap_one = jnp.bitwise_xor(jnp.bitwise_and(place, 1), odd) == 1
    swap_two = jnp.bitwise_xor(place // 2, odd) == 1
    outs = (out0_ref, out1_ref, out2_ref, out3_ref)

    def last_step(i, carry):
        results = [{}, {}]
        for k in range(2):
            start = OCTET + 2 * OCTET * i + OCTET * k
            emit = lambda layer, j, value: results[k].update({(layer, j): value})
            evaluate(s, field_ref, winds_ref, first_ref, 3, start, (HALO, 2 * HALO), emit)
        at = pl.multiple_of(2 * OCTET * i, 2 * OCTET)
        for layer in range(s.layers):
            rows = [
                jnp.concatenate([result[layer, HALO + t] for result in results], axis=0).astype(jnp.bfloat16)
                for t in range(HALO)
            ]
            rows = [jnp.where(swap_one, rows[t ^ 1], rows[t]) for t in range(HALO)]
            rows = [jnp.where(swap_two, rows[t ^ 2], rows[t]) for t in range(HALO)]
            for d, out_ref in enumerate(outs):
                out_ref[layer, pl.ds(at, 2 * OCTET), :] = rows[d]
        return carry

    lax.fori_loop(0, LANES // (2 * OCTET), last_step, 0)


def dot(a, b, contract):
    return lax.dot_general(a, b, (contract, ((), ())), preferred_element_type=jnp.float32)


def dot_three(a, b, contract=((1,), (0,))):
    (a_high, a_low), (b_high, b_low) = a, b
    return dot(a_high, b_low, contract) + dot(a_low, b_high, contract) + dot(a_high, b_high, contract)


def analysis_kernel(s, total_members, piece0_ref, piece1_ref, piece2_ref, piece3_ref, obs_ref, side_ref, out0_ref, out1_ref, out2_ref, out3_ref):
    mem, side = lax.axis_index("mem"), lax.axis_index("gy")
    outs = (out0_ref, out1_ref, out2_ref, out3_ref)
    pieces = (piece0_ref, piece1_ref, piece2_ref, piece3_ref)
    width = 2 * LANES
    cells_total = s.layers * width
    inverse = 1.0 / total_members
    members = jnp.concatenate(
        [
            jnp.concatenate([pieces[2 * dx + dy][layer] for layer in range(s.layers) for dy in range(2)], axis=0)
            for dx in range(2)
        ],
        axis=1,
    )
    mean_row = dot(jnp.ones((OCTET, total_members), jnp.bfloat16), members, ((1,), (1,)))[0:1] * inverse
    mean = dot(members, jnp.ones((total_members, LANES), jnp.bfloat16), ((1,), (0,))) * inverse
    perturbation = jnp.concatenate(
        [(members[:, i : i + LANES].astype(jnp.float32) - mean).astype(jnp.bfloat16) for i in range(0, total_members, LANES)],
        axis=1,
    )

    count = obs_ref.shape[1]
    mine = lax.rem(mem, 2) == side
    obs = padded_rows(jnp.where(mine, obs_ref[...], side_ref[pl.ds(s.obs_at, OCTET), :])).T
    cells = obs[:, 0:1].astype(jnp.int32)
    values, errors = obs[:, 1:2], obs[:, 2:3]
    column = jnp.bitwise_and(cells, width - 1)
    layer_of = jnp.right_shift(cells, width.bit_length() - 1)
    half = jnp.bitwise_xor(jnp.right_shift(column, LANES.bit_length() - 1), side)
    index = layer_of * width + half * LANES + jnp.bitwise_and(column, LANES - 1)
    chosen = jnp.where(lax.broadcasted_iota(jnp.int32, (count, cells_total), 1) == index, 1.0, 0.0)
    picked = dot(chosen.astype(jnp.bfloat16), members, ((1,), (0,)))
    base = jnp.sum(picked, axis=1, keepdims=True) * inverse
    offset = column.astype(jnp.float32) - 0.5 * (width - 1)
    weight = jnp.zeros_like(values)
    for shift in (-1, 0, 1):
        distance = (shift * width + offset) / width
        weight = weight + jnp.exp(-0.5 * distance * distance) / errors
    scale = jnp.sqrt(weight)
    scaled = (picked - base) * scale
    innovation = (values - base) * scale
    parts = split_two(scaled)
    size = (total_members, total_members)
    diagonal = lax.broadcasted_iota(jnp.int32, size, 0) == lax.broadcasted_iota(jnp.int32, size, 1)
    identity = jnp.where(diagonal, 1.0, 0.0)
    gram = dot_three(parts, parts, ((0,), (0,))) + (total_members - 1.0) * identity
    square = jnp.sum(jnp.sum(gram * gram, axis=0, keepdims=True), axis=1, keepdims=True)
    frob = jnp.sqrt(square)
    current = gram / frob
    middle = 1.5 * identity - 0.5 * current
    root = middle
    for step in range(1, ROOT_STEPS):
        middle_parts = split_two(middle)
        current = dot_three(split_two(current), middle_parts)
        root_parts = split_two(root)
        middle = 1.5 * identity - 0.5 * dot_three(root_parts, split_two(current))
        root = dot_three(split_two(middle), root_parts)
    projected = jnp.sum(scaled * innovation, axis=0, keepdims=True)
    once = jnp.sum(root * projected, axis=1, keepdims=True)
    mean_weights = jnp.sum(root * once, axis=0, keepdims=True) / frob
    weights = (math.sqrt(total_members - 1.0) * root / jnp.sqrt(frob) + mean_weights).astype(jnp.bfloat16)
    for dx in range(2):
        for part in range(2):
            rows = slice((2 * dx + part) * s.local, (2 * dx + part + 1) * s.local)
            block = dot(weights[rows], perturbation, ((1,), (1,))) + mean_row
            block = block.astype(jnp.bfloat16)
            for dy in range(2):
                for layer in range(s.layers):
                    at = (layer * 2 + dy) * LANES
                    outs[2 * dx + dy][part, layer] = block[:, at : at + LANES]


def place_rows_kernel(s, *refs):
    pieces, passed, out_ref, rows_ref = refs[:4], refs[4:8], refs[8], refs[9]
    mem = lax.axis_index("mem")
    odd = lax.rem(mem, 2)
    place = (mem // 2) * 2 + lax.axis_index("gy")
    for d in range(4):
        for ref, part, parity in ((pieces[d], 0, odd), (passed[d], 1, 1 - odd)):
            row = 4 * parity + jnp.bitwise_xor(place, d)
            for layer in range(s.layers):
                for octet in range(0, s.local // OCTET, 2):
                    value = ref[part, layer, octet * OCTET : (octet + 2) * OCTET, :].astype(jnp.float32)
                    start = octet * OCTET * s.per_member + layer * s.rows + row
                    rows_ref[pl.ds(start, 2 * OCTET, stride=s.per_member), :] = value
    out_ref[...] = rows_ref[...].astype(jnp.bfloat16).reshape(out_ref.shape)


def vmem_call(kernel, outs, scratch, *args, aliases=None):
    spec = pl.BlockSpec(memory_space=pltpu.VMEM)
    return pl.pallas_call(
        kernel,
        out_shape=outs,
        in_specs=[spec] * len(args),
        out_specs=jax.tree.map(lambda _: spec, outs),
        scratch_shapes=[pltpu.VMEM(shape, dtype) for shape, dtype in scratch],
        input_output_aliases=aliases or {},
        compiler_params=pltpu.CompilerParams(vmem_limit_bytes=VMEM_GRANT),
    )(*args)


def on_device_tile(prior_sample_set, flow_speeds, observed_cells, observed_values, error_variance):
    local, layers, rows, columns = prior_sample_set.shape
    s = Sizes(local, layers, rows)
    n_gx = lax.axis_size("gx")
    f32, bf16 = jnp.float32, jnp.bfloat16
    shaped = jax.ShapeDtypeStruct

    pair = [(m, m ^ 1) for m in range(4)]

    def step(m):
        return 1 if m % 2 == 0 else n_gx - 1

    along = [(m * n_gx + z, m * n_gx + (z + step(m)) % n_gx) for m in range(4) for z in range(n_gx)]
    across = [(0, 1), (1, 0)]
    diagonal = [
        ((m * n_gx + z) * 2 + y, (m * n_gx + (z + step(m)) % n_gx) * 2 + 1 - y)
        for m in range(4) for z in range(n_gx) for y in range(2)
    ]
    owners = [((x * 2 + y) * 2 + c, (x * 2 + c) * 2 + y) for x in range(2) for c in range(2) for y in range(2)]

    sib = lax.ppermute(prior_sample_set, "mem", pair).reshape(local * layers * rows, columns)
    count = observed_cells.shape[-1]
    vmem, hbm = pl.BlockSpec(memory_space=pltpu.VMEM), pl.BlockSpec(memory_space=pltpu.HBM)
    own, wind, obs = pl.pallas_call(
        functools.partial(fetch_kernel, s),
        out_shape=(
            shaped((local * layers * rows, columns), f32),
            shaped((2 * layers * rows, columns), f32),
            shaped((OCTET, count), f32),
        ),
        in_specs=[hbm] * 5,
        out_specs=(vmem, vmem, vmem),
        scratch_shapes=[
            pltpu.VMEM((1, count), jnp.int32),
            pltpu.VMEM((1, count), f32),
            pltpu.VMEM((1, count), f32),
            pltpu.SemaphoreType.DMA((5,)),
        ],
        compiler_params=pltpu.CompilerParams(vmem_limit_bytes=VMEM_GRANT),
    )(
        *(
            pltpu.with_memory_space_constraint(x, pltpu.HBM)
            for x in (
                prior_sample_set.reshape(local * layers * rows, columns),
                flow_speeds.reshape(2 * layers * rows, columns),
                observed_cells.reshape(1, count),
                observed_values.reshape(1, count),
                error_variance.reshape(1, count),
            )
        )
    )
    obs_sib = lax.ppermute(obs, "mem", pair)

    field_shape = shaped((layers * DOMAIN * EXTENT, LANES), f32)
    winds_shape = shaped((2 * layers * DOMAIN * EXTENT, LANES), f32)
    halo_out, field = vmem_call(
        functools.partial(pack_halo_kernel, s),
        (shaped((s.halo_rows + 3 * s.wind_rows, LANES), bf16), field_shape),
        [((s.wind_rows, LANES), f32)],
        own, sib, wind,
    )
    halo = lax.ppermute(halo_out, ("mem", "gx"), along)
    field, side_out, corner_out, winds = vmem_call(
        functools.partial(pack_edges_kernel, s),
        (
            field_shape,
            shaped((s.obs_at + OCTET, LANES), f32),
            shaped((s.corner_rows + 3 * s.wind_rows, LANES), bf16),
            winds_shape,
        ),
        [],
        own, sib, wind, halo_out, obs_sib, field,
        aliases={5: 0},
    )
    side = lax.ppermute(side_out, "gy", across)
    corner = lax.ppermute(corner_out, ("mem", "gx", "gy"), diagonal)
    field, winds, first, second = vmem_call(
        functools.partial(inner_kernel, s),
        (field_shape, winds_shape, field_shape, field_shape),
        [],
        field, winds, side,
        aliases={0: 0, 1: 1},
    )
    piece = shaped((layers, LANES, s.members), bf16)
    *pieces, _, _, _, _ = vmem_call(
        functools.partial(forecast_kernel, s),
        (piece, piece, piece, piece, field_shape, winds_shape, field_shape, field_shape),
        [],
        field, winds, first, second, halo, corner,
        aliases={0: 4, 1: 5, 2: 6, 3: 7},
    )

    def flip(d):
        dx, dy = d // 2, d % 2
        return [((m * 2 + y), ((m ^ (2 * dx)) * 2 + (y ^ dy))) for m in range(4) for y in range(2)]

    def exchange(parts):
        return [parts[0]] + [lax.ppermute(parts[d], ("mem", "gy"), flip(d)) for d in range(1, 4)]

    answer = shaped((2, layers, local, LANES), bf16)
    outgoing = vmem_call(
        functools.partial(analysis_kernel, s, 4 * local),
        (answer, answer, answer, answer),
        [],
        *exchange(pieces), obs, side,
    )
    returned = exchange(outgoing)
    passed = [lax.ppermute(part, "mem", pair) for part in returned]
    return vmem_call(
        functools.partial(place_rows_kernel, s),
        shaped((local, layers, rows, columns), bf16),
        [((local * layers * rows, LANES), f32)],
        *returned, *passed,
    )


def on_device(prior_sample_set, flow_speeds, observed_cells, observed_values, error_variance):
    local, layers, rows, columns = prior_sample_set.shape
    suits = (
        lax.axis_size("mem") == 4
        and lax.axis_size("gy") == 2
        and rows == 2 * HALO
        and columns == LANES
        and observed_cells.shape[-2] == 1
        and 2 * local == LANES
        and observed_cells.shape[-1] == LANES
    )
    form = on_device_tile if suits else on_device_general
    return form(prior_sample_set, flow_speeds, observed_cells, observed_values, error_variance)


def solution(mesh):
    in_specs = (
        P("mem", None, "gx", "gy"),
        P(None, None, "gx", "gy"),
        P("gx", "gy", "mem", None, None),
        P("gx", "gy", "mem", None, None),
        P("gx", "gy", "mem", None, None),
    )
    out_specs = P("mem", None, "gx", "gy")
    return jax.shard_map(
        on_device, mesh=mesh, in_specs=in_specs, out_specs=out_specs, check_vma=False
    )
```

```python
import functools

import jax
import jax.numpy as jnp
from jax import lax
from jax.experimental import pallas as pl
from jax.experimental.pallas import tpu as pltpu
from jax.sharding import PartitionSpec as P


ROOT_STEPS = 4


diffusion = 0.1
coupling = 0.2


def with_halo(block, sides, width):
    for axis, dim in sides:
        count = lax.axis_size(axis)
        forward = [(i, i + 1) for i in range(count - 1)]
        forward.append((count - 1, 0))
        backward = [(target, source) for source, target in forward]
        low = lax.ppermute(
            lax.slice_in_dim(block, block.shape[dim] - width, None, axis=dim), axis, forward
        )
        high = lax.ppermute(lax.slice_in_dim(block, 0, width, axis=dim), axis, backward)
        block = jnp.concatenate([low, block, high], axis=dim)
    return block


def tendency(model_mesh_field, wind_x, wind_y):
    centre = model_mesh_field[:, :, 1:-1, 1:-1]
    north = model_mesh_field[:, :, 2:, 1:-1]
    south = model_mesh_field[:, :, :-2, 1:-1]
    east = model_mesh_field[:, :, 1:-1, 2:]
    west = model_mesh_field[:, :, 1:-1, :-2]
    layer_mean = jnp.mean(centre, axis=1, keepdims=True)
    return (
        -0.5 * wind_x * (north - south)
        - 0.5 * wind_y * (east - west)
        + diffusion * (north + south + east + west - 4.0 * centre)
        + coupling * (layer_mean - centre)
    )


def crop_margin(array, width):
    return array[:, :, width : array.shape[2] - width, width : array.shape[3] - width]


def deep_step(model_mesh_field, wind_pad):
    padded = with_halo(model_mesh_field, (("gx", 2), ("gy", 3)), 4)
    wind_three = crop_margin(wind_pad, 1)
    wind_two = crop_margin(wind_pad, 2)
    wind_one = crop_margin(wind_pad, 3)
    wind_zero = crop_margin(wind_pad, 4)
    section_one = tendency(padded, wind_three[0], wind_three[1])
    section_two = tendency(crop_margin(padded, 1) + 0.5 * section_one, wind_two[0], wind_two[1])
    section_three = tendency(crop_margin(padded, 2) + 0.5 * section_two, wind_one[0], wind_one[1])
    section_four = tendency(crop_margin(padded, 3) + section_three, wind_zero[0], wind_zero[1])
    return (
        crop_margin(padded, 4)
        + (
            crop_margin(section_one, 3)
            + 2.0 * crop_margin(section_two, 2)
            + 2.0 * crop_margin(section_three, 1)
            + section_four
        )
        / 6.0
    )


def transform_device(weights, rolled):
    return jnp.einsum("qik,ilsqc->klsqc", weights, rolled, preferred_element_type=jnp.float32)


def analyze(strip_block, cells, values, errors, transform):
    realization_vectors, layer_stack, rows, width = strip_block.shape
    patches, count = cells.shape
    patch = width // patches
    highest = lax.Precision.HIGHEST
    mean_field = jnp.mean(strip_block, axis=0, dtype=jnp.float32)
    layer_of = cells // (rows * patch)
    row_of = cells // patch % rows
    column = cells % patch
    starts = (jnp.arange(patches, dtype=jnp.int32) * patch)[:, None]
    flat_index = layer_of * (rows * width) + row_of * width + starts + column
    picked = jnp.take(
        strip_block.reshape(realization_vectors, layer_stack * rows * width),
        flat_index.reshape(-1),
        axis=1,
    )
    base = jnp.take(mean_field.reshape(-1), flat_index.reshape(-1)).reshape(patches, count)
    spread = picked.astype(jnp.float32).reshape(realization_vectors, patches, count) - base[None]
    innovation = values - base
    offset = column.astype(jnp.float32) - 0.5 * (patch - 1)
    spread_parts = []
    innovation_parts = []
    for shift in (-1, 0, 1):
        distance = (shift * patch + jnp.roll(offset, -shift, axis=0)) / patch
        scale = jnp.sqrt(jnp.exp(-0.5 * distance * distance) / jnp.roll(errors, -shift, axis=0))
        spread_parts.append(jnp.roll(spread, -shift, axis=1) * scale[None])
        innovation_parts.append(jnp.roll(innovation, -shift, axis=0) * scale)
    scaled = jnp.concatenate(spread_parts, axis=2)
    scaled_innovation = jnp.concatenate(innovation_parts, axis=1)
    identity = jnp.eye(realization_vectors, dtype=jnp.float32)
    gram = (
        jnp.einsum("kpj,ipj->pki", scaled, scaled, precision=highest)
        + (realization_vectors - 1.0) * identity
    )
    frob = jnp.sqrt(jnp.sum(gram * gram, axis=(1, 2)))
    current = gram / frob[:, None, None]
    root = jnp.broadcast_to(identity, gram.shape)
    for _ in range(ROOT_STEPS):
        middle = 1.5 * identity - 0.5 * jnp.einsum("pab,pbc->pac", root, current, precision=highest)
        current = jnp.einsum("pab,pbc->pac", current, middle, precision=highest)
        root = jnp.einsum("pab,pbc->pac", middle, root, precision=highest)
    projected = jnp.einsum("kpj,pj->pk", scaled, scaled_innovation, precision=highest)
    once = jnp.einsum("pab,pb->pa", root, projected, precision=highest)
    twice = jnp.einsum("pab,pb->pa", root, once, precision=highest)
    mean_weights = twice / frob[:, None]
    weights = (
        jnp.sqrt(realization_vectors - 1.0) * root / jnp.sqrt(frob)[:, None, None]
        + mean_weights[:, :, None]
    ).astype(jnp.bfloat16)
    perturbation = (strip_block - mean_field[None]).astype(jnp.bfloat16)
    rolled = jnp.roll(perturbation, -(patch // 2), axis=3).reshape(
        realization_vectors, layer_stack, rows, patches, patch
    )
    first = transform(weights, rolled)
    second = transform(jnp.roll(weights, -1, axis=0), rolled)
    position = (jnp.arange(patch, dtype=jnp.float32) + 0.5) / patch
    increment = ((1.0 - position) * first + position * second).reshape(
        realization_vectors, layer_stack, rows, width
    )
    return (jnp.roll(increment, patch // 2, axis=3) + mean_field[None]).astype(jnp.bfloat16)


def on_device_general(prior_sample_set, flow_speeds, observed_cells, observed_values, error_variance):
    member_group_count = lax.axis_size("mem")
    northward_group_count = lax.axis_size("gy")
    local_member_states, layer_stack, rows_x, column_count_north = prior_sample_set.shape
    band_row_count = rows_x // (member_group_count * northward_group_count)
    all_members = local_member_states * member_group_count
    model_mesh_field = prior_sample_set
    wind_pad = with_halo(flow_speeds, (("gx", 2), ("gy", 3)), 4)
    model_mesh_field = deep_step(model_mesh_field, wind_pad)
    advance_sample_set = model_mesh_field.astype(jnp.bfloat16)
    flattened_realizations = advance_sample_set.reshape(
        local_member_states,
        layer_stack,
        northward_group_count,
        member_group_count,
        band_row_count,
        column_count_north,
    )
    flattened_realizations = flattened_realizations.transpose(3, 2, 0, 1, 4, 5).reshape(
        member_group_count * northward_group_count,
        local_member_states,
        layer_stack,
        band_row_count,
        column_count_north,
    )
    received = lax.all_to_all(
        flattened_realizations, ("mem", "gy"), split_axis=0, concat_axis=0, tiled=True
    )
    received = received.reshape(
        member_group_count,
        northward_group_count,
        local_member_states,
        layer_stack,
        band_row_count,
        column_count_north,
    )
    columns = received.transpose(0, 2, 3, 4, 1, 5).reshape(
        all_members, layer_stack, band_row_count, northward_group_count * column_count_north
    )
    cells = observed_cells.reshape(observed_cells.shape[-2], observed_cells.shape[-1])
    values = observed_values.reshape(observed_values.shape[-2], observed_values.shape[-1])
    errors = error_variance.reshape(error_variance.shape[-2], error_variance.shape[-1])
    analysed = analyze(columns, cells, values, errors, transform_device)
    outgoing = analysed.reshape(
        member_group_count,
        local_member_states,
        layer_stack,
        band_row_count,
        northward_group_count,
        column_count_north,
    )
    outgoing = outgoing.transpose(0, 4, 1, 2, 3, 5).reshape(
        member_group_count * northward_group_count,
        local_member_states,
        layer_stack,
        band_row_count,
        column_count_north,
    )
    returned = lax.all_to_all(outgoing, ("mem", "gy"), split_axis=0, concat_axis=0, tiled=True)
    returned = returned.reshape(
        member_group_count,
        northward_group_count,
        local_member_states,
        layer_stack,
        band_row_count,
        column_count_north,
    )
    return returned.transpose(2, 3, 1, 0, 4, 5).reshape(
        local_member_states, layer_stack, rows_x, column_count_north
    )


LANES = 128
HALO = 4
OCTET = 8
DOMAIN = 3 * HALO
EXTENT = LANES + 2 * OCTET
VMEM_GRANT = 24 << 20
STAGE_FACTORS = (1.0 / 4.0, 1.0 / 3.0, 1.0 / 2.0, 1.0)


def split_two(x):
    high = x.astype(jnp.bfloat16)
    return high, (x - high.astype(jnp.float32)).astype(jnp.bfloat16)


def split_three(x):
    high = x.astype(jnp.bfloat16)
    rest = x - high.astype(jnp.float32)
    middle = rest.astype(jnp.bfloat16)
    return high, middle, (rest - middle.astype(jnp.float32)).astype(jnp.bfloat16)


def tile_row(odd, j):
    return jnp.where(odd == 1, DOMAIN - 1 - j, j - HALO)


def domain_row(odd, row):
    return jnp.where(odd == 1, DOMAIN - 1 - row, row + HALO)


class Sizes:
    def __init__(self, local, layers, rows):
        self.local = local
        self.layers = layers
        self.rows = rows
        self.members = 2 * local
        self.per_member = layers * rows
        self.halo_rows = layers * (HALO + 1) * LANES
        self.wind_rows = 2 * layers * HALO
        self.side_rows = layers * 2 * HALO * OCTET
        self.corner_rows = layers * HALO * OCTET
        self.piece_rows = layers * LANES
        self.obs_rows = 2 * OCTET

    def field_at(self, layer, j):
        return (layer * DOMAIN + j) * EXTENT

    def wind_at(self, part, layer, j):
        return ((part * self.layers + layer) * DOMAIN + j) * EXTENT


def columns_first(s, odd, own_ref, sib_ref, layer, j):
    start = layer * s.rows + tile_row(odd, j)
    parts = [ref[pl.ds(start, s.local, stride=s.per_member), :] for ref in (own_ref, sib_ref)]
    return jnp.concatenate(parts, axis=0).T


def wind_scale(odd, value):
    half = 0.5 / diffusion
    sign = jnp.where(odd == 1, -half, half)
    row = lax.broadcasted_iota(jnp.int32, value.shape, 0)
    return value * jnp.where(row < value.shape[0] // 2, sign, half)


def fetch_kernel(
    prior_ref, wind_ref, cells_ref, values_ref, errors_ref, own_ref, wind_out_ref, obs_ref,
    cells_vmem, values_vmem, errors_vmem, sems,
):
    copies = [
        pltpu.make_async_copy(source, target, sems.at[i])
        for i, (source, target) in enumerate(
            (
                (cells_ref, cells_vmem), (values_ref, values_vmem), (errors_ref, errors_vmem),
                (wind_ref, wind_out_ref), (prior_ref, own_ref),
            )
        )
    ]
    for copy in copies:
        copy.start()
    obs_ref[...] = jnp.zeros_like(obs_ref)
    for copy in copies[:3]:
        copy.wait()
    obs_ref[0:1, :] = cells_vmem[...].astype(jnp.float32)
    obs_ref[1:2, :] = values_vmem[...]
    obs_ref[2:3, :] = errors_vmem[...]
    for copy in copies[3:]:
        copy.wait()


def pack_halo_kernel(s, own_ref, sib_ref, wind_ref, out_ref, field_ref, rows_ref):
    odd = lax.rem(lax.axis_index("mem"), 2)
    for layer in range(s.layers):
        base = layer * (HALO + 1) * LANES
        for j in range(HALO):
            value = columns_first(s, odd, own_ref, sib_ref, layer, 2 * HALO + j)
            field_ref[pl.ds(s.field_at(layer, 2 * HALO + j) + OCTET, LANES), :] = value
            high, low = split_two(value)
            out_ref[pl.ds(base + (HALO - j) * LANES, LANES), :] = high
            if j == HALO - 1:
                out_ref[pl.ds(base, LANES), :] = low
    for block in range(2 * s.layers):
        for j in range(HALO):
            row = block * s.rows + tile_row(odd, 2 * HALO + j)
            rows_ref[pl.ds(block * HALO + j, 1), :] = wind_ref[pl.ds(row, 1), :]
    for i, part in enumerate(split_three(wind_scale(odd, rows_ref[...]))):
        out_ref[pl.ds(s.halo_rows + i * s.wind_rows, s.wind_rows), :] = part


def spread(parts, rows, targets, store):
    stacked = jnp.concatenate(parts, axis=0)
    turned = stacked.T
    source = lax.broadcasted_iota(jnp.int32, (stacked.shape[0], LANES), 0)
    for first, second in zip(targets[::2], targets[1::2], strict=True):
        chosen = [jnp.where(lax.rem(source, rows) == row, 1.0, 0.0) for row in (first, second)]
        both = dot(turned, jnp.concatenate(chosen, axis=1).astype(jnp.bfloat16), ((1,), (0,)))
        store(first, both[:, :LANES])
        store(second, both[:, LANES:])


def pack_edges_kernel(s, own_ref, sib_ref, wind_ref, halo_ref, _, field_ref, side_ref, corner_ref, winds_ref):
    odd = lax.rem(lax.axis_index("mem"), 2)
    for layer in range(s.layers):
        for j in range(HALO, 2 * HALO):
            value = columns_first(s, odd, own_ref, sib_ref, layer, j)
            field_ref[pl.ds(s.field_at(layer, j) + OCTET, LANES), :] = value
    for layer in range(s.layers):
        for j in range(HALO, DOMAIN):
            at = s.field_at(layer, j) + OCTET
            to = (layer * 2 * HALO + j - HALO) * OCTET
            side_ref[pl.ds(to, HALO), :] = field_ref[pl.ds(at + LANES - HALO, HALO), :]
            side_ref[pl.ds(to + HALO, HALO), :] = field_ref[pl.ds(at, HALO), :]
        to, at = layer * HALO * OCTET, (layer * 2 * HALO + HALO) * OCTET
        corner_ref[pl.ds(to, HALO * OCTET), :] = side_ref[pl.ds(at, HALO * OCTET), :].astype(jnp.bfloat16)
    corner_ref[pl.ds(s.corner_rows, 3 * s.wind_rows), :] = halo_ref[pl.ds(s.halo_rows, 3 * s.wind_rows), :]
    scaled = wind_scale(odd, wind_ref[...])
    side_ref[pl.ds(s.side_rows, 2 * s.layers * s.rows), :] = scaled

    def store(row, value):
        at = s.wind_at(row // s.rows // s.layers, row // s.rows % s.layers, domain_row(odd, row % s.rows))
        winds_ref[pl.ds(pl.multiple_of(at, OCTET) + OCTET, LANES), :] = value

    rows = 2 * s.layers * s.rows
    spread(split_three(scaled), rows, list(range(rows)), store)


def set_wind_edges(winds_ref, turned, row, at):
    edge = jnp.concatenate([turned[LANES - OCTET :], turned[:OCTET]], axis=0)
    value = jnp.broadcast_to(edge[:, row : row + 1], (2 * OCTET, LANES))
    winds_ref[pl.ds(at + HALO, HALO), :] = value[HALO : 2 * HALO]
    winds_ref[pl.ds(at + OCTET + LANES, HALO), :] = value[OCTET : OCTET + HALO]


def padded_rows(x):
    return jnp.concatenate([x, jnp.zeros((LANES - x.shape[0], LANES), x.dtype)], axis=0)


def set_field_edges(s, field_ref, layer, j, edge):
    at = s.field_at(layer, j)
    field_ref[pl.ds(at + HALO, HALO), :] = edge[:HALO]
    field_ref[pl.ds(at + OCTET + LANES, HALO), :] = edge[HALO:]


def evaluate(s, field_ref, winds_ref, from_ref, stage, start, wanted, emit):
    factor, share = STAGE_FACTORS[stage] * diffusion, coupling / s.layers / diffusion
    own_share = 4.0 + coupling / diffusion - share
    centre = {}
    for j in range(wanted[0] - 1, wanted[1] + 1):
        for layer in range(s.layers):
            centre[layer, j] = from_ref[pl.ds(s.field_at(layer, j) + start, OCTET), :]
    for j in range(*wanted):
        for layer in range(s.layers):
            at = s.field_at(layer, j) + start
            others = sum(centre[k, j] for k in range(s.layers) if k != layer)
            north, south = centre[layer, j + 1], centre[layer, j - 1]
            east, west = from_ref[pl.ds(at + 1, OCTET), :], from_ref[pl.ds(at - 1, OCTET), :]
            along = winds_ref[pl.ds(s.wind_at(0, layer, j) + start, OCTET), :]
            across = winds_ref[pl.ds(s.wind_at(1, layer, j) + start, OCTET), :]
            total = along * (south - north) + across * (west - east)
            total = total + ((north + south) + (east + west))
            total = total + ((others if share == 1.0 else share * others) - own_share * centre[layer, j])
            emit(layer, j, field_ref[pl.ds(at, OCTET), :] + factor * total)


def run_stage(s, field_ref, winds_ref, from_ref, to_ref, stage, wanted):
    def step(i, carry):
        for k in range(2):
            start = 2 * OCTET * i + OCTET * k

            def emit(layer, j, value):
                to_ref[pl.ds(s.field_at(layer, j) + start, OCTET), :] = value

            evaluate(s, field_ref, winds_ref, from_ref, stage, start, wanted, emit)
        return carry

    lax.fori_loop(0, EXTENT // (2 * OCTET), step, 0)


def inner_kernel(s, _, __, side_ref, field_ref, winds_ref, first_ref, second_ref):
    odd = lax.rem(lax.axis_index("mem"), 2)
    for layer in range(s.layers):
        for j in range(HALO, DOMAIN):
            edge = side_ref[pl.ds((layer * 2 * HALO + j - HALO) * OCTET, OCTET), :]
            set_field_edges(s, field_ref, layer, j, edge)
    beside = padded_rows(side_ref[pl.ds(s.side_rows, 2 * s.layers * s.rows), :]).T
    for block in range(2 * s.layers):
        for row in range(s.rows):
            at = s.wind_at(block // s.layers, block % s.layers, domain_row(odd, row))
            set_wind_edges(winds_ref, beside, block * s.rows + row, pl.multiple_of(at, OCTET))
    refs = (field_ref, first_ref, second_ref, first_ref)
    for stage in range(3):
        wanted = (HALO + 1 + stage, DOMAIN - 1 - stage)
        run_stage(s, field_ref, winds_ref, refs[stage], refs[stage + 1], stage, wanted)


def forecast_kernel(
    s, _, __, ___, ____, halo_ref, corner_ref, obs_ref,
    out0_ref, out1_ref, out2_ref, out3_ref, field_ref, winds_ref, first_ref, second_ref,
):
    mem = lax.axis_index("mem")
    odd = lax.rem(mem, 2)
    place = (mem // 2) * 2 + lax.axis_index("gy")

    for layer in range(s.layers):
        corner = corner_ref[pl.ds(layer * HALO * OCTET, HALO * OCTET), :].astype(jnp.float32)
        for j in range(HALO):
            base = layer * (HALO + 1) * LANES
            value = halo_ref[pl.ds(base + (HALO - j) * LANES, LANES), :].astype(jnp.float32)
            if j == HALO - 1:
                value = value + halo_ref[pl.ds(base, LANES), :].astype(jnp.float32)
            field_ref[pl.ds(s.field_at(layer, j) + OCTET, LANES), :] = value
            set_field_edges(s, field_ref, layer, j, corner[j * OCTET : (j + 1) * OCTET])
    far = [corner_ref[pl.ds(s.corner_rows + i * s.wind_rows, s.wind_rows), :].astype(jnp.float32) for i in range(3)]
    beyond = padded_rows(far[0] + far[1] + far[2]).T
    targets = [block * HALO + j for block in range(2 * s.layers) for j in range(1, HALO)]

    def wind_at(row):
        return s.wind_at(row // HALO // s.layers, row // HALO % s.layers, row % HALO)

    for row in targets:
        set_wind_edges(winds_ref, beyond, row, wind_at(row))

    def store(row, value):
        winds_ref[pl.ds(wind_at(row) + OCTET, LANES), :] = value

    near = [halo_ref[pl.ds(s.halo_rows + i * s.wind_rows, s.wind_rows), :] for i in range(3)]
    spread(near, s.wind_rows, targets, store)

    refs = (field_ref, first_ref, second_ref, first_ref)
    for stage in range(3):
        wanted = (1 + stage, HALO + 1 + stage)
        run_stage(s, field_ref, winds_ref, refs[stage], refs[stage + 1], stage, wanted)

    for i, part in enumerate(split_three(obs_ref[...])):
        out1_ref[pl.ds(s.piece_rows + i * s.obs_rows, s.obs_rows), :] = part
    swap_one = jnp.bitwise_xor(jnp.bitwise_and(place, 1), odd) == 1
    swap_two = jnp.bitwise_xor(place // 2, odd) == 1
    outs = (out0_ref, out1_ref, out2_ref, out3_ref)

    def last_step(i, carry):
        results = [{}, {}]
        for k in range(2):
            start = OCTET + 2 * OCTET * i + OCTET * k
            emit = lambda layer, j, value: results[k].update({(layer, j): value})
            evaluate(s, field_ref, winds_ref, first_ref, 3, start, (HALO, 2 * HALO), emit)
        at = pl.multiple_of(2 * OCTET * i, 2 * OCTET)
        for layer in range(s.layers):
            rows = [
                jnp.concatenate([result[layer, HALO + t] for result in results], axis=0).astype(jnp.bfloat16)
                for t in range(HALO)
            ]
            rows = [jnp.where(swap_one, rows[t ^ 1], rows[t]) for t in range(HALO)]
            rows = [jnp.where(swap_two, rows[t ^ 2], rows[t]) for t in range(HALO)]
            for d, out_ref in enumerate(outs):
                out_ref[pl.ds(layer * LANES + at, 2 * OCTET), :] = rows[d]
        return carry

    lax.fori_loop(0, LANES // (2 * OCTET), last_step, 0)


def dot(a, b, contract):
    return lax.dot_general(a, b, (contract, ((), ())), preferred_element_type=jnp.float32)


def beside(*parts):
    return jnp.concatenate(parts, axis=1)


def below(*parts):
    return jnp.concatenate(parts, axis=0)


def dot_split(a, b):
    (a_high, a_low), (b_high, b_low) = split_two(a), split_two(b)
    row = beside(b_high, b_low)
    both = dot(beside(a_high, a_low), below(row, row), ((1,), (0,)))
    return both[:, : b.shape[1]] + both[:, b.shape[1] :]


def root_parts(product, vector, total_members):
    count = product.shape[0]
    size = (count, count)
    diagonal = lax.broadcasted_iota(jnp.int32, size, 0) == lax.broadcasted_iota(jnp.int32, size, 1)

    def total(x):
        return jnp.sum(jnp.sum(x, axis=0, keepdims=True), axis=1, keepdims=True)

    def plus(x, scalar):
        return jnp.where(diagonal, x + scalar, x)

    def twice(matrix, column):
        once = jnp.sum(matrix * column, axis=0, keepdims=True)
        return jnp.sum(matrix * once, axis=1, keepdims=True)

    least = total_members - 1.0
    trace = total(jnp.where(diagonal, product, 0.0))
    square = total(product * product) + (2.0 * least) * trace + least * least * total_members
    inverse = lax.rsqrt(square)
    b = product * inverse
    x = least * inverse
    z = jnp.ones_like(x)
    m = 1.5 - 0.5 * x
    middle = plus(-0.5 * b, m)
    y = plus((0.25 * x - m) * b + 0.25 * dot_split(b, b), -x * m)
    near = plus(m * m * b + dot_split(y, b), m * m * x)
    slope = plus(y, m * m)
    x, z = x * m * m, m
    root = middle
    vector = twice(middle, vector)
    root_slope = jnp.where(diagonal, -0.5, 0.0)
    for step in range(1, ROOT_STEPS):
        m = 1.5 - 0.5 * x
        middle = plus(-0.5 * near, 1.5)
        root_slope = m * root_slope - 0.5 * dot_split(slope, root)
        vector = twice(middle, vector)
        z = m * z
        if step < ROOT_STEPS - 1:
            root = dot_split(middle, root)
            rest = plus(near, -x)
            y = dot_split(near, plus(0.25 * rest, -m))
            slope = m * m * slope + dot_split(y, slope)
            near = m * m * near + dot_split(y, rest)
            x = x * m * m
    return inverse, z, root_slope, vector


def analysis_kernel(
    s, total_members, piece0_ref, piece1_ref, piece2_ref, piece3_ref, obs_ref,
    send_ref, perturbation_ref, weights_ref, mean_ref,
):
    mem, side = lax.axis_index("mem"), lax.axis_index("gy")
    pieces = (piece0_ref, piece1_ref, piece2_ref, piece3_ref)
    width = 2 * LANES
    cells_total = s.layers * width
    inverse_count = 1.0 / total_members
    members = beside(
        *(
            below(*(pieces[2 * dx + dy][layer * LANES : (layer + 1) * LANES] for layer in range(s.layers) for dy in range(2)))
            for dx in range(2)
        )
    )
    mean_row = dot(jnp.ones((OCTET, total_members), jnp.bfloat16), members, ((1,), (1,))) * inverse_count
    mean = dot(members, jnp.ones((total_members, LANES), jnp.bfloat16), ((1,), (0,))) * inverse_count
    perturbation = beside(
        *(
            (members[:, i : i + LANES].astype(jnp.float32) - mean).astype(jnp.bfloat16)
            for i in range(0, total_members, LANES)
        )
    )
    perturbation_ref[...] = perturbation
    mean_ref[...] = mean_row

    count = obs_ref.shape[1]
    far = [piece1_ref[pl.ds(s.piece_rows + i * s.obs_rows, s.obs_rows), :].astype(jnp.float32) for i in range(3)]
    mine = lax.rem(mem, 2) == side
    obs = padded_rows(jnp.where(mine, obs_ref[...], far[0] + far[1] + far[2])).T
    cells = obs[:, 0:1].astype(jnp.int32)
    values, errors = obs[:, 1:2], obs[:, 2:3]
    column = jnp.bitwise_and(cells, width - 1)
    layer_of = jnp.right_shift(cells, width.bit_length() - 1)
    half = jnp.bitwise_xor(jnp.right_shift(column, LANES.bit_length() - 1), side)
    index = layer_of * width + half * LANES + jnp.bitwise_and(column, LANES - 1)
    chosen = jnp.where(lax.broadcasted_iota(jnp.int32, (count, cells_total), 1) == index, 1.0, 0.0)
    picked = dot(chosen.astype(jnp.bfloat16), members, ((1,), (0,)))
    base = jnp.sum(picked, axis=1, keepdims=True) * inverse_count
    offset = column.astype(jnp.float32) - 0.5 * (width - 1)
    weight = jnp.zeros_like(values)
    for shift in (-1, 0, 1):
        distance = (shift * width + offset) / width
        weight = weight + jnp.exp(-0.5 * distance * distance) / errors
    scale = jnp.sqrt(weight)
    scaled = (picked - base) * scale
    innovation = (values - base) * scale

    high, low = split_two(scaled)
    quarters = dot(below(high, low), below(high, low), ((1,), (1,)))
    halves = quarters[:count] + quarters[count:]
    inverse, z, slope, twice = root_parts(halves[:, :count] + halves[:, count:], innovation, total_members)
    slope_high, slope_low = split_two(slope * inverse)
    both = beside(slope_high, slope_low)
    carried = dot(both, below(high, high), ((1,), (0,))) + dot(both, below(low, low), ((1,), (0,)))
    carried_high, carried_low = split_two(carried)
    turned = below(high, low)
    spread_part = dot(turned, below(carried_high, carried_high), ((0,), (0,)))
    spread_part = spread_part + dot(turned, below(carried_low, carried_low), ((0,), (0,)))
    mean_weights = jnp.sum(scaled * twice, axis=0, keepdims=True) * inverse
    size = (total_members, total_members)
    diagonal = lax.broadcasted_iota(jnp.int32, size, 0) == lax.broadcasted_iota(jnp.int32, size, 1)
    full = jnp.where(diagonal, spread_part + z, spread_part)
    weights = (full * jnp.sqrt((total_members - 1.0) * inverse) + mean_weights).astype(jnp.bfloat16)
    weights_ref[...] = weights
    for dx in range(2):
        block = answer_rows(s, weights, perturbation, mean_row, dx, 1)
        for dy in range(2):
            for layer in range(s.layers):
                at = (layer * 2 + dy) * LANES
                send_ref[2 * dx + dy, layer] = block[:, at : at + LANES]


def answer_rows(s, weights, perturbation, mean_row, dx, part):
    first = (2 * dx + part) * s.local
    block = dot(weights[first : first + s.local], perturbation, ((1,), (1,))) + mean_row[0:1]
    return block.astype(jnp.bfloat16)


def answer_kernel(s, perturbation_ref, weights_ref, mean_ref, *outs):
    for dx in range(2):
        block = answer_rows(s, weights_ref[...], perturbation_ref[...], mean_ref[...], dx, 0)
        for dy in range(2):
            for layer in range(s.layers):
                at = (layer * 2 + dy) * LANES
                outs[2 * dx + dy][0, layer] = block[:, at : at + LANES]


def join_kernel(received_ref, *refs):
    for d in range(4):
        refs[4 + d][1] = received_ref[d]


def place_rows_kernel(s, *refs):
    pieces, out_ref, rows_ref = refs[:4], refs[4], refs[5]
    mem = lax.axis_index("mem")
    odd = lax.rem(mem, 2)
    place = (mem // 2) * 2 + lax.axis_index("gy")
    for d in range(4):
        for part, parity in ((0, odd), (1, 1 - odd)):
            row = 4 * parity + jnp.bitwise_xor(place, d)
            for layer in range(s.layers):
                for octet in range(0, s.local // OCTET, 2):
                    value = pieces[d][part, layer, octet * OCTET : (octet + 2) * OCTET, :].astype(jnp.float32)
                    start = octet * OCTET * s.per_member + layer * s.rows + row
                    rows_ref[pl.ds(start, 2 * OCTET, stride=s.per_member), :] = value
    out_ref[...] = rows_ref[...].astype(jnp.bfloat16).reshape(out_ref.shape)


def vmem_call(kernel, outs, scratch, *args, aliases=None):
    spec = pl.BlockSpec(memory_space=pltpu.VMEM)
    return pl.pallas_call(
        kernel,
        out_shape=outs,
        in_specs=[spec] * len(args),
        out_specs=jax.tree.map(lambda _: spec, outs),
        scratch_shapes=[pltpu.VMEM(shape, dtype) for shape, dtype in scratch],
        input_output_aliases=aliases or {},
        compiler_params=pltpu.CompilerParams(vmem_limit_bytes=VMEM_GRANT),
    )(*args)


def on_device_tile(prior_sample_set, flow_speeds, observed_cells, observed_values, error_variance):
    local, layers, rows, columns = prior_sample_set.shape
    s = Sizes(local, layers, rows)
    n_gx = lax.axis_size("gx")
    f32, bf16 = jnp.float32, jnp.bfloat16
    shaped = jax.ShapeDtypeStruct

    pair = [(m, m ^ 1) for m in range(4)]

    def step(m):
        return 1 if m % 2 == 0 else n_gx - 1

    along = [(m * n_gx + z, m * n_gx + (z + step(m)) % n_gx) for m in range(4) for z in range(n_gx)]
    across = [(0, 1), (1, 0)]
    diagonal = [
        ((m * n_gx + z) * 2 + y, (m * n_gx + (z + step(m)) % n_gx) * 2 + 1 - y)
        for m in range(4) for z in range(n_gx) for y in range(2)
    ]

    sib = lax.ppermute(prior_sample_set, "mem", pair).reshape(local * layers * rows, columns)
    count = observed_cells.shape[-1]
    vmem, hbm = pl.BlockSpec(memory_space=pltpu.VMEM), pl.BlockSpec(memory_space=pltpu.HBM)
    own, wind, obs = pl.pallas_call(
        fetch_kernel,
        out_shape=(
            shaped((local * layers * rows, columns), f32),
            shaped((2 * layers * rows, columns), f32),
            shaped((2 * OCTET, count), f32),
        ),
        in_specs=[hbm] * 5,
        out_specs=(vmem, vmem, vmem),
        scratch_shapes=[
            pltpu.VMEM((1, count), jnp.int32),
            pltpu.VMEM((1, count), f32),
            pltpu.VMEM((1, count), f32),
            pltpu.SemaphoreType.DMA((5,)),
        ],
        compiler_params=pltpu.CompilerParams(vmem_limit_bytes=VMEM_GRANT),
    )(
        *(
            pltpu.with_memory_space_constraint(x, pltpu.HBM)
            for x in (
                prior_sample_set.reshape(local * layers * rows, columns),
                flow_speeds.reshape(2 * layers * rows, columns),
                observed_cells.reshape(1, count),
                observed_values.reshape(1, count),
                error_variance.reshape(1, count),
            )
        )
    )
    obs_sib = lax.ppermute(obs, "mem", pair)

    field_shape = shaped((layers * DOMAIN * EXTENT, LANES), f32)
    winds_shape = shaped((2 * layers * DOMAIN * EXTENT, LANES), f32)
    halo_out, field = vmem_call(
        functools.partial(pack_halo_kernel, s),
        (shaped((s.halo_rows + 3 * s.wind_rows, LANES), bf16), field_shape),
        [((s.wind_rows, LANES), f32)],
        own, sib, wind,
    )
    halo = lax.ppermute(halo_out, ("mem", "gx"), along)
    field, side_out, corner_out, winds = vmem_call(
        functools.partial(pack_edges_kernel, s),
        (
            field_shape,
            shaped((s.side_rows + 2 * layers * rows, LANES), f32),
            shaped((s.corner_rows + 3 * s.wind_rows, LANES), bf16),
            winds_shape,
        ),
        [],
        own, sib, wind, halo_out, field,
        aliases={4: 0},
    )
    side = lax.ppermute(side_out, "gy", across)
    corner = lax.ppermute(corner_out, ("mem", "gx", "gy"), diagonal)
    field, winds, first, second = vmem_call(
        functools.partial(inner_kernel, s),
        (field_shape, winds_shape, field_shape, field_shape),
        [],
        field, winds, side,
        aliases={0: 0, 1: 1},
    )
    piece = shaped((s.piece_rows, s.members), bf16)
    piece_obs = shaped((s.piece_rows + 3 * s.obs_rows, s.members), bf16)
    *pieces, _, _, _, _ = vmem_call(
        functools.partial(forecast_kernel, s),
        (piece, piece_obs, piece, piece, field_shape, winds_shape, field_shape, field_shape),
        [],
        field, winds, first, second, halo, corner, obs_sib,
        aliases={0: 4, 1: 5, 2: 6, 3: 7},
    )

    def flip(d):
        dx, dy = d // 2, d % 2
        return [((m * 2 + y), ((m ^ (2 * dx)) * 2 + (y ^ dy))) for m in range(4) for y in range(2)]

    def exchange(parts):
        arrived = [parts[0]]
        for d in range(1, 4):
            arrived.append(lax.ppermute(parts[d], ("mem", "gy"), flip(d)))
        return arrived

    total = 4 * local
    send, perturbation, weights, mean = vmem_call(
        functools.partial(analysis_kernel, s, total),
        (
            shaped((4, layers, local, LANES), bf16),
            shaped((layers * 2 * LANES, total), bf16),
            shaped((total, total), bf16),
            shaped((OCTET, layers * 2 * LANES), f32),
        ),
        [],
        *exchange(pieces), obs,
    )
    received = lax.ppermute(send, "mem", pair)
    answer = shaped((2, layers, local, LANES), bf16)
    answers = vmem_call(
        functools.partial(answer_kernel, s), (answer, answer, answer, answer), [], perturbation, weights, mean
    )
    answers = vmem_call(
        join_kernel, (answer, answer, answer, answer), [], received, *answers, aliases={1 + d: d for d in range(4)}
    )
    return vmem_call(
        functools.partial(place_rows_kernel, s),
        shaped((local, layers, rows, columns), bf16),
        [((local * layers * rows, LANES), f32)],
        *exchange(answers),
    )


def on_device(prior_sample_set, flow_speeds, observed_cells, observed_values, error_variance):
    local, _, rows, columns = prior_sample_set.shape
    suits = (
        lax.axis_size("mem") == 4
        and lax.axis_size("gy") == 2
        and rows == 2 * HALO
        and columns == LANES
        and observed_cells.shape[-2] == 1
        and 2 * local == LANES
        and observed_cells.shape[-1] == LANES
    )
    form = on_device_tile if suits else on_device_general
    return form(prior_sample_set, flow_speeds, observed_cells, observed_values, error_variance)


def solution(mesh):
    in_specs = (
        P("mem", None, "gx", "gy"),
        P(None, None, "gx", "gy"),
        P("gx", "gy", "mem", None, None),
        P("gx", "gy", "mem", None, None),
        P("gx", "gy", "mem", None, None),
    )
    out_specs = P("mem", None, "gx", "gy")
    return jax.shard_map(
        on_device, mesh=mesh, in_specs=in_specs, out_specs=out_specs, check_vma=False
    )
```

```python
import functools

import jax
import jax.numpy as jnp
from jax import lax
from jax.experimental import pallas as pl
from jax.experimental.pallas import tpu as pltpu
from jax.sharding import PartitionSpec as P


ROOT_STEPS = 4


diffusion = 0.1
coupling = 0.2


def with_halo(block, sides, width):
    for axis, dim in sides:
        count = lax.axis_size(axis)
        forward = [(i, i + 1) for i in range(count - 1)]
        forward.append((count - 1, 0))
        backward = [(target, source) for source, target in forward]
        low = lax.ppermute(
            lax.slice_in_dim(block, block.shape[dim] - width, None, axis=dim), axis, forward
        )
        high = lax.ppermute(lax.slice_in_dim(block, 0, width, axis=dim), axis, backward)
        block = jnp.concatenate([low, block, high], axis=dim)
    return block


def tendency(model_mesh_field, wind_x, wind_y):
    centre = model_mesh_field[:, :, 1:-1, 1:-1]
    north = model_mesh_field[:, :, 2:, 1:-1]
    south = model_mesh_field[:, :, :-2, 1:-1]
    east = model_mesh_field[:, :, 1:-1, 2:]
    west = model_mesh_field[:, :, 1:-1, :-2]
    layer_mean = jnp.mean(centre, axis=1, keepdims=True)
    return (
        -0.5 * wind_x * (north - south)
        - 0.5 * wind_y * (east - west)
        + diffusion * (north + south + east + west - 4.0 * centre)
        + coupling * (layer_mean - centre)
    )


def crop_margin(array, width):
    return array[:, :, width : array.shape[2] - width, width : array.shape[3] - width]


def deep_step(model_mesh_field, wind_pad):
    padded = with_halo(model_mesh_field, (("gx", 2), ("gy", 3)), 4)
    wind_three = crop_margin(wind_pad, 1)
    wind_two = crop_margin(wind_pad, 2)
    wind_one = crop_margin(wind_pad, 3)
    wind_zero = crop_margin(wind_pad, 4)
    section_one = tendency(padded, wind_three[0], wind_three[1])
    section_two = tendency(crop_margin(padded, 1) + 0.5 * section_one, wind_two[0], wind_two[1])
    section_three = tendency(crop_margin(padded, 2) + 0.5 * section_two, wind_one[0], wind_one[1])
    section_four = tendency(crop_margin(padded, 3) + section_three, wind_zero[0], wind_zero[1])
    return (
        crop_margin(padded, 4)
        + (
            crop_margin(section_one, 3)
            + 2.0 * crop_margin(section_two, 2)
            + 2.0 * crop_margin(section_three, 1)
            + section_four
        )
        / 6.0
    )


def transform_device(weights, rolled):
    return jnp.einsum("qik,ilsqc->klsqc", weights, rolled, preferred_element_type=jnp.float32)


def analyze(strip_block, cells, values, errors, transform):
    realization_vectors, layer_stack, rows, width = strip_block.shape
    patches, count = cells.shape
    patch = width // patches
    highest = lax.Precision.HIGHEST
    mean_field = jnp.mean(strip_block, axis=0, dtype=jnp.float32)
    layer_of = cells // (rows * patch)
    row_of = cells // patch % rows
    column = cells % patch
    starts = (jnp.arange(patches, dtype=jnp.int32) * patch)[:, None]
    flat_index = layer_of * (rows * width) + row_of * width + starts + column
    picked = jnp.take(
        strip_block.reshape(realization_vectors, layer_stack * rows * width),
        flat_index.reshape(-1),
        axis=1,
    )
    base = jnp.take(mean_field.reshape(-1), flat_index.reshape(-1)).reshape(patches, count)
    spread = picked.astype(jnp.float32).reshape(realization_vectors, patches, count) - base[None]
    innovation = values - base
    offset = column.astype(jnp.float32) - 0.5 * (patch - 1)
    spread_parts = []
    innovation_parts = []
    for shift in (-1, 0, 1):
        distance = (shift * patch + jnp.roll(offset, -shift, axis=0)) / patch
        scale = jnp.sqrt(jnp.exp(-0.5 * distance * distance) / jnp.roll(errors, -shift, axis=0))
        spread_parts.append(jnp.roll(spread, -shift, axis=1) * scale[None])
        innovation_parts.append(jnp.roll(innovation, -shift, axis=0) * scale)
    scaled = jnp.concatenate(spread_parts, axis=2)
    scaled_innovation = jnp.concatenate(innovation_parts, axis=1)
    identity = jnp.eye(realization_vectors, dtype=jnp.float32)
    gram = (
        jnp.einsum("kpj,ipj->pki", scaled, scaled, precision=highest)
        + (realization_vectors - 1.0) * identity
    )
    frob = jnp.sqrt(jnp.sum(gram * gram, axis=(1, 2)))
    current = gram / frob[:, None, None]
    root = jnp.broadcast_to(identity, gram.shape)
    for _ in range(ROOT_STEPS):
        middle = 1.5 * identity - 0.5 * jnp.einsum("pab,pbc->pac", root, current, precision=highest)
        current = jnp.einsum("pab,pbc->pac", current, middle, precision=highest)
        root = jnp.einsum("pab,pbc->pac", middle, root, precision=highest)
    projected = jnp.einsum("kpj,pj->pk", scaled, scaled_innovation, precision=highest)
    once = jnp.einsum("pab,pb->pa", root, projected, precision=highest)
    twice = jnp.einsum("pab,pb->pa", root, once, precision=highest)
    mean_weights = twice / frob[:, None]
    weights = (
        jnp.sqrt(realization_vectors - 1.0) * root / jnp.sqrt(frob)[:, None, None]
        + mean_weights[:, :, None]
    ).astype(jnp.bfloat16)
    perturbation = (strip_block - mean_field[None]).astype(jnp.bfloat16)
    rolled = jnp.roll(perturbation, -(patch // 2), axis=3).reshape(
        realization_vectors, layer_stack, rows, patches, patch
    )
    first = transform(weights, rolled)
    second = transform(jnp.roll(weights, -1, axis=0), rolled)
    position = (jnp.arange(patch, dtype=jnp.float32) + 0.5) / patch
    increment = ((1.0 - position) * first + position * second).reshape(
        realization_vectors, layer_stack, rows, width
    )
    return (jnp.roll(increment, patch // 2, axis=3) + mean_field[None]).astype(jnp.bfloat16)


def on_device_general(prior_sample_set, flow_speeds, observed_cells, observed_values, error_variance):
    member_group_count = lax.axis_size("mem")
    northward_group_count = lax.axis_size("gy")
    local_member_states, layer_stack, rows_x, column_count_north = prior_sample_set.shape
    band_row_count = rows_x // (member_group_count * northward_group_count)
    all_members = local_member_states * member_group_count
    model_mesh_field = prior_sample_set
    wind_pad = with_halo(flow_speeds, (("gx", 2), ("gy", 3)), 4)
    model_mesh_field = deep_step(model_mesh_field, wind_pad)
    advance_sample_set = model_mesh_field.astype(jnp.bfloat16)
    flattened_realizations = advance_sample_set.reshape(
        local_member_states,
        layer_stack,
        northward_group_count,
        member_group_count,
        band_row_count,
        column_count_north,
    )
    flattened_realizations = flattened_realizations.transpose(3, 2, 0, 1, 4, 5).reshape(
        member_group_count * northward_group_count,
        local_member_states,
        layer_stack,
        band_row_count,
        column_count_north,
    )
    received = lax.all_to_all(
        flattened_realizations, ("mem", "gy"), split_axis=0, concat_axis=0, tiled=True
    )
    received = received.reshape(
        member_group_count,
        northward_group_count,
        local_member_states,
        layer_stack,
        band_row_count,
        column_count_north,
    )
    columns = received.transpose(0, 2, 3, 4, 1, 5).reshape(
        all_members, layer_stack, band_row_count, northward_group_count * column_count_north
    )
    cells = observed_cells.reshape(observed_cells.shape[-2], observed_cells.shape[-1])
    values = observed_values.reshape(observed_values.shape[-2], observed_values.shape[-1])
    errors = error_variance.reshape(error_variance.shape[-2], error_variance.shape[-1])
    analysed = analyze(columns, cells, values, errors, transform_device)
    outgoing = analysed.reshape(
        member_group_count,
        local_member_states,
        layer_stack,
        band_row_count,
        northward_group_count,
        column_count_north,
    )
    outgoing = outgoing.transpose(0, 4, 1, 2, 3, 5).reshape(
        member_group_count * northward_group_count,
        local_member_states,
        layer_stack,
        band_row_count,
        column_count_north,
    )
    returned = lax.all_to_all(outgoing, ("mem", "gy"), split_axis=0, concat_axis=0, tiled=True)
    returned = returned.reshape(
        member_group_count,
        northward_group_count,
        local_member_states,
        layer_stack,
        band_row_count,
        column_count_north,
    )
    return returned.transpose(2, 3, 1, 0, 4, 5).reshape(
        local_member_states, layer_stack, rows_x, column_count_north
    )


LANES = 128
HALO = 4
OCTET = 8
DOMAIN = 3 * HALO
EXTENT = LANES + 2 * OCTET
VMEM_GRANT = 24 << 20
LARGEST = 6.0
WIDENING = 11.06 / LARGEST
STAGE_FACTORS = (1.0 / 4.0, 1.0 / 3.0, 1.0 / 2.0, 1.0)


def split_two(x):
    high = x.astype(jnp.bfloat16)
    return high, (x - high.astype(jnp.float32)).astype(jnp.bfloat16)


def split_three(x):
    high = x.astype(jnp.bfloat16)
    rest = x - high.astype(jnp.float32)
    middle = rest.astype(jnp.bfloat16)
    return high, middle, (rest - middle.astype(jnp.float32)).astype(jnp.bfloat16)


def tile_row(odd, j):
    return jnp.where(odd == 1, DOMAIN - 1 - j, j - HALO)


def domain_row(odd, row):
    return jnp.where(odd == 1, DOMAIN - 1 - row, row + HALO)


class Sizes:
    def __init__(self, local, layers, rows):
        self.local = local
        self.layers = layers
        self.rows = rows
        self.members = 2 * local
        self.per_member = layers * rows
        self.halo_rows = HALO * LANES
        self.wind_rows = 2 * layers * HALO
        self.side_rows = layers * 2 * HALO * OCTET
        self.corner_rows = layers * HALO * OCTET
        self.piece_rows = layers * LANES
        self.obs_rows = 2 * OCTET

    def field_at(self, layer, j):
        return (layer * DOMAIN + j) * EXTENT

    def wind_at(self, part, layer, j):
        return ((part * self.layers + layer) * DOMAIN + j) * EXTENT


def columns_first(s, odd, own_ref, sib_ref, layer, j):
    start = layer * s.rows + tile_row(odd, j)
    parts = [ref[pl.ds(start, s.local, stride=s.per_member), :] for ref in (own_ref, sib_ref)]
    return jnp.concatenate(parts, axis=0).T


def wind_scale(odd, value):
    half = 0.5 / diffusion
    sign = jnp.where(odd == 1, -half, half)
    row = lax.broadcasted_iota(jnp.int32, value.shape, 0)
    return value * jnp.where(row < value.shape[0] // 2, sign, half)


def widened(u):
    v = WIDENING * jnp.abs(u)
    series = v * (1.0 + v * (1.0 / 2.0) * (1.0 + v * (1.0 / 3.0) * (1.0 + v * (1.0 / 4.0))))
    g = jnp.where(v < 0.05, series, jnp.exp(v) - 1.0)
    return jnp.where(u < 0.0, -g, g)


def narrowed(w):
    g = jnp.abs(w)
    series = g * (1.0 - g * (1.0 / 2.0 - g * (1.0 / 3.0 - g * (1.0 / 4.0 - g * (1.0 / 5.0)))))
    u = jnp.where(g < 0.05, series, jnp.log(1.0 + g)) * (1.0 / WIDENING)
    return jnp.where(w < 0.0, -u, u)


def fetch_kernel(
    s, prior_ref, wind_ref, cells_ref, values_ref, errors_ref,
    own_ref, wind_out_ref, obs_ref, same_ref, other_ref,
    cells_vmem, values_vmem, errors_vmem, rows_ref, sems,
):
    odd = lax.rem(lax.axis_index("mem"), 2)
    copies = [
        pltpu.make_async_copy(source, target, sems.at[i])
        for i, (source, target) in enumerate(
            (
                (cells_ref, cells_vmem), (values_ref, values_vmem), (errors_ref, errors_vmem),
                (wind_ref, wind_out_ref), (prior_ref, own_ref),
            )
        )
    ]
    for copy in copies:
        copy.start()
    obs_ref[...] = jnp.zeros_like(obs_ref)
    for copy in copies[:4]:
        copy.wait()
    obs_ref[0:1, :] = cells_vmem[...].astype(jnp.float32)
    obs_ref[1:2, :] = values_vmem[...]
    obs_ref[2:3, :] = errors_vmem[...]
    for block in range(2 * s.layers):
        for j in range(HALO):
            row = block * s.rows + tile_row(odd, 2 * HALO + j)
            rows_ref[pl.ds(block * HALO + j, 1), :] = wind_out_ref[pl.ds(row, 1), :]
    for i, part in enumerate(split_three(wind_scale(odd, rows_ref[...]))):
        same_ref[pl.ds(s.halo_rows + i * s.wind_rows, s.wind_rows), :] = part.astype(jnp.float32)
    copies[4].wait()
    for parity, out_ref in ((odd, same_ref), (1 - odd, other_ref)):
        for j in range(HALO):
            row = tile_row(parity, 2 * HALO + j)
            parts = [own_ref[pl.ds(layer * s.rows + row, s.local, stride=s.per_member), :] for layer in range(s.layers)]
            value = jnp.concatenate(parts, axis=0).T
            out_ref[pl.ds(j * LANES, LANES), :] = widened(value) if j == HALO - 1 else value


def spread(parts, rows, targets, store):
    stacked = jnp.concatenate(parts, axis=0)
    turned = stacked.T
    source = lax.broadcasted_iota(jnp.int32, (stacked.shape[0], LANES), 0)
    for first, second in zip(targets[::2], targets[1::2], strict=True):
        chosen = [jnp.where(lax.rem(source, rows) == row, 1.0, 0.0) for row in (first, second)]
        both = dot(turned, jnp.concatenate(chosen, axis=1).astype(jnp.bfloat16), ((1,), (0,)))
        store(first, both[:, :LANES])
        store(second, both[:, LANES:])


def pack_edges_kernel(s, own_ref, sib_ref, wind_ref, same_ref, field_ref, side_ref, corner_ref, winds_ref):
    odd = lax.rem(lax.axis_index("mem"), 2)
    for layer in range(s.layers):
        for j in range(HALO, DOMAIN):
            value = columns_first(s, odd, own_ref, sib_ref, layer, j)
            field_ref[pl.ds(s.field_at(layer, j) + OCTET, LANES), :] = value
            to = (layer * 2 * HALO + j - HALO) * OCTET
            side_ref[pl.ds(to, HALO), :] = value[LANES - HALO :]
            side_ref[pl.ds(to + HALO, HALO), :] = value[:HALO]
        to, at = layer * HALO * OCTET, (layer * 2 * HALO + HALO) * OCTET
        corner_ref[pl.ds(to, HALO * OCTET), :] = side_ref[pl.ds(at, HALO * OCTET), :].astype(jnp.bfloat16)
    winds = same_ref[pl.ds(s.halo_rows, 3 * s.wind_rows), :]
    corner_ref[pl.ds(s.corner_rows, 3 * s.wind_rows), :] = winds.astype(jnp.bfloat16)
    scaled = wind_scale(odd, wind_ref[...])
    side_ref[pl.ds(s.side_rows, 2 * s.layers * s.rows), :] = scaled

    def store(row, value):
        at = s.wind_at(row // s.rows // s.layers, row // s.rows % s.layers, domain_row(odd, row % s.rows))
        winds_ref[pl.ds(pl.multiple_of(at, OCTET) + OCTET, LANES), :] = value

    rows = 2 * s.layers * s.rows
    spread(split_three(scaled), rows, list(range(rows)), store)


def set_wind_edges(winds_ref, turned, row, at):
    edge = jnp.concatenate([turned[LANES - OCTET :], turned[:OCTET]], axis=0)
    value = jnp.broadcast_to(edge[:, row : row + 1], (2 * OCTET, LANES))
    winds_ref[pl.ds(at + HALO, HALO), :] = value[HALO : 2 * HALO]
    winds_ref[pl.ds(at + OCTET + LANES, HALO), :] = value[OCTET : OCTET + HALO]


def padded_rows(x):
    return jnp.concatenate([x, jnp.zeros((LANES - x.shape[0], LANES), x.dtype)], axis=0)


def set_field_edges(s, field_ref, layer, j, edge):
    at = s.field_at(layer, j)
    field_ref[pl.ds(at + HALO, HALO), :] = edge[:HALO]
    field_ref[pl.ds(at + OCTET + LANES, HALO), :] = edge[HALO:]


def evaluate(s, field_ref, winds_ref, from_ref, stage, start, wanted, emit):
    factor, share = STAGE_FACTORS[stage] * diffusion, coupling / s.layers / diffusion
    own_share = 4.0 + coupling / diffusion - share
    centre = {}
    for j in range(wanted[0] - 1, wanted[1] + 1):
        for layer in range(s.layers):
            centre[layer, j] = from_ref[pl.ds(s.field_at(layer, j) + start, OCTET), :]
    for j in range(*wanted):
        for layer in range(s.layers):
            at = s.field_at(layer, j) + start
            others = sum(centre[k, j] for k in range(s.layers) if k != layer)
            north, south = centre[layer, j + 1], centre[layer, j - 1]
            east, west = from_ref[pl.ds(at + 1, OCTET), :], from_ref[pl.ds(at - 1, OCTET), :]
            along = winds_ref[pl.ds(s.wind_at(0, layer, j) + start, OCTET), :]
            across = winds_ref[pl.ds(s.wind_at(1, layer, j) + start, OCTET), :]
            total = along * (south - north) + across * (west - east)
            total = total + ((north + south) + (east + west))
            total = total + ((others if share == 1.0 else share * others) - own_share * centre[layer, j])
            emit(layer, j, field_ref[pl.ds(at, OCTET), :] + factor * total)


def run_stage(s, field_ref, winds_ref, from_ref, to_ref, stage, wanted):
    def step(i, carry):
        for k in range(2):
            start = 2 * OCTET * i + OCTET * k

            def emit(layer, j, value):
                to_ref[pl.ds(s.field_at(layer, j) + start, OCTET), :] = value

            evaluate(s, field_ref, winds_ref, from_ref, stage, start, wanted, emit)
        return carry

    lax.fori_loop(0, EXTENT // (2 * OCTET), step, 0)


def inner_kernel(s, _, __, side_ref, field_ref, winds_ref, first_ref, second_ref):
    odd = lax.rem(lax.axis_index("mem"), 2)
    for layer in range(s.layers):
        for j in range(HALO, DOMAIN):
            edge = side_ref[pl.ds((layer * 2 * HALO + j - HALO) * OCTET, OCTET), :]
            set_field_edges(s, field_ref, layer, j, edge)
    beside = padded_rows(side_ref[pl.ds(s.side_rows, 2 * s.layers * s.rows), :]).T
    for block in range(2 * s.layers):
        for row in range(s.rows):
            at = s.wind_at(block // s.layers, block % s.layers, domain_row(odd, row))
            set_wind_edges(winds_ref, beside, block * s.rows + row, pl.multiple_of(at, OCTET))
    refs = (field_ref, first_ref, second_ref, first_ref)
    for stage in range(3):
        wanted = (HALO + 1 + stage, DOMAIN - 1 - stage)
        run_stage(s, field_ref, winds_ref, refs[stage], refs[stage + 1], stage, wanted)


def forecast_kernel(
    s, _, __, ___, ____, same_ref, other_ref, corner_ref, obs_ref,
    out0_ref, out1_ref, out2_ref, out3_ref, field_ref, winds_ref, first_ref, second_ref,
):
    mem = lax.axis_index("mem")
    odd = lax.rem(mem, 2)
    place = (mem // 2) * 2 + lax.axis_index("gy")

    lower = lax.broadcasted_iota(jnp.int32, (LANES, LANES), 1) < s.local
    for j in range(HALO):
        both = []
        for ref in (same_ref, other_ref):
            value = ref[pl.ds(j * LANES, LANES), :]
            both.append(narrowed(value) if j == HALO - 1 else value)
        same, other = both
        layer_fields = (
            jnp.where(lower, same, pltpu.roll(other, s.local, 1)),
            jnp.where(lower, pltpu.roll(same, s.local, 1), other),
        )
        for layer, value in enumerate(layer_fields):
            field_ref[pl.ds(s.field_at(layer, j) + OCTET, LANES), :] = value
    for layer in range(s.layers):
        corner = corner_ref[pl.ds(layer * HALO * OCTET, HALO * OCTET), :].astype(jnp.float32)
        for j in range(HALO):
            set_field_edges(s, field_ref, layer, j, corner[j * OCTET : (j + 1) * OCTET])
    far = [corner_ref[pl.ds(s.corner_rows + i * s.wind_rows, s.wind_rows), :].astype(jnp.float32) for i in range(3)]
    beyond = padded_rows(far[0] + far[1] + far[2]).T
    targets = [block * HALO + j for block in range(2 * s.layers) for j in range(1, HALO)]

    def wind_at(row):
        return s.wind_at(row // HALO // s.layers, row // HALO % s.layers, row % HALO)

    for row in targets:
        set_wind_edges(winds_ref, beyond, row, wind_at(row))

    def store(row, value):
        winds_ref[pl.ds(wind_at(row) + OCTET, LANES), :] = value

    near = [same_ref[pl.ds(s.halo_rows + i * s.wind_rows, s.wind_rows), :].astype(jnp.bfloat16) for i in range(3)]
    spread(near, s.wind_rows, targets, store)

    refs = (field_ref, first_ref, second_ref, first_ref)
    for stage in range(3):
        wanted = (1 + stage, HALO + 1 + stage)
        run_stage(s, field_ref, winds_ref, refs[stage], refs[stage + 1], stage, wanted)

    for i, part in enumerate(split_three(obs_ref[...])):
        out1_ref[pl.ds(s.piece_rows + i * s.obs_rows, s.obs_rows), :] = part
    swap_one = jnp.bitwise_xor(jnp.bitwise_and(place, 1), odd) == 1
    swap_two = jnp.bitwise_xor(place // 2, odd) == 1
    outs = (out0_ref, out1_ref, out2_ref, out3_ref)

    def last_step(i, carry):
        results = [{}, {}]
        for k in range(2):
            start = OCTET + 2 * OCTET * i + OCTET * k
            emit = lambda layer, j, value: results[k].update({(layer, j): value})
            evaluate(s, field_ref, winds_ref, first_ref, 3, start, (HALO, 2 * HALO), emit)
        at = pl.multiple_of(2 * OCTET * i, 2 * OCTET)
        for layer in range(s.layers):
            rows = [
                jnp.concatenate([result[layer, HALO + t] for result in results], axis=0).astype(jnp.bfloat16)
                for t in range(HALO)
            ]
            rows = [jnp.where(swap_one, rows[t ^ 1], rows[t]) for t in range(HALO)]
            rows = [jnp.where(swap_two, rows[t ^ 2], rows[t]) for t in range(HALO)]
            for d, out_ref in enumerate(outs):
                out_ref[pl.ds(layer * LANES + at, 2 * OCTET), :] = rows[d]
        return carry

    lax.fori_loop(0, LANES // (2 * OCTET), last_step, 0)


def dot(a, b, contract):
    return lax.dot_general(a, b, (contract, ((), ())), preferred_element_type=jnp.float32)


def beside(*parts):
    return jnp.concatenate(parts, axis=1)


def below(*parts):
    return jnp.concatenate(parts, axis=0)


def dot_split(a, b):
    (a_high, a_low), (b_high, b_low) = split_two(a), split_two(b)
    row = beside(b_high, b_low)
    both = dot(beside(a_high, a_low), below(row, row), ((1,), (0,)))
    return both[:, : b.shape[1]] + both[:, b.shape[1] :]


def root_parts(product, vector, total_members):
    count = product.shape[0]
    size = (count, count)
    diagonal = lax.broadcasted_iota(jnp.int32, size, 0) == lax.broadcasted_iota(jnp.int32, size, 1)

    def total(x):
        return jnp.sum(jnp.sum(x, axis=0, keepdims=True), axis=1, keepdims=True)

    def plus(x, scalar):
        return jnp.where(diagonal, x + scalar, x)

    def twice(matrix, column):
        once = jnp.sum(matrix * column, axis=0, keepdims=True)
        return jnp.sum(matrix * once, axis=1, keepdims=True)

    least = total_members - 1.0
    trace = total(jnp.where(diagonal, product, 0.0))
    square = total(product * product) + (2.0 * least) * trace + least * least * total_members
    inverse = lax.rsqrt(square)
    b = product * inverse
    x = least * inverse
    z = jnp.ones_like(x)
    m = 1.5 - 0.5 * x
    middle = plus(-0.5 * b, m)
    y = plus((0.25 * x - m) * b + 0.25 * dot_split(b, b), -x * m)
    near = plus(m * m * b + dot_split(y, b), m * m * x)
    slope = plus(y, m * m)
    x, z = x * m * m, m
    root = middle
    vector = twice(middle, vector)
    root_slope = jnp.where(diagonal, -0.5, 0.0)
    for step in range(1, ROOT_STEPS):
        m = 1.5 - 0.5 * x
        middle = plus(-0.5 * near, 1.5)
        root_slope = m * root_slope - 0.5 * dot_split(slope, root)
        vector = twice(middle, vector)
        z = m * z
        if step < ROOT_STEPS - 1:
            root = dot_split(middle, root)
            rest = plus(near, -x)
            y = dot_split(near, plus(0.25 * rest, -m))
            slope = m * m * slope + dot_split(y, slope)
            near = m * m * near + dot_split(y, rest)
            x = x * m * m
    return inverse, z, root_slope, vector


def analysis_kernel(
    s, total_members, piece0_ref, piece1_ref, piece2_ref, piece3_ref, obs_ref,
    send_ref, perturbation_ref, weights_ref, mean_ref,
):
    mem, side = lax.axis_index("mem"), lax.axis_index("gy")
    pieces = (piece0_ref, piece1_ref, piece2_ref, piece3_ref)
    width = 2 * LANES
    cells_total = s.layers * width
    inverse_count = 1.0 / total_members
    members = beside(
        *(
            below(*(pieces[2 * dx + dy][layer * LANES : (layer + 1) * LANES] for layer in range(s.layers) for dy in range(2)))
            for dx in range(2)
        )
    )
    mean_row = dot(jnp.ones((OCTET, total_members), jnp.bfloat16), members, ((1,), (1,))) * inverse_count
    mean = dot(members, jnp.ones((total_members, LANES), jnp.bfloat16), ((1,), (0,))) * inverse_count
    perturbation = beside(
        *(
            (members[:, i : i + LANES].astype(jnp.float32) - mean).astype(jnp.bfloat16)
            for i in range(0, total_members, LANES)
        )
    )
    perturbation_ref[...] = perturbation
    mean_ref[...] = mean_row

    count = obs_ref.shape[1]
    far = [piece1_ref[pl.ds(s.piece_rows + i * s.obs_rows, s.obs_rows), :].astype(jnp.float32) for i in range(3)]
    mine = lax.rem(mem, 2) == side
    obs = padded_rows(jnp.where(mine, obs_ref[...], far[0] + far[1] + far[2])).T
    cells = obs[:, 0:1].astype(jnp.int32)
    values, errors = obs[:, 1:2], obs[:, 2:3]
    column = jnp.bitwise_and(cells, width - 1)
    layer_of = jnp.right_shift(cells, width.bit_length() - 1)
    half = jnp.bitwise_xor(jnp.right_shift(column, LANES.bit_length() - 1), side)
    index = layer_of * width + half * LANES + jnp.bitwise_and(column, LANES - 1)
    chosen = jnp.where(lax.broadcasted_iota(jnp.int32, (count, cells_total), 1) == index, 1.0, 0.0)
    picked = dot(chosen.astype(jnp.bfloat16), members, ((1,), (0,)))
    base = jnp.sum(picked, axis=1, keepdims=True) * inverse_count
    offset = column.astype(jnp.float32) - 0.5 * (width - 1)
    weight = jnp.zeros_like(values)
    for shift in (-1, 0, 1):
        distance = (shift * width + offset) / width
        weight = weight + jnp.exp(-0.5 * distance * distance) / errors
    scale = jnp.sqrt(weight)
    scaled = (picked - base) * scale
    innovation = (values - base) * scale

    high, low = split_two(scaled)
    quarters = dot(below(high, low), below(high, low), ((1,), (1,)))
    halves = quarters[:count] + quarters[count:]
    inverse, z, slope, twice = root_parts(halves[:, :count] + halves[:, count:], innovation, total_members)
    slope_high, slope_low = split_two(slope * inverse)
    both = beside(slope_high, slope_low)
    carried = dot(both, below(high, high), ((1,), (0,))) + dot(both, below(low, low), ((1,), (0,)))
    carried_high, carried_low = split_two(carried)
    turned = below(high, low)
    spread_part = dot(turned, below(carried_high, carried_high), ((0,), (0,)))
    spread_part = spread_part + dot(turned, below(carried_low, carried_low), ((0,), (0,)))
    mean_weights = jnp.sum(scaled * twice, axis=0, keepdims=True) * inverse
    size = (total_members, total_members)
    diagonal = lax.broadcasted_iota(jnp.int32, size, 0) == lax.broadcasted_iota(jnp.int32, size, 1)
    full = jnp.where(diagonal, spread_part + z, spread_part)
    weights = (full * jnp.sqrt((total_members - 1.0) * inverse) + mean_weights).astype(jnp.bfloat16)
    weights_ref[...] = weights
    for dx in range(2):
        block = answer_rows(s, weights, perturbation, mean_row, dx, 1)
        for dy in range(2):
            for layer in range(s.layers):
                at = (layer * 2 + dy) * LANES
                send_ref[2 * dx + dy, layer] = block[:, at : at + LANES]


def answer_rows(s, weights, perturbation, mean_row, dx, part):
    first = (2 * dx + part) * s.local
    block = dot(weights[first : first + s.local], perturbation, ((1,), (1,))) + mean_row[0:1]
    return block.astype(jnp.bfloat16)


def answer_kernel(s, perturbation_ref, weights_ref, mean_ref, *outs):
    for dx in range(2):
        block = answer_rows(s, weights_ref[...], perturbation_ref[...], mean_ref[...], dx, 0)
        for dy in range(2):
            for layer in range(s.layers):
                at = (layer * 2 + dy) * LANES
                outs[2 * dx + dy][0, layer] = block[:, at : at + LANES]


def join_kernel(received_ref, *refs):
    for d in range(4):
        refs[4 + d][1] = received_ref[d]


def place_rows_kernel(s, *refs):
    pieces, out_ref, rows_ref = refs[:4], refs[4], refs[5]
    mem = lax.axis_index("mem")
    odd = lax.rem(mem, 2)
    place = (mem // 2) * 2 + lax.axis_index("gy")
    for d in range(4):
        for part, parity in ((0, odd), (1, 1 - odd)):
            row = 4 * parity + jnp.bitwise_xor(place, d)
            for layer in range(s.layers):
                for octet in range(0, s.local // OCTET, 2):
                    value = pieces[d][part, layer, octet * OCTET : (octet + 2) * OCTET, :].astype(jnp.float32)
                    start = octet * OCTET * s.per_member + layer * s.rows + row
                    rows_ref[pl.ds(start, 2 * OCTET, stride=s.per_member), :] = value
    out_ref[...] = rows_ref[...].astype(jnp.bfloat16).reshape(out_ref.shape)


def vmem_call(kernel, outs, scratch, *args, aliases=None):
    spec = pl.BlockSpec(memory_space=pltpu.VMEM)
    return pl.pallas_call(
        kernel,
        out_shape=outs,
        in_specs=[spec] * len(args),
        out_specs=jax.tree.map(lambda _: spec, outs),
        scratch_shapes=[pltpu.VMEM(shape, dtype) for shape, dtype in scratch],
        input_output_aliases=aliases or {},
        compiler_params=pltpu.CompilerParams(vmem_limit_bytes=VMEM_GRANT),
    )(*args)


def on_device_tile(prior_sample_set, flow_speeds, observed_cells, observed_values, error_variance):
    local, layers, rows, columns = prior_sample_set.shape
    s = Sizes(local, layers, rows)
    n_gx = lax.axis_size("gx")
    f32, bf16 = jnp.float32, jnp.bfloat16
    shaped = jax.ShapeDtypeStruct

    pair = [(m, m ^ 1) for m in range(4)]

    def step(m):
        return 1 if m % 2 == 0 else n_gx - 1

    along = [(m * n_gx + z, m * n_gx + (z + step(m)) % n_gx) for m in range(4) for z in range(n_gx)]
    along_other = [
        (m * n_gx + z, (m ^ 1) * n_gx + (z + step(m ^ 1)) % n_gx) for m in range(4) for z in range(n_gx)
    ]
    across = [(0, 1), (1, 0)]
    diagonal = [
        ((m * n_gx + z) * 2 + y, (m * n_gx + (z + step(m)) % n_gx) * 2 + 1 - y)
        for m in range(4) for z in range(n_gx) for y in range(2)
    ]

    sib = lax.ppermute(prior_sample_set, "mem", pair).reshape(local * layers * rows, columns)
    count = observed_cells.shape[-1]
    vmem, hbm = pl.BlockSpec(memory_space=pltpu.VMEM), pl.BlockSpec(memory_space=pltpu.HBM)
    own, wind, obs, same_out, other_out = pl.pallas_call(
        functools.partial(fetch_kernel, s),
        out_shape=(
            shaped((local * layers * rows, columns), f32),
            shaped((2 * layers * rows, columns), f32),
            shaped((2 * OCTET, count), f32),
            shaped((s.halo_rows + 3 * s.wind_rows, LANES), f32),
            shaped((s.halo_rows, LANES), f32),
        ),
        in_specs=[hbm] * 5,
        out_specs=(vmem, vmem, vmem, vmem, vmem),
        scratch_shapes=[
            pltpu.VMEM((1, count), jnp.int32),
            pltpu.VMEM((1, count), f32),
            pltpu.VMEM((1, count), f32),
            pltpu.VMEM((s.wind_rows, LANES), f32),
            pltpu.SemaphoreType.DMA((5,)),
        ],
        compiler_params=pltpu.CompilerParams(vmem_limit_bytes=VMEM_GRANT),
    )(
        *(
            pltpu.with_memory_space_constraint(x, pltpu.HBM)
            for x in (
                prior_sample_set.reshape(local * layers * rows, columns),
                flow_speeds.reshape(2 * layers * rows, columns),
                observed_cells.reshape(1, count),
                observed_values.reshape(1, count),
                error_variance.reshape(1, count),
            )
        )
    )
    obs_sib = lax.ppermute(obs, "mem", pair)

    field_shape = shaped((layers * DOMAIN * EXTENT, LANES), f32)
    winds_shape = shaped((2 * layers * DOMAIN * EXTENT, LANES), f32)
    same = lax.ppermute(same_out.astype(jnp.float16), ("mem", "gx"), along).astype(f32)
    other = lax.ppermute(other_out.astype(jnp.float16), ("mem", "gx"), along_other).astype(f32)
    field, side_out, corner_out, winds = vmem_call(
        functools.partial(pack_edges_kernel, s),
        (
            field_shape,
            shaped((s.side_rows + 2 * layers * rows, LANES), f32),
            shaped((s.corner_rows + 3 * s.wind_rows, LANES), bf16),
            winds_shape,
        ),
        [],
        own, sib, wind, same_out,
    )
    side = lax.ppermute(side_out, "gy", across)
    corner = lax.ppermute(corner_out, ("mem", "gx", "gy"), diagonal)
    field, winds, first, second = vmem_call(
        functools.partial(inner_kernel, s),
        (field_shape, winds_shape, field_shape, field_shape),
        [],
        field, winds, side,
        aliases={0: 0, 1: 1},
    )
    piece = shaped((s.piece_rows, s.members), bf16)
    piece_obs = shaped((s.piece_rows + 3 * s.obs_rows, s.members), bf16)
    *pieces, _, _, _, _ = vmem_call(
        functools.partial(forecast_kernel, s),
        (piece, piece_obs, piece, piece, field_shape, winds_shape, field_shape, field_shape),
        [],
        field, winds, first, second, same, other, corner, obs_sib,
        aliases={0: 4, 1: 5, 2: 6, 3: 7},
    )

    def flip(d):
        dx, dy = d // 2, d % 2
        return [((m * 2 + y), ((m ^ (2 * dx)) * 2 + (y ^ dy))) for m in range(4) for y in range(2)]

    def exchange(parts):
        arrived = [parts[0]]
        for d in range(1, 4):
            arrived.append(lax.ppermute(parts[d], ("mem", "gy"), flip(d)))
        return arrived

    total = 4 * local
    send, perturbation, weights, mean = vmem_call(
        functools.partial(analysis_kernel, s, total),
        (
            shaped((4, layers, local, LANES), bf16),
            shaped((layers * 2 * LANES, total), bf16),
            shaped((total, total), bf16),
            shaped((OCTET, layers * 2 * LANES), f32),
        ),
        [],
        *exchange(pieces), obs,
    )
    received = lax.ppermute(send, "mem", pair)
    answer = shaped((2, layers, local, LANES), bf16)
    answers = vmem_call(
        functools.partial(answer_kernel, s), (answer, answer, answer, answer), [], perturbation, weights, mean
    )
    answers = vmem_call(
        join_kernel, (answer, answer, answer, answer), [], received, *answers, aliases={1 + d: d for d in range(4)}
    )
    return vmem_call(
        functools.partial(place_rows_kernel, s),
        shaped((local, layers, rows, columns), bf16),
        [((local * layers * rows, LANES), f32)],
        *exchange(answers),
    )


def on_device(prior_sample_set, flow_speeds, observed_cells, observed_values, error_variance):
    local, _, rows, columns = prior_sample_set.shape
    suits = (
        lax.axis_size("mem") == 4
        and lax.axis_size("gy") == 2
        and rows == 2 * HALO
        and columns == LANES
        and observed_cells.shape[-2] == 1
        and 2 * local == LANES
        and observed_cells.shape[-1] == LANES
    )
    form = on_device_tile if suits else on_device_general
    return form(prior_sample_set, flow_speeds, observed_cells, observed_values, error_variance)


def solution(mesh):
    in_specs = (
        P("mem", None, "gx", "gy"),
        P(None, None, "gx", "gy"),
        P("gx", "gy", "mem", None, None),
        P("gx", "gy", "mem", None, None),
        P("gx", "gy", "mem", None, None),
    )
    out_specs = P("mem", None, "gx", "gy")
    return jax.shard_map(
        on_device, mesh=mesh, in_specs=in_specs, out_specs=out_specs, check_vma=False
    )
```

```python
import functools

import jax
import jax.numpy as jnp
from jax import lax
from jax.experimental import pallas as pl
from jax.experimental.pallas import tpu as pltpu
from jax.sharding import PartitionSpec as P


ROOT_STEPS = 4


diffusion = 0.1
coupling = 0.2


def with_halo(block, sides, width):
    for axis, dim in sides:
        count = lax.axis_size(axis)
        forward = [(i, i + 1) for i in range(count - 1)]
        forward.append((count - 1, 0))
        backward = [(target, source) for source, target in forward]
        low = lax.ppermute(
            lax.slice_in_dim(block, block.shape[dim] - width, None, axis=dim), axis, forward
        )
        high = lax.ppermute(lax.slice_in_dim(block, 0, width, axis=dim), axis, backward)
        block = jnp.concatenate([low, block, high], axis=dim)
    return block


def tendency(model_mesh_field, wind_x, wind_y):
    centre = model_mesh_field[:, :, 1:-1, 1:-1]
    north = model_mesh_field[:, :, 2:, 1:-1]
    south = model_mesh_field[:, :, :-2, 1:-1]
    east = model_mesh_field[:, :, 1:-1, 2:]
    west = model_mesh_field[:, :, 1:-1, :-2]
    layer_mean = jnp.mean(centre, axis=1, keepdims=True)
    return (
        -0.5 * wind_x * (north - south)
        - 0.5 * wind_y * (east - west)
        + diffusion * (north + south + east + west - 4.0 * centre)
        + coupling * (layer_mean - centre)
    )


def crop_margin(array, width):
    return array[:, :, width : array.shape[2] - width, width : array.shape[3] - width]


def deep_step(model_mesh_field, wind_pad):
    padded = with_halo(model_mesh_field, (("gx", 2), ("gy", 3)), 4)
    wind_three = crop_margin(wind_pad, 1)
    wind_two = crop_margin(wind_pad, 2)
    wind_one = crop_margin(wind_pad, 3)
    wind_zero = crop_margin(wind_pad, 4)
    section_one = tendency(padded, wind_three[0], wind_three[1])
    section_two = tendency(crop_margin(padded, 1) + 0.5 * section_one, wind_two[0], wind_two[1])
    section_three = tendency(crop_margin(padded, 2) + 0.5 * section_two, wind_one[0], wind_one[1])
    section_four = tendency(crop_margin(padded, 3) + section_three, wind_zero[0], wind_zero[1])
    return (
        crop_margin(padded, 4)
        + (
            crop_margin(section_one, 3)
            + 2.0 * crop_margin(section_two, 2)
            + 2.0 * crop_margin(section_three, 1)
            + section_four
        )
        / 6.0
    )


def transform_device(weights, rolled):
    return jnp.einsum("qik,ilsqc->klsqc", weights, rolled, preferred_element_type=jnp.float32)


def analyze(strip_block, cells, values, errors, transform):
    realization_vectors, layer_stack, rows, width = strip_block.shape
    patches, count = cells.shape
    patch = width // patches
    highest = lax.Precision.HIGHEST
    mean_field = jnp.mean(strip_block, axis=0, dtype=jnp.float32)
    layer_of = cells // (rows * patch)
    row_of = cells // patch % rows
    column = cells % patch
    starts = (jnp.arange(patches, dtype=jnp.int32) * patch)[:, None]
    flat_index = layer_of * (rows * width) + row_of * width + starts + column
    picked = jnp.take(
        strip_block.reshape(realization_vectors, layer_stack * rows * width),
        flat_index.reshape(-1),
        axis=1,
    )
    base = jnp.take(mean_field.reshape(-1), flat_index.reshape(-1)).reshape(patches, count)
    spread = picked.astype(jnp.float32).reshape(realization_vectors, patches, count) - base[None]
    innovation = values - base
    offset = column.astype(jnp.float32) - 0.5 * (patch - 1)
    spread_parts = []
    innovation_parts = []
    for shift in (-1, 0, 1):
        distance = (shift * patch + jnp.roll(offset, -shift, axis=0)) / patch
        scale = jnp.sqrt(jnp.exp(-0.5 * distance * distance) / jnp.roll(errors, -shift, axis=0))
        spread_parts.append(jnp.roll(spread, -shift, axis=1) * scale[None])
        innovation_parts.append(jnp.roll(innovation, -shift, axis=0) * scale)
    scaled = jnp.concatenate(spread_parts, axis=2)
    scaled_innovation = jnp.concatenate(innovation_parts, axis=1)
    identity = jnp.eye(realization_vectors, dtype=jnp.float32)
    gram = (
        jnp.einsum("kpj,ipj->pki", scaled, scaled, precision=highest)
        + (realization_vectors - 1.0) * identity
    )
    frob = jnp.sqrt(jnp.sum(gram * gram, axis=(1, 2)))
    current = gram / frob[:, None, None]
    root = jnp.broadcast_to(identity, gram.shape)
    for _ in range(ROOT_STEPS):
        middle = 1.5 * identity - 0.5 * jnp.einsum("pab,pbc->pac", root, current, precision=highest)
        current = jnp.einsum("pab,pbc->pac", current, middle, precision=highest)
        root = jnp.einsum("pab,pbc->pac", middle, root, precision=highest)
    projected = jnp.einsum("kpj,pj->pk", scaled, scaled_innovation, precision=highest)
    once = jnp.einsum("pab,pb->pa", root, projected, precision=highest)
    twice = jnp.einsum("pab,pb->pa", root, once, precision=highest)
    mean_weights = twice / frob[:, None]
    weights = (
        jnp.sqrt(realization_vectors - 1.0) * root / jnp.sqrt(frob)[:, None, None]
        + mean_weights[:, :, None]
    ).astype(jnp.bfloat16)
    perturbation = (strip_block - mean_field[None]).astype(jnp.bfloat16)
    rolled = jnp.roll(perturbation, -(patch // 2), axis=3).reshape(
        realization_vectors, layer_stack, rows, patches, patch
    )
    first = transform(weights, rolled)
    second = transform(jnp.roll(weights, -1, axis=0), rolled)
    position = (jnp.arange(patch, dtype=jnp.float32) + 0.5) / patch
    increment = ((1.0 - position) * first + position * second).reshape(
        realization_vectors, layer_stack, rows, width
    )
    return (jnp.roll(increment, patch // 2, axis=3) + mean_field[None]).astype(jnp.bfloat16)


def on_device_general(prior_sample_set, flow_speeds, observed_cells, observed_values, error_variance):
    member_group_count = lax.axis_size("mem")
    northward_group_count = lax.axis_size("gy")
    local_member_states, layer_stack, rows_x, column_count_north = prior_sample_set.shape
    band_row_count = rows_x // (member_group_count * northward_group_count)
    all_members = local_member_states * member_group_count
    model_mesh_field = prior_sample_set
    wind_pad = with_halo(flow_speeds, (("gx", 2), ("gy", 3)), 4)
    model_mesh_field = deep_step(model_mesh_field, wind_pad)
    advance_sample_set = model_mesh_field.astype(jnp.bfloat16)
    flattened_realizations = advance_sample_set.reshape(
        local_member_states,
        layer_stack,
        northward_group_count,
        member_group_count,
        band_row_count,
        column_count_north,
    )
    flattened_realizations = flattened_realizations.transpose(3, 2, 0, 1, 4, 5).reshape(
        member_group_count * northward_group_count,
        local_member_states,
        layer_stack,
        band_row_count,
        column_count_north,
    )
    received = lax.all_to_all(
        flattened_realizations, ("mem", "gy"), split_axis=0, concat_axis=0, tiled=True
    )
    received = received.reshape(
        member_group_count,
        northward_group_count,
        local_member_states,
        layer_stack,
        band_row_count,
        column_count_north,
    )
    columns = received.transpose(0, 2, 3, 4, 1, 5).reshape(
        all_members, layer_stack, band_row_count, northward_group_count * column_count_north
    )
    cells = observed_cells.reshape(observed_cells.shape[-2], observed_cells.shape[-1])
    values = observed_values.reshape(observed_values.shape[-2], observed_values.shape[-1])
    errors = error_variance.reshape(error_variance.shape[-2], error_variance.shape[-1])
    analysed = analyze(columns, cells, values, errors, transform_device)
    outgoing = analysed.reshape(
        member_group_count,
        local_member_states,
        layer_stack,
        band_row_count,
        northward_group_count,
        column_count_north,
    )
    outgoing = outgoing.transpose(0, 4, 1, 2, 3, 5).reshape(
        member_group_count * northward_group_count,
        local_member_states,
        layer_stack,
        band_row_count,
        column_count_north,
    )
    returned = lax.all_to_all(outgoing, ("mem", "gy"), split_axis=0, concat_axis=0, tiled=True)
    returned = returned.reshape(
        member_group_count,
        northward_group_count,
        local_member_states,
        layer_stack,
        band_row_count,
        column_count_north,
    )
    return returned.transpose(2, 3, 1, 0, 4, 5).reshape(
        local_member_states, layer_stack, rows_x, column_count_north
    )


LANES = 128
HALO = 4
OCTET = 8
GROUP = 32
DOMAIN = 3 * HALO
EXTENT = LANES + 2 * OCTET
VMEM_GRANT = 24 << 20
LARGEST = 6.0
WIDENING = 11.06 / LARGEST
PRIOR_COPIES = 4
STAGE_FACTORS = (1.0 / 4.0, 1.0 / 3.0, 1.0 / 2.0, 1.0)


def split_two(x):
    high = x.astype(jnp.bfloat16)
    return high, (x - high.astype(jnp.float32)).astype(jnp.bfloat16)


def split_three(x):
    high = x.astype(jnp.bfloat16)
    rest = x - high.astype(jnp.float32)
    middle = rest.astype(jnp.bfloat16)
    return high, middle, (rest - middle.astype(jnp.float32)).astype(jnp.bfloat16)


def tile_row(odd, j):
    return jnp.where(odd == 1, DOMAIN - 1 - j, j - HALO)


def domain_row(odd, row):
    return jnp.where(odd == 1, DOMAIN - 1 - row, row + HALO)


class Sizes:
    def __init__(self, local, layers, rows):
        self.local = local
        self.layers = layers
        self.rows = rows
        self.members = 2 * local
        self.per_member = layers * rows
        self.halo_rows = HALO * LANES
        self.wind_rows = 2 * layers * HALO
        self.side_rows = layers * 2 * HALO * OCTET
        self.corner_rows = layers * HALO * OCTET
        self.piece_rows = layers * LANES
        self.obs_rows = 2 * OCTET

    def field_at(self, layer, j):
        return (layer * DOMAIN + j) * EXTENT

    def wind_at(self, part, layer, j):
        return ((part * self.layers + layer) * DOMAIN + j) * EXTENT


def columns_first(s, odd, own_ref, sib_ref, layer, j):
    start = layer * s.rows + tile_row(odd, j)
    parts = [ref[pl.ds(start, s.local, stride=s.per_member), :] for ref in (own_ref, sib_ref)]
    return jnp.concatenate(parts, axis=0).T


def wind_scale(odd, value):
    half = 0.5 / diffusion
    sign = jnp.where(odd == 1, -half, half)
    row = lax.broadcasted_iota(jnp.int32, value.shape, 0)
    return value * jnp.where(row < value.shape[0] // 2, sign, half)


def widened(u):
    v = WIDENING * jnp.abs(u)
    series = v * (1.0 + v * (1.0 / 2.0) * (1.0 + v * (1.0 / 3.0) * (1.0 + v * (1.0 / 4.0))))
    g = jnp.where(v < 0.05, series, jnp.exp(v) - 1.0)
    return jnp.where(u < 0.0, -g, g)


def narrowed(w):
    g = jnp.abs(w)
    series = g * (1.0 - g * (1.0 / 2.0 - g * (1.0 / 3.0 - g * (1.0 / 4.0 - g * (1.0 / 5.0)))))
    u = jnp.where(g < 0.05, series, jnp.log(1.0 + g)) * (1.0 / WIDENING)
    return jnp.where(w < 0.0, -u, u)


def fetch_kernel(
    s, prior_ref, wind_ref, cells_ref, values_ref, errors_ref,
    own_ref, wind_out_ref, obs_ref, same_ref, other_ref,
    cells_vmem, values_vmem, errors_vmem, rows_ref, sems,
):
    odd = lax.rem(lax.axis_index("mem"), 2)
    copies = [
        pltpu.make_async_copy(source, target, sems.at[i])
        for i, (source, target) in enumerate(
            (
                (cells_ref, cells_vmem), (values_ref, values_vmem), (errors_ref, errors_vmem),
                (wind_ref, wind_out_ref),
            )
        )
    ]
    share = own_ref.shape[0] // PRIOR_COPIES
    for i in range(PRIOR_COPIES):
        part = pl.ds(i * share, share)
        copies.append(pltpu.make_async_copy(prior_ref.at[part], own_ref.at[part], sems.at[4 + i]))
    for copy in copies[4:] + copies[:4]:
        copy.start()
    obs_ref[...] = jnp.zeros_like(obs_ref)
    for copy in copies[:4]:
        copy.wait()
    obs_ref[0:1, :] = cells_vmem[...].astype(jnp.float32)
    obs_ref[1:2, :] = values_vmem[...]
    obs_ref[2:3, :] = errors_vmem[...]
    for block in range(2 * s.layers):
        for j in range(HALO):
            row = block * s.rows + tile_row(odd, 2 * HALO + j)
            rows_ref[pl.ds(block * HALO + j, 1), :] = wind_out_ref[pl.ds(row, 1), :]
    for i, part in enumerate(split_three(wind_scale(odd, rows_ref[...]))):
        same_ref[pl.ds(s.halo_rows + i * s.wind_rows, s.wind_rows), :] = part.astype(jnp.float32)
    for copy in copies[4:]:
        copy.wait()
    for parity, out_ref in ((odd, same_ref), (1 - odd, other_ref)):
        for j in range(HALO):
            row = tile_row(parity, 2 * HALO + j)
            parts = [own_ref[pl.ds(layer * s.rows + row, s.local, stride=s.per_member), :] for layer in range(s.layers)]
            value = jnp.concatenate(parts, axis=0).T
            out_ref[pl.ds(j * LANES, LANES), :] = widened(value) if j == HALO - 1 else value


def spread(parts, rows, targets, store):
    stacked = jnp.concatenate(parts, axis=0)
    turned = stacked.T
    source = lax.broadcasted_iota(jnp.int32, (stacked.shape[0], LANES), 0)
    for first, second in zip(targets[::2], targets[1::2], strict=True):
        chosen = [jnp.where(lax.rem(source, rows) == row, 1.0, 0.0) for row in (first, second)]
        both = dot(turned, jnp.concatenate(chosen, axis=1).astype(jnp.bfloat16), ((1,), (0,)))
        store(first, both[:, :LANES])
        store(second, both[:, LANES:])


def column_ends(x):
    turned = padded_rows(x).T
    return jnp.concatenate([turned[LANES - HALO :], turned[:HALO]], axis=0)


def packed_ends(x):
    parts = [part.astype(jnp.float32) for part in split_three(column_ends(x))]
    packed = parts[0] + pltpu.roll(parts[1], GROUP, 1) + pltpu.roll(parts[2], 2 * GROUP, 1)
    return jnp.concatenate([packed, jnp.zeros_like(packed)], axis=0).astype(jnp.bfloat16)


def unpacked_ends(x):
    packed = x.astype(jnp.float32)[: 2 * HALO]
    return packed + pltpu.roll(packed, LANES - GROUP, 1) + pltpu.roll(packed, LANES - 2 * GROUP, 1)


def pack_edges_kernel(s, own_ref, sib_ref, wind_ref, same_ref, field_ref, side_ref, corner_ref):
    odd = lax.rem(lax.axis_index("mem"), 2)
    for layer in range(s.layers):
        rows = []
        for j in range(HALO, DOMAIN):
            value = columns_first(s, odd, own_ref, sib_ref, layer, j)
            field_ref[pl.ds(s.field_at(layer, j) + OCTET, LANES), :] = value
            rows += [value[LANES - HALO :], value[:HALO]]
        count = len(rows) // 2
        high, low = split_two(jnp.concatenate(rows, axis=0))
        side_ref[pl.ds(layer * 2 * HALO * OCTET, 2 * HALO * OCTET), :] = high
        low = low.astype(jnp.float32)
        nearest = [low[i * OCTET + 2 : i * OCTET + 6] for i in range(2 * HALO)]
        at = s.side_rows + 2 * OCTET + layer * 2 * HALO * HALO
        side_ref[pl.ds(at, 2 * HALO * HALO), :] = jnp.concatenate(nearest, axis=0).astype(jnp.bfloat16)
        corner_ref[pl.ds(layer * HALO * OCTET, HALO * OCTET), :] = jnp.concatenate(rows[count:], axis=0).astype(jnp.bfloat16)
    near = [same_ref[pl.ds(s.halo_rows + i * s.wind_rows, s.wind_rows), :] for i in range(3)]
    corner_ref[pl.ds(s.corner_rows, 2 * OCTET), :] = packed_ends(near[0] + near[1] + near[2])
    side_ref[pl.ds(s.side_rows, 2 * OCTET), :] = packed_ends(wind_scale(odd, wind_ref[...]))


def spread_winds_kernel(s, wind_ref, winds_ref):
    odd = lax.rem(lax.axis_index("mem"), 2)
    scaled = wind_scale(odd, wind_ref[...])

    def store(row, value):
        at = s.wind_at(row // s.rows // s.layers, row // s.rows % s.layers, domain_row(odd, row % s.rows))
        winds_ref[pl.ds(pl.multiple_of(at, OCTET) + OCTET, LANES), :] = value

    rows = 2 * s.layers * s.rows
    spread(split_three(scaled), rows, list(range(rows)), store)


def set_wind_edges(winds_ref, ends, row, at):
    value = jnp.broadcast_to(ends[:, row : row + 1], (2 * HALO, LANES))
    winds_ref[pl.ds(at + HALO, HALO), :] = value[:HALO]
    winds_ref[pl.ds(at + OCTET + LANES, HALO), :] = value[HALO:]


def padded_rows(x):
    return jnp.concatenate([x, jnp.zeros((LANES - x.shape[0], LANES), x.dtype)], axis=0)


def set_field_edges(s, field_ref, layer, j, edge):
    at = s.field_at(layer, j)
    field_ref[pl.ds(at + HALO, HALO), :] = edge[:HALO]
    field_ref[pl.ds(at + OCTET + LANES, HALO), :] = edge[HALO:]


def evaluate(s, field_ref, winds_ref, from_ref, stage, start, wanted, emit):
    factor, share = STAGE_FACTORS[stage] * diffusion, coupling / s.layers / diffusion
    own_share = 4.0 + coupling / diffusion - share
    centre = {}
    for j in range(wanted[0] - 1, wanted[1] + 1):
        for layer in range(s.layers):
            centre[layer, j] = from_ref[pl.ds(s.field_at(layer, j) + start, OCTET), :]
    for j in range(*wanted):
        for layer in range(s.layers):
            at = s.field_at(layer, j) + start
            others = sum(centre[k, j] for k in range(s.layers) if k != layer)
            north, south = centre[layer, j + 1], centre[layer, j - 1]
            east, west = from_ref[pl.ds(at + 1, OCTET), :], from_ref[pl.ds(at - 1, OCTET), :]
            along = winds_ref[pl.ds(s.wind_at(0, layer, j) + start, OCTET), :]
            across = winds_ref[pl.ds(s.wind_at(1, layer, j) + start, OCTET), :]
            total = along * (south - north) + across * (west - east)
            total = total + ((north + south) + (east + west))
            total = total + ((others if share == 1.0 else share * others) - own_share * centre[layer, j])
            emit(layer, j, field_ref[pl.ds(at, OCTET), :] + factor * total)


def run_stage(s, field_ref, winds_ref, from_ref, to_ref, stage, wanted):
    def step(i, carry):
        for k in range(2):
            start = 2 * OCTET * i + OCTET * k

            def emit(layer, j, value):
                to_ref[pl.ds(s.field_at(layer, j) + start, OCTET), :] = value

            evaluate(s, field_ref, winds_ref, from_ref, stage, start, wanted, emit)
        return carry

    lax.fori_loop(0, EXTENT // (2 * OCTET), step, 0)


def inner_kernel(s, _, __, side_ref, field_ref, winds_ref, first_ref, second_ref):
    odd = lax.rem(lax.axis_index("mem"), 2)
    for layer in range(s.layers):
        edges = side_ref[pl.ds(layer * 2 * HALO * OCTET, 2 * HALO * OCTET), :].astype(jnp.float32)
        at = s.side_rows + 2 * OCTET + layer * 2 * HALO * HALO
        low = side_ref[pl.ds(at, 2 * HALO * HALO), :].astype(jnp.float32)
        for j in range(HALO, DOMAIN):
            i = j - HALO
            edge = edges[i * OCTET : (i + 1) * OCTET]
            nearest = edge[2:6] + low[i * HALO : (i + 1) * HALO]
            set_field_edges(s, field_ref, layer, j, jnp.concatenate([edge[:2], nearest, edge[6:]], axis=0))
    beside = unpacked_ends(side_ref[pl.ds(s.side_rows, 2 * OCTET), :])
    for block in range(2 * s.layers):
        for row in range(s.rows):
            at = s.wind_at(block // s.layers, block % s.layers, domain_row(odd, row))
            set_wind_edges(winds_ref, beside, block * s.rows + row, pl.multiple_of(at, OCTET))
    refs = (field_ref, first_ref, second_ref, first_ref)
    for stage in range(3):
        wanted = (HALO + 1 + stage, DOMAIN - 1 - stage)
        run_stage(s, field_ref, winds_ref, refs[stage], refs[stage + 1], stage, wanted)


def forecast_kernel(
    s, _, __, ___, ____, same_ref, other_ref, corner_ref, obs_ref,
    out0_ref, out1_ref, out2_ref, out3_ref, field_ref, winds_ref, first_ref, second_ref,
):
    mem = lax.axis_index("mem")
    odd = lax.rem(mem, 2)
    place = (mem // 2) * 2 + lax.axis_index("gy")

    lower = lax.broadcasted_iota(jnp.int32, (LANES, LANES), 1) < s.local
    for j in range(HALO):
        both = []
        for ref in (same_ref, other_ref):
            value = ref[pl.ds(j * LANES, LANES), :]
            both.append(narrowed(value) if j == HALO - 1 else value)
        same, other = both
        layer_fields = (
            jnp.where(lower, same, pltpu.roll(other, s.local, 1)),
            jnp.where(lower, pltpu.roll(same, s.local, 1), other),
        )
        for layer, value in enumerate(layer_fields):
            field_ref[pl.ds(s.field_at(layer, j) + OCTET, LANES), :] = value
    for layer in range(s.layers):
        corner = corner_ref[pl.ds(layer * HALO * OCTET, HALO * OCTET), :].astype(jnp.float32)
        for j in range(HALO):
            set_field_edges(s, field_ref, layer, j, corner[j * OCTET : (j + 1) * OCTET])
    beyond = unpacked_ends(corner_ref[pl.ds(s.corner_rows, 2 * OCTET), :])
    targets = [block * HALO + j for block in range(2 * s.layers) for j in range(1, HALO)]

    def wind_at(row):
        return s.wind_at(row // HALO // s.layers, row // HALO % s.layers, row % HALO)

    for row in targets:
        set_wind_edges(winds_ref, beyond, row, wind_at(row))

    def store(row, value):
        winds_ref[pl.ds(wind_at(row) + OCTET, LANES), :] = value

    near = [same_ref[pl.ds(s.halo_rows + i * s.wind_rows, s.wind_rows), :].astype(jnp.bfloat16) for i in range(3)]
    spread(near, s.wind_rows, targets, store)

    refs = (field_ref, first_ref, second_ref, first_ref)
    for stage in range(3):
        wanted = (1 + stage, HALO + 1 + stage)
        run_stage(s, field_ref, winds_ref, refs[stage], refs[stage + 1], stage, wanted)

    for i, part in enumerate(split_three(obs_ref[...])):
        out1_ref[pl.ds(s.piece_rows + i * s.obs_rows, s.obs_rows), :] = part
    swap_one = jnp.bitwise_xor(jnp.bitwise_and(place, 1), odd) == 1
    swap_two = jnp.bitwise_xor(place // 2, odd) == 1
    outs = (out0_ref, out1_ref, out2_ref, out3_ref)

    def last_step(i, carry):
        results = [{}, {}]
        for k in range(2):
            start = OCTET + 2 * OCTET * i + OCTET * k
            emit = lambda layer, j, value: results[k].update({(layer, j): value})
            evaluate(s, field_ref, winds_ref, first_ref, 3, start, (HALO, 2 * HALO), emit)
        at = pl.multiple_of(2 * OCTET * i, 2 * OCTET)
        for layer in range(s.layers):
            rows = [
                jnp.concatenate([result[layer, HALO + t] for result in results], axis=0).astype(jnp.bfloat16)
                for t in range(HALO)
            ]
            rows = [jnp.where(swap_one, rows[t ^ 1], rows[t]) for t in range(HALO)]
            rows = [jnp.where(swap_two, rows[t ^ 2], rows[t]) for t in range(HALO)]
            for d, out_ref in enumerate(outs):
                out_ref[pl.ds(layer * LANES + at, 2 * OCTET), :] = rows[d]
        return carry

    lax.fori_loop(0, LANES // (2 * OCTET), last_step, 0)


def dot(a, b, contract):
    return lax.dot_general(a, b, (contract, ((), ())), preferred_element_type=jnp.float32)


def beside(*parts):
    return jnp.concatenate(parts, axis=1)


def below(*parts):
    return jnp.concatenate(parts, axis=0)


def dot_split(a, b):
    (a_high, a_low), (b_high, b_low) = split_two(a), split_two(b)
    row = beside(b_high, b_low)
    both = dot(beside(a_high, a_low), below(row, row), ((1,), (0,)))
    return both[:, : b.shape[1]] + both[:, b.shape[1] :]


def root_parts(product, vector, total_members):
    count = product.shape[0]
    size = (count, count)
    diagonal = lax.broadcasted_iota(jnp.int32, size, 0) == lax.broadcasted_iota(jnp.int32, size, 1)

    def total(x):
        return jnp.sum(jnp.sum(x, axis=0, keepdims=True), axis=1, keepdims=True)

    def plus(x, scalar):
        return jnp.where(diagonal, x + scalar, x)

    def twice(matrix, column):
        once = jnp.sum(matrix * column, axis=0, keepdims=True)
        return jnp.sum(matrix * once, axis=1, keepdims=True)

    least = total_members - 1.0
    trace = total(jnp.where(diagonal, product, 0.0))
    square = total(product * product) + (2.0 * least) * trace + least * least * total_members
    inverse = lax.rsqrt(square)
    b = product * inverse
    x = least * inverse
    z = jnp.ones_like(x)
    m = 1.5 - 0.5 * x
    middle = plus(-0.5 * b, m)
    y = plus((0.25 * x - m) * b + 0.25 * dot_split(b, b), -x * m)
    near = plus(m * m * b + dot_split(y, b), m * m * x)
    slope = plus(y, m * m)
    x, z = x * m * m, m
    root = middle
    vector = twice(middle, vector)
    root_slope = jnp.where(diagonal, -0.5, 0.0)
    for step in range(1, ROOT_STEPS):
        m = 1.5 - 0.5 * x
        middle = plus(-0.5 * near, 1.5)
        root_slope = m * root_slope - 0.5 * dot_split(slope, root)
        vector = twice(middle, vector)
        z = m * z
        if step < ROOT_STEPS - 1:
            root = dot_split(middle, root)
            rest = plus(near, -x)
            y = dot_split(near, plus(0.25 * rest, -m))
            slope = m * m * slope + dot_split(y, slope)
            near = m * m * near + dot_split(y, rest)
            x = x * m * m
    return inverse, z, root_slope, vector


def analysis_kernel(
    s, total_members, piece0_ref, piece1_ref, piece2_ref, piece3_ref, obs_ref,
    send_ref, perturbation_ref, weights_ref, mean_ref,
):
    mem, side = lax.axis_index("mem"), lax.axis_index("gy")
    pieces = (piece0_ref, piece1_ref, piece2_ref, piece3_ref)
    width = 2 * LANES
    cells_total = s.layers * width
    inverse_count = 1.0 / total_members
    members = beside(
        *(
            below(*(pieces[2 * dx + dy][layer * LANES : (layer + 1) * LANES] for layer in range(s.layers) for dy in range(2)))
            for dx in range(2)
        )
    )
    mean_row = dot(jnp.ones((OCTET, total_members), jnp.bfloat16), members, ((1,), (1,))) * inverse_count
    mean = dot(members, jnp.ones((total_members, LANES), jnp.bfloat16), ((1,), (0,))) * inverse_count
    perturbation = beside(
        *(
            (members[:, i : i + LANES].astype(jnp.float32) - mean).astype(jnp.bfloat16)
            for i in range(0, total_members, LANES)
        )
    )
    perturbation_ref[...] = perturbation
    mean_ref[...] = mean_row

    count = obs_ref.shape[1]
    far = [piece1_ref[pl.ds(s.piece_rows + i * s.obs_rows, s.obs_rows), :].astype(jnp.float32) for i in range(3)]
    mine = lax.rem(mem, 2) == side
    obs = padded_rows(jnp.where(mine, obs_ref[...], far[0] + far[1] + far[2])).T
    cells = obs[:, 0:1].astype(jnp.int32)
    values, errors = obs[:, 1:2], obs[:, 2:3]
    column = jnp.bitwise_and(cells, width - 1)
    layer_of = jnp.right_shift(cells, width.bit_length() - 1)
    half = jnp.bitwise_xor(jnp.right_shift(column, LANES.bit_length() - 1), side)
    index = layer_of * width + half * LANES + jnp.bitwise_and(column, LANES - 1)
    chosen = jnp.where(lax.broadcasted_iota(jnp.int32, (count, cells_total), 1) == index, 1.0, 0.0)
    picked = dot(chosen.astype(jnp.bfloat16), members, ((1,), (0,)))
    base = jnp.sum(picked, axis=1, keepdims=True) * inverse_count
    offset = column.astype(jnp.float32) - 0.5 * (width - 1)
    weight = jnp.zeros_like(values)
    for shift in (-1, 0, 1):
        distance = (shift * width + offset) / width
        weight = weight + jnp.exp(-0.5 * distance * distance) / errors
    scale = jnp.sqrt(weight)
    scaled = (picked - base) * scale
    innovation = (values - base) * scale

    high, low = split_two(scaled)
    quarters = dot(below(high, low), below(high, low), ((1,), (1,)))
    halves = quarters[:count] + quarters[count:]
    inverse, z, slope, twice = root_parts(halves[:, :count] + halves[:, count:], innovation, total_members)
    slope_high, slope_low = split_two(slope * inverse)
    both = beside(slope_high, slope_low)
    carried = dot(both, below(high, high), ((1,), (0,))) + dot(both, below(low, low), ((1,), (0,)))
    carried_high, carried_low = split_two(carried)
    turned = below(high, low)
    spread_part = dot(turned, below(carried_high, carried_high), ((0,), (0,)))
    spread_part = spread_part + dot(turned, below(carried_low, carried_low), ((0,), (0,)))
    mean_weights = jnp.sum(scaled * twice, axis=0, keepdims=True) * inverse
    size = (total_members, total_members)
    diagonal = lax.broadcasted_iota(jnp.int32, size, 0) == lax.broadcasted_iota(jnp.int32, size, 1)
    full = jnp.where(diagonal, spread_part + z, spread_part)
    weights = (full * jnp.sqrt((total_members - 1.0) * inverse) + mean_weights).astype(jnp.bfloat16)
    weights_ref[...] = weights
    for dx in range(2):
        block = answer_rows(s, weights, perturbation, mean_row, dx, 1)
        for dy in range(2):
            for layer in range(s.layers):
                at = (layer * 2 + dy) * LANES
                send_ref[2 * dx + dy, layer] = block[:, at : at + LANES]


def answer_rows(s, weights, perturbation, mean_row, dx, part):
    first = (2 * dx + part) * s.local
    block = dot(weights[first : first + s.local], perturbation, ((1,), (1,))) + mean_row[0:1]
    return block.astype(jnp.bfloat16)


def answer_kernel(s, perturbation_ref, weights_ref, mean_ref, *outs):
    for dx in range(2):
        block = answer_rows(s, weights_ref[...], perturbation_ref[...], mean_ref[...], dx, 0)
        for dy in range(2):
            for layer in range(s.layers):
                at = (layer * 2 + dy) * LANES
                outs[2 * dx + dy][0, layer] = block[:, at : at + LANES]


def join_kernel(received_ref, *refs):
    for d in range(4):
        refs[4 + d][1] = received_ref[d]


def place_rows_kernel(s, *refs):
    pieces, out_ref, rows_ref, packed_ref, sems = refs[:4], refs[4], refs[5], refs[6], refs[7]
    mem = lax.axis_index("mem")
    odd = lax.rem(mem, 2)
    place = (mem // 2) * 2 + lax.axis_index("gy")
    count = 2 * OCTET
    copies = []
    for first in range(0, s.local, count):
        for d in range(4):
            for part, parity in ((0, odd), (1, 1 - odd)):
                row = 4 * parity + jnp.bitwise_xor(place, d)
                for layer in range(s.layers):
                    value = pieces[d][part, layer, first : first + count, :].astype(jnp.float32)
                    start = first * s.per_member + layer * s.rows + row
                    rows_ref[pl.ds(start, count, stride=s.per_member), :] = value
        rows = rows_ref[pl.ds(first * s.per_member, count * s.per_member), :]
        packed_ref[pl.ds(first, count)] = rows.astype(jnp.bfloat16).reshape(count, s.layers, s.rows, LANES)
        copies.append(
            pltpu.make_async_copy(
                packed_ref.at[pl.ds(first, count)], out_ref.at[pl.ds(first, count)], sems.at[first // count]
            )
        )
        copies[-1].start()
    for copy in copies:
        copy.wait()


def vmem_call(kernel, outs, scratch, *args, aliases=None):
    spec = pl.BlockSpec(memory_space=pltpu.VMEM)
    return pl.pallas_call(
        kernel,
        out_shape=outs,
        in_specs=[spec] * len(args),
        out_specs=jax.tree.map(lambda _: spec, outs),
        scratch_shapes=[pltpu.VMEM(shape, dtype) for shape, dtype in scratch],
        input_output_aliases=aliases or {},
        compiler_params=pltpu.CompilerParams(vmem_limit_bytes=VMEM_GRANT),
    )(*args)


def on_device_tile(prior_sample_set, flow_speeds, observed_cells, observed_values, error_variance):
    local, layers, rows, columns = prior_sample_set.shape
    s = Sizes(local, layers, rows)
    n_gx = lax.axis_size("gx")
    f32, bf16 = jnp.float32, jnp.bfloat16
    shaped = jax.ShapeDtypeStruct

    pair = [(m, m ^ 1) for m in range(4)]

    def step(m):
        return 1 if m % 2 == 0 else n_gx - 1

    along = [(m * n_gx + z, m * n_gx + (z + step(m)) % n_gx) for m in range(4) for z in range(n_gx)]
    along_other = [
        (m * n_gx + z, (m ^ 1) * n_gx + (z + step(m ^ 1)) % n_gx) for m in range(4) for z in range(n_gx)
    ]
    across = [(0, 1), (1, 0)]
    diagonal = [
        ((m * n_gx + z) * 2 + y, (m * n_gx + (z + step(m)) % n_gx) * 2 + 1 - y)
        for m in range(4) for z in range(n_gx) for y in range(2)
    ]

    sib = lax.ppermute(prior_sample_set, "mem", pair).reshape(local * layers * rows, columns)
    count = observed_cells.shape[-1]
    vmem, hbm = pl.BlockSpec(memory_space=pltpu.VMEM), pl.BlockSpec(memory_space=pltpu.HBM)
    own, wind, obs, same_out, other_out = pl.pallas_call(
        functools.partial(fetch_kernel, s),
        out_shape=(
            shaped((local * layers * rows, columns), f32),
            shaped((2 * layers * rows, columns), f32),
            shaped((2 * OCTET, count), f32),
            shaped((s.halo_rows + 3 * s.wind_rows, LANES), f32),
            shaped((s.halo_rows, LANES), f32),
        ),
        in_specs=[hbm] * 5,
        out_specs=(vmem, vmem, vmem, vmem, vmem),
        scratch_shapes=[
            pltpu.VMEM((1, count), jnp.int32),
            pltpu.VMEM((1, count), f32),
            pltpu.VMEM((1, count), f32),
            pltpu.VMEM((s.wind_rows, LANES), f32),
            pltpu.SemaphoreType.DMA((4 + PRIOR_COPIES,)),
        ],
        compiler_params=pltpu.CompilerParams(vmem_limit_bytes=VMEM_GRANT),
    )(
        *(
            pltpu.with_memory_space_constraint(x, pltpu.HBM)
            for x in (
                prior_sample_set.reshape(local * layers * rows, columns),
                flow_speeds.reshape(2 * layers * rows, columns),
                observed_cells.reshape(1, count),
                observed_values.reshape(1, count),
                error_variance.reshape(1, count),
            )
        )
    )
    obs_sib = lax.ppermute(obs, "mem", pair)

    field_shape = shaped((layers * DOMAIN * EXTENT, LANES), f32)
    winds_shape = shaped((2 * layers * DOMAIN * EXTENT, LANES), f32)
    same = lax.ppermute(same_out.astype(jnp.float16), ("mem", "gx"), along).astype(f32)
    other = lax.ppermute(other_out.astype(jnp.float16), ("mem", "gx"), along_other).astype(f32)
    field, side_out, corner_out = vmem_call(
        functools.partial(pack_edges_kernel, s),
        (
            field_shape,
            shaped((s.side_rows + 2 * OCTET + layers * 2 * HALO * HALO, LANES), bf16),
            shaped((s.corner_rows + 2 * OCTET, LANES), bf16),
        ),
        [],
        own, sib, wind, same_out,
    )
    winds = vmem_call(functools.partial(spread_winds_kernel, s), winds_shape, [], wind)
    side = lax.ppermute(side_out, "gy", across)
    corner = lax.ppermute(corner_out, ("mem", "gx", "gy"), diagonal)
    field, winds, first, second = vmem_call(
        functools.partial(inner_kernel, s),
        (field_shape, winds_shape, field_shape, field_shape),
        [],
        field, winds, side,
        aliases={0: 0, 1: 1},
    )
    piece = shaped((s.piece_rows, s.members), bf16)
    piece_obs = shaped((s.piece_rows + 3 * s.obs_rows, s.members), bf16)
    *pieces, _, _, _, _ = vmem_call(
        functools.partial(forecast_kernel, s),
        (piece, piece_obs, piece, piece, field_shape, winds_shape, field_shape, field_shape),
        [],
        field, winds, first, second, same, other, corner, obs_sib,
        aliases={0: 4, 1: 5, 2: 6, 3: 7},
    )

    def flip(d):
        dx, dy = d // 2, d % 2
        return [((m * 2 + y), ((m ^ (2 * dx)) * 2 + (y ^ dy))) for m in range(4) for y in range(2)]

    def exchange(parts):
        arrived = [parts[0]]
        for d in range(1, 4):
            arrived.append(lax.ppermute(parts[d], ("mem", "gy"), flip(d)))
        return arrived

    total = 4 * local
    send, perturbation, weights, mean = vmem_call(
        functools.partial(analysis_kernel, s, total),
        (
            shaped((4, layers, local, LANES), bf16),
            shaped((layers * 2 * LANES, total), bf16),
            shaped((total, total), bf16),
            shaped((OCTET, layers * 2 * LANES), f32),
        ),
        [],
        *exchange(pieces), obs,
    )
    received = lax.ppermute(send, "mem", pair)
    answer = shaped((2, layers, local, LANES), bf16)
    answers = vmem_call(
        functools.partial(answer_kernel, s), (answer, answer, answer, answer), [], perturbation, weights, mean
    )
    answers = vmem_call(
        join_kernel, (answer, answer, answer, answer), [], received, *answers, aliases={1 + d: d for d in range(4)}
    )
    return pl.pallas_call(
        functools.partial(place_rows_kernel, s),
        out_shape=shaped((local, layers, rows, columns), bf16),
        in_specs=[vmem] * 4,
        out_specs=hbm,
        scratch_shapes=[
            pltpu.VMEM((local * layers * rows, LANES), f32),
            pltpu.VMEM((local, layers, rows, columns), bf16),
            pltpu.SemaphoreType.DMA((local // (2 * OCTET),)),
        ],
        compiler_params=pltpu.CompilerParams(vmem_limit_bytes=VMEM_GRANT),
    )(*exchange(answers))


def on_device(prior_sample_set, flow_speeds, observed_cells, observed_values, error_variance):
    local, _, rows, columns = prior_sample_set.shape
    suits = (
        lax.axis_size("mem") == 4
        and lax.axis_size("gy") == 2
        and rows == 2 * HALO
        and columns == LANES
        and observed_cells.shape[-2] == 1
        and 2 * local == LANES
        and observed_cells.shape[-1] == LANES
    )
    form = on_device_tile if suits else on_device_general
    return form(prior_sample_set, flow_speeds, observed_cells, observed_values, error_variance)


def solution(mesh):
    in_specs = (
        P("mem", None, "gx", "gy"),
        P(None, None, "gx", "gy"),
        P("gx", "gy", "mem", None, None),
        P("gx", "gy", "mem", None, None),
        P("gx", "gy", "mem", None, None),
    )
    out_specs = P("mem", None, "gx", "gy")
    return jax.shard_map(
        on_device, mesh=mesh, in_specs=in_specs, out_specs=out_specs, check_vma=False
    )
```

```python
import functools

import jax
import jax.numpy as jnp
from jax import lax
from jax.experimental import pallas as pl
from jax.experimental.pallas import tpu as pltpu
from jax.sharding import PartitionSpec as P


ROOT_STEPS = 4


diffusion = 0.1
coupling = 0.2


def with_halo(block, sides, width):
    for axis, dim in sides:
        count = lax.axis_size(axis)
        forward = [(i, i + 1) for i in range(count - 1)]
        forward.append((count - 1, 0))
        backward = [(target, source) for source, target in forward]
        low = lax.ppermute(
            lax.slice_in_dim(block, block.shape[dim] - width, None, axis=dim), axis, forward
        )
        high = lax.ppermute(lax.slice_in_dim(block, 0, width, axis=dim), axis, backward)
        block = jnp.concatenate([low, block, high], axis=dim)
    return block


def tendency(model_mesh_field, wind_x, wind_y):
    centre = model_mesh_field[:, :, 1:-1, 1:-1]
    north = model_mesh_field[:, :, 2:, 1:-1]
    south = model_mesh_field[:, :, :-2, 1:-1]
    east = model_mesh_field[:, :, 1:-1, 2:]
    west = model_mesh_field[:, :, 1:-1, :-2]
    layer_mean = jnp.mean(centre, axis=1, keepdims=True)
    return (
        -0.5 * wind_x * (north - south)
        - 0.5 * wind_y * (east - west)
        + diffusion * (north + south + east + west - 4.0 * centre)
        + coupling * (layer_mean - centre)
    )


def crop_margin(array, width):
    return array[:, :, width : array.shape[2] - width, width : array.shape[3] - width]


def deep_step(model_mesh_field, wind_pad):
    padded = with_halo(model_mesh_field, (("gx", 2), ("gy", 3)), 4)
    wind_three = crop_margin(wind_pad, 1)
    wind_two = crop_margin(wind_pad, 2)
    wind_one = crop_margin(wind_pad, 3)
    wind_zero = crop_margin(wind_pad, 4)
    section_one = tendency(padded, wind_three[0], wind_three[1])
    section_two = tendency(crop_margin(padded, 1) + 0.5 * section_one, wind_two[0], wind_two[1])
    section_three = tendency(crop_margin(padded, 2) + 0.5 * section_two, wind_one[0], wind_one[1])
    section_four = tendency(crop_margin(padded, 3) + section_three, wind_zero[0], wind_zero[1])
    return (
        crop_margin(padded, 4)
        + (
            crop_margin(section_one, 3)
            + 2.0 * crop_margin(section_two, 2)
            + 2.0 * crop_margin(section_three, 1)
            + section_four
        )
        / 6.0
    )


def transform_device(weights, rolled):
    return jnp.einsum("qik,ilsqc->klsqc", weights, rolled, preferred_element_type=jnp.float32)


def analyze(strip_block, cells, values, errors, transform):
    realization_vectors, layer_stack, rows, width = strip_block.shape
    patches, count = cells.shape
    patch = width // patches
    highest = lax.Precision.HIGHEST
    mean_field = jnp.mean(strip_block, axis=0, dtype=jnp.float32)
    layer_of = cells // (rows * patch)
    row_of = cells // patch % rows
    column = cells % patch
    starts = (jnp.arange(patches, dtype=jnp.int32) * patch)[:, None]
    flat_index = layer_of * (rows * width) + row_of * width + starts + column
    picked = jnp.take(
        strip_block.reshape(realization_vectors, layer_stack * rows * width),
        flat_index.reshape(-1),
        axis=1,
    )
    base = jnp.take(mean_field.reshape(-1), flat_index.reshape(-1)).reshape(patches, count)
    spread = picked.astype(jnp.float32).reshape(realization_vectors, patches, count) - base[None]
    innovation = values - base
    offset = column.astype(jnp.float32) - 0.5 * (patch - 1)
    spread_parts = []
    innovation_parts = []
    for shift in (-1, 0, 1):
        distance = (shift * patch + jnp.roll(offset, -shift, axis=0)) / patch
        scale = jnp.sqrt(jnp.exp(-0.5 * distance * distance) / jnp.roll(errors, -shift, axis=0))
        spread_parts.append(jnp.roll(spread, -shift, axis=1) * scale[None])
        innovation_parts.append(jnp.roll(innovation, -shift, axis=0) * scale)
    scaled = jnp.concatenate(spread_parts, axis=2)
    scaled_innovation = jnp.concatenate(innovation_parts, axis=1)
    identity = jnp.eye(realization_vectors, dtype=jnp.float32)
    gram = (
        jnp.einsum("kpj,ipj->pki", scaled, scaled, precision=highest)
        + (realization_vectors - 1.0) * identity
    )
    frob = jnp.sqrt(jnp.sum(gram * gram, axis=(1, 2)))
    current = gram / frob[:, None, None]
    root = jnp.broadcast_to(identity, gram.shape)
    for _ in range(ROOT_STEPS):
        middle = 1.5 * identity - 0.5 * jnp.einsum("pab,pbc->pac", root, current, precision=highest)
        current = jnp.einsum("pab,pbc->pac", current, middle, precision=highest)
        root = jnp.einsum("pab,pbc->pac", middle, root, precision=highest)
    projected = jnp.einsum("kpj,pj->pk", scaled, scaled_innovation, precision=highest)
    once = jnp.einsum("pab,pb->pa", root, projected, precision=highest)
    twice = jnp.einsum("pab,pb->pa", root, once, precision=highest)
    mean_weights = twice / frob[:, None]
    weights = (
        jnp.sqrt(realization_vectors - 1.0) * root / jnp.sqrt(frob)[:, None, None]
        + mean_weights[:, :, None]
    ).astype(jnp.bfloat16)
    perturbation = (strip_block - mean_field[None]).astype(jnp.bfloat16)
    rolled = jnp.roll(perturbation, -(patch // 2), axis=3).reshape(
        realization_vectors, layer_stack, rows, patches, patch
    )
    first = transform(weights, rolled)
    second = transform(jnp.roll(weights, -1, axis=0), rolled)
    position = (jnp.arange(patch, dtype=jnp.float32) + 0.5) / patch
    increment = ((1.0 - position) * first + position * second).reshape(
        realization_vectors, layer_stack, rows, width
    )
    return (jnp.roll(increment, patch // 2, axis=3) + mean_field[None]).astype(jnp.bfloat16)


def on_device_general(prior_sample_set, flow_speeds, observed_cells, observed_values, error_variance):
    member_group_count = lax.axis_size("mem")
    northward_group_count = lax.axis_size("gy")
    local_member_states, layer_stack, rows_x, column_count_north = prior_sample_set.shape
    band_row_count = rows_x // (member_group_count * northward_group_count)
    all_members = local_member_states * member_group_count
    model_mesh_field = prior_sample_set
    wind_pad = with_halo(flow_speeds, (("gx", 2), ("gy", 3)), 4)
    model_mesh_field = deep_step(model_mesh_field, wind_pad)
    advance_sample_set = model_mesh_field.astype(jnp.bfloat16)
    flattened_realizations = advance_sample_set.reshape(
        local_member_states,
        layer_stack,
        northward_group_count,
        member_group_count,
        band_row_count,
        column_count_north,
    )
    flattened_realizations = flattened_realizations.transpose(3, 2, 0, 1, 4, 5).reshape(
        member_group_count * northward_group_count,
        local_member_states,
        layer_stack,
        band_row_count,
        column_count_north,
    )
    received = lax.all_to_all(
        flattened_realizations, ("mem", "gy"), split_axis=0, concat_axis=0, tiled=True
    )
    received = received.reshape(
        member_group_count,
        northward_group_count,
        local_member_states,
        layer_stack,
        band_row_count,
        column_count_north,
    )
    columns = received.transpose(0, 2, 3, 4, 1, 5).reshape(
        all_members, layer_stack, band_row_count, northward_group_count * column_count_north
    )
    cells = observed_cells.reshape(observed_cells.shape[-2], observed_cells.shape[-1])
    values = observed_values.reshape(observed_values.shape[-2], observed_values.shape[-1])
    errors = error_variance.reshape(error_variance.shape[-2], error_variance.shape[-1])
    analysed = analyze(columns, cells, values, errors, transform_device)
    outgoing = analysed.reshape(
        member_group_count,
        local_member_states,
        layer_stack,
        band_row_count,
        northward_group_count,
        column_count_north,
    )
    outgoing = outgoing.transpose(0, 4, 1, 2, 3, 5).reshape(
        member_group_count * northward_group_count,
        local_member_states,
        layer_stack,
        band_row_count,
        column_count_north,
    )
    returned = lax.all_to_all(outgoing, ("mem", "gy"), split_axis=0, concat_axis=0, tiled=True)
    returned = returned.reshape(
        member_group_count,
        northward_group_count,
        local_member_states,
        layer_stack,
        band_row_count,
        column_count_north,
    )
    return returned.transpose(2, 3, 1, 0, 4, 5).reshape(
        local_member_states, layer_stack, rows_x, column_count_north
    )


LANES = 128
HALO = 4
OCTET = 8
GROUP = 32
DOMAIN = 3 * HALO
EXTENT = LANES + 2 * OCTET
VMEM_GRANT = 24 << 20
LARGEST = 6.0
WIDENING = 11.06 / LARGEST
PRIOR_COPIES = 4
STAGE_FACTORS = (1.0 / 4.0, 1.0 / 3.0, 1.0 / 2.0, 1.0)


def split_two(x):
    high = x.astype(jnp.bfloat16)
    return high, (x - high.astype(jnp.float32)).astype(jnp.bfloat16)


def split_three(x):
    high = x.astype(jnp.bfloat16)
    rest = x - high.astype(jnp.float32)
    middle = rest.astype(jnp.bfloat16)
    return high, middle, (rest - middle.astype(jnp.float32)).astype(jnp.bfloat16)


def tile_row(odd, j):
    return jnp.where(odd == 1, DOMAIN - 1 - j, j - HALO)


def domain_row(odd, row):
    return jnp.where(odd == 1, DOMAIN - 1 - row, row + HALO)


class Sizes:
    def __init__(self, local, layers, rows):
        self.local = local
        self.layers = layers
        self.rows = rows
        self.members = 2 * local
        self.per_member = layers * rows
        self.halo_rows = HALO * LANES
        self.wind_rows = 2 * layers * HALO
        self.side_rows = layers * 2 * HALO * OCTET
        self.corner_rows = layers * HALO * OCTET
        self.piece_rows = layers * LANES
        self.obs_rows = 2 * OCTET

    def field_at(self, layer, j):
        return (layer * DOMAIN + j) * EXTENT

    def wind_at(self, part, layer, j):
        return ((part * self.layers + layer) * DOMAIN + j) * EXTENT


def columns_first(s, odd, own_ref, sib_ref, layer, j):
    start = layer * s.rows + tile_row(odd, j)
    parts = [ref[pl.ds(start, s.local, stride=s.per_member), :] for ref in (own_ref, sib_ref)]
    return jnp.concatenate(parts, axis=0).T


def wind_scale(odd, value):
    half = 0.5 / diffusion
    sign = jnp.where(odd == 1, -half, half)
    row = lax.broadcasted_iota(jnp.int32, value.shape, 0)
    return value * jnp.where(row < value.shape[0] // 2, sign, half)


def widened(u):
    v = WIDENING * jnp.abs(u)
    series = v * (1.0 + v * (1.0 / 2.0) * (1.0 + v * (1.0 / 3.0) * (1.0 + v * (1.0 / 4.0))))
    g = jnp.where(v < 0.05, series, jnp.exp(v) - 1.0)
    return jnp.where(u < 0.0, -g, g)


def narrowed(w):
    g = jnp.abs(w)
    series = g * (1.0 - g * (1.0 / 2.0 - g * (1.0 / 3.0 - g * (1.0 / 4.0 - g * (1.0 / 5.0)))))
    u = jnp.where(g < 0.05, series, jnp.log(1.0 + g)) * (1.0 / WIDENING)
    return jnp.where(w < 0.0, -u, u)


def fetch_kernel(
    s, prior_ref, wind_ref, cells_ref, values_ref, errors_ref,
    own_ref, wind_out_ref, obs_ref, same_ref, other_ref,
    cells_vmem, values_vmem, errors_vmem, rows_ref, sems,
):
    odd = lax.rem(lax.axis_index("mem"), 2)
    copies = [
        pltpu.make_async_copy(source, target, sems.at[i])
        for i, (source, target) in enumerate(
            (
                (cells_ref, cells_vmem), (values_ref, values_vmem), (errors_ref, errors_vmem),
                (wind_ref, wind_out_ref),
            )
        )
    ]
    share = own_ref.shape[0] // PRIOR_COPIES
    for i in range(PRIOR_COPIES):
        part = pl.ds(i * share, share)
        copies.append(pltpu.make_async_copy(prior_ref.at[part], own_ref.at[part], sems.at[4 + i]))
    for copy in copies[4:] + copies[:4]:
        copy.start()
    obs_ref[...] = jnp.zeros_like(obs_ref)
    for copy in copies[:4]:
        copy.wait()
    obs_ref[0:1, :] = cells_vmem[...].astype(jnp.float32)
    obs_ref[1:2, :] = values_vmem[...]
    obs_ref[2:3, :] = errors_vmem[...]
    for block in range(2 * s.layers):
        for j in range(HALO):
            row = block * s.rows + tile_row(odd, 2 * HALO + j)
            rows_ref[pl.ds(block * HALO + j, 1), :] = wind_out_ref[pl.ds(row, 1), :]
    for i, part in enumerate(split_three(wind_scale(odd, rows_ref[...]))):
        same_ref[pl.ds(s.halo_rows + i * s.wind_rows, s.wind_rows), :] = part.astype(jnp.float32)
    for copy in copies[4:]:
        copy.wait()
    for parity, out_ref in ((odd, same_ref), (1 - odd, other_ref)):
        for j in range(HALO):
            row = tile_row(parity, 2 * HALO + j)
            parts = [own_ref[pl.ds(layer * s.rows + row, s.local, stride=s.per_member), :] for layer in range(s.layers)]
            value = jnp.concatenate(parts, axis=0).T
            out_ref[pl.ds(j * LANES, LANES), :] = widened(value) if j == HALO - 1 else value


def spread(parts, rows, targets, store):
    stacked = jnp.concatenate(parts, axis=0)
    turned = stacked.T
    source = lax.broadcasted_iota(jnp.int32, (stacked.shape[0], LANES), 0)
    for first, second in zip(targets[::2], targets[1::2], strict=True):
        chosen = [jnp.where(lax.rem(source, rows) == row, 1.0, 0.0) for row in (first, second)]
        both = dot(turned, jnp.concatenate(chosen, axis=1).astype(jnp.bfloat16), ((1,), (0,)))
        store(first, both[:, :LANES])
        store(second, both[:, LANES:])


def column_ends(x):
    turned = padded_rows(x).T
    return jnp.concatenate([turned[LANES - HALO :], turned[:HALO]], axis=0)


def packed_ends(x):
    parts = [part.astype(jnp.float32) for part in split_three(column_ends(x))]
    packed = parts[0] + pltpu.roll(parts[1], GROUP, 1) + pltpu.roll(parts[2], 2 * GROUP, 1)
    return jnp.concatenate([packed, jnp.zeros_like(packed)], axis=0).astype(jnp.bfloat16)


def unpacked_ends(x):
    packed = x.astype(jnp.float32)[: 2 * HALO]
    return packed + pltpu.roll(packed, LANES - GROUP, 1) + pltpu.roll(packed, LANES - 2 * GROUP, 1)


def pack_edges_kernel(s, own_ref, sib_ref, wind_ref, same_ref, field_ref, side_ref, corner_ref):
    odd = lax.rem(lax.axis_index("mem"), 2)
    for layer in range(s.layers):
        rows = []
        for j in range(HALO, DOMAIN):
            value = columns_first(s, odd, own_ref, sib_ref, layer, j)
            field_ref[pl.ds(s.field_at(layer, j) + OCTET, LANES), :] = value
            rows += [value[LANES - HALO :], value[:HALO]]
        count = len(rows) // 2
        high, low = split_two(jnp.concatenate(rows, axis=0))
        side_ref[pl.ds(layer * 2 * HALO * OCTET, 2 * HALO * OCTET), :] = high
        low = low.astype(jnp.float32)
        nearest = [low[i * OCTET + 2 : i * OCTET + 6] for i in range(2 * HALO)]
        at = s.side_rows + 2 * OCTET + layer * 2 * HALO * HALO
        side_ref[pl.ds(at, 2 * HALO * HALO), :] = jnp.concatenate(nearest, axis=0).astype(jnp.bfloat16)
        corner_ref[pl.ds(layer * HALO * OCTET, HALO * OCTET), :] = jnp.concatenate(rows[count:], axis=0).astype(jnp.bfloat16)
    near = [same_ref[pl.ds(s.halo_rows + i * s.wind_rows, s.wind_rows), :] for i in range(3)]
    corner_ref[pl.ds(s.corner_rows, 2 * OCTET), :] = packed_ends(near[0] + near[1] + near[2])
    side_ref[pl.ds(s.side_rows, 2 * OCTET), :] = packed_ends(wind_scale(odd, wind_ref[...]))


def spread_winds_kernel(s, wind_ref, winds_ref):
    odd = lax.rem(lax.axis_index("mem"), 2)
    scaled = wind_scale(odd, wind_ref[...])

    def store(row, value):
        at = s.wind_at(row // s.rows // s.layers, row // s.rows % s.layers, domain_row(odd, row % s.rows))
        winds_ref[pl.ds(pl.multiple_of(at, OCTET) + OCTET, LANES), :] = value

    rows = 2 * s.layers * s.rows
    spread(split_three(scaled), rows, list(range(rows)), store)


def set_wind_edges(winds_ref, ends, row, at):
    value = jnp.broadcast_to(ends[:, row : row + 1], (2 * HALO, LANES))
    winds_ref[pl.ds(at + HALO, HALO), :] = value[:HALO]
    winds_ref[pl.ds(at + OCTET + LANES, HALO), :] = value[HALO:]


def padded_rows(x):
    return jnp.concatenate([x, jnp.zeros((LANES - x.shape[0], LANES), x.dtype)], axis=0)


def set_field_edges(s, field_ref, layer, j, edge):
    at = s.field_at(layer, j)
    field_ref[pl.ds(at + HALO, HALO), :] = edge[:HALO]
    field_ref[pl.ds(at + OCTET + LANES, HALO), :] = edge[HALO:]


def evaluate(s, field_ref, winds_ref, from_ref, stage, start, wanted, emit):
    factor, share = STAGE_FACTORS[stage] * diffusion, coupling / s.layers / diffusion
    own_share = 4.0 + coupling / diffusion - share
    centre = {}
    for j in range(wanted[0] - 1, wanted[1] + 1):
        for layer in range(s.layers):
            centre[layer, j] = from_ref[pl.ds(s.field_at(layer, j) + start, OCTET), :]
    for j in range(*wanted):
        for layer in range(s.layers):
            at = s.field_at(layer, j) + start
            others = sum(centre[k, j] for k in range(s.layers) if k != layer)
            north, south = centre[layer, j + 1], centre[layer, j - 1]
            east, west = from_ref[pl.ds(at + 1, OCTET), :], from_ref[pl.ds(at - 1, OCTET), :]
            along = winds_ref[pl.ds(s.wind_at(0, layer, j) + start, OCTET), :]
            across = winds_ref[pl.ds(s.wind_at(1, layer, j) + start, OCTET), :]
            total = along * (south - north) + across * (west - east)
            total = total + ((north + south) + (east + west))
            total = total + ((others if share == 1.0 else share * others) - own_share * centre[layer, j])
            emit(layer, j, field_ref[pl.ds(at, OCTET), :] + factor * total)


def run_stage(s, field_ref, winds_ref, from_ref, to_ref, stage, wanted):
    def step(i, carry):
        for k in range(2):
            start = 2 * OCTET * i + OCTET * k

            def emit(layer, j, value):
                to_ref[pl.ds(s.field_at(layer, j) + start, OCTET), :] = value

            evaluate(s, field_ref, winds_ref, from_ref, stage, start, wanted, emit)
        return carry

    lax.fori_loop(0, EXTENT // (2 * OCTET), step, 0)


def inner_kernel(s, field_ref, winds_ref, first_ref, second_ref):
    refs = (field_ref, first_ref, second_ref, first_ref)
    for stage in range(3):
        wanted = (HALO + 1 + stage, DOMAIN - 1 - stage)
        run_stage(s, field_ref, winds_ref, refs[stage], refs[stage + 1], stage, wanted)


def run_ends_stage(s, field_ref, winds_ref, from_ref, to_ref, stage, wanted):
    def step(i, carry):
        for k in range(2):
            start = LANES * i + OCTET * k

            def emit(layer, j, value):
                to_ref[pl.ds(s.field_at(layer, j) + start, OCTET), :] = value

            evaluate(s, field_ref, winds_ref, from_ref, stage, start, wanted, emit)
        return carry

    lax.fori_loop(0, 2, step, 0)


def ends_kernel(s, _, __, ___, ____, side_ref, field_ref, winds_ref, first_ref, second_ref, ends1_ref, ends2_ref):
    odd = lax.rem(lax.axis_index("mem"), 2)
    for layer in range(s.layers):
        edges = side_ref[pl.ds(layer * 2 * HALO * OCTET, 2 * HALO * OCTET), :].astype(jnp.float32)
        at = s.side_rows + 2 * OCTET + layer * 2 * HALO * HALO
        low = side_ref[pl.ds(at, 2 * HALO * HALO), :].astype(jnp.float32)
        for j in range(HALO, DOMAIN):
            i = j - HALO
            edge = edges[i * OCTET : (i + 1) * OCTET]
            nearest = edge[2:6] + low[i * HALO : (i + 1) * HALO]
            set_field_edges(s, field_ref, layer, j, jnp.concatenate([edge[:2], nearest, edge[6:]], axis=0))
    beside = unpacked_ends(side_ref[pl.ds(s.side_rows, 2 * OCTET), :])
    for block in range(2 * s.layers):
        for row in range(s.rows):
            at = s.wind_at(block // s.layers, block % s.layers, domain_row(odd, row))
            set_wind_edges(winds_ref, beside, block * s.rows + row, pl.multiple_of(at, OCTET))
    refs = (field_ref, ends1_ref, ends2_ref, ends1_ref)
    for stage in range(3):
        wanted = (HALO + 1 + stage, DOMAIN - 1 - stage)
        run_ends_stage(s, field_ref, winds_ref, refs[stage], refs[stage + 1], stage, wanted)
    near = lax.broadcasted_iota(jnp.int32, (OCTET, LANES), 0) < HALO
    for to_ref, from_ref, wanted in (
        (first_ref, ends1_ref, (HALO + 1, HALO + 5)),
        (second_ref, ends2_ref, (HALO + 2, HALO + 4)),
    ):
        for layer in range(s.layers):
            for j in range(*wanted):
                at = s.field_at(layer, j)
                for start, choose in ((0, None), (OCTET, near), (LANES, ~near), (LANES + OCTET, None)):
                    part = pl.ds(at + start, OCTET)
                    value = from_ref[part, :]
                    to_ref[part, :] = value if choose is None else jnp.where(choose, value, to_ref[part, :])


def forecast_kernel(
    s, _, __, ___, ____, same_ref, other_ref, corner_ref, obs_ref,
    out0_ref, out1_ref, out2_ref, out3_ref, field_ref, winds_ref, first_ref, second_ref,
):
    mem = lax.axis_index("mem")
    odd = lax.rem(mem, 2)
    place = (mem // 2) * 2 + lax.axis_index("gy")

    lower = lax.broadcasted_iota(jnp.int32, (LANES, LANES), 1) < s.local
    for j in range(HALO):
        both = []
        for ref in (same_ref, other_ref):
            value = ref[pl.ds(j * LANES, LANES), :]
            both.append(narrowed(value) if j == HALO - 1 else value)
        same, other = both
        layer_fields = (
            jnp.where(lower, same, pltpu.roll(other, s.local, 1)),
            jnp.where(lower, pltpu.roll(same, s.local, 1), other),
        )
        for layer, value in enumerate(layer_fields):
            field_ref[pl.ds(s.field_at(layer, j) + OCTET, LANES), :] = value
    for layer in range(s.layers):
        corner = corner_ref[pl.ds(layer * HALO * OCTET, HALO * OCTET), :].astype(jnp.float32)
        for j in range(HALO):
            set_field_edges(s, field_ref, layer, j, corner[j * OCTET : (j + 1) * OCTET])
    beyond = unpacked_ends(corner_ref[pl.ds(s.corner_rows, 2 * OCTET), :])
    targets = [block * HALO + j for block in range(2 * s.layers) for j in range(1, HALO)]

    def wind_at(row):
        return s.wind_at(row // HALO // s.layers, row // HALO % s.layers, row % HALO)

    for row in targets:
        set_wind_edges(winds_ref, beyond, row, wind_at(row))

    def store(row, value):
        winds_ref[pl.ds(wind_at(row) + OCTET, LANES), :] = value

    near = [same_ref[pl.ds(s.halo_rows + i * s.wind_rows, s.wind_rows), :].astype(jnp.bfloat16) for i in range(3)]
    spread(near, s.wind_rows, targets, store)

    refs = (field_ref, first_ref, second_ref, first_ref)
    for stage in range(3):
        wanted = (1 + stage, HALO + 1 + stage)
        run_stage(s, field_ref, winds_ref, refs[stage], refs[stage + 1], stage, wanted)

    for i, part in enumerate(split_three(obs_ref[...])):
        out1_ref[pl.ds(s.piece_rows + i * s.obs_rows, s.obs_rows), :] = part
    swap_one = jnp.bitwise_xor(jnp.bitwise_and(place, 1), odd) == 1
    swap_two = jnp.bitwise_xor(place // 2, odd) == 1
    outs = (out0_ref, out1_ref, out2_ref, out3_ref)

    def last_step(i, carry):
        results = [{}, {}]
        for k in range(2):
            start = OCTET + 2 * OCTET * i + OCTET * k
            emit = lambda layer, j, value: results[k].update({(layer, j): value})
            evaluate(s, field_ref, winds_ref, first_ref, 3, start, (HALO, 2 * HALO), emit)
        at = pl.multiple_of(2 * OCTET * i, 2 * OCTET)
        for layer in range(s.layers):
            rows = [
                jnp.concatenate([result[layer, HALO + t] for result in results], axis=0).astype(jnp.bfloat16)
                for t in range(HALO)
            ]
            rows = [jnp.where(swap_one, rows[t ^ 1], rows[t]) for t in range(HALO)]
            rows = [jnp.where(swap_two, rows[t ^ 2], rows[t]) for t in range(HALO)]
            for d, out_ref in enumerate(outs):
                out_ref[pl.ds(layer * LANES + at, 2 * OCTET), :] = rows[d]
        return carry

    lax.fori_loop(0, LANES // (2 * OCTET), last_step, 0)


def dot(a, b, contract):
    return lax.dot_general(a, b, (contract, ((), ())), preferred_element_type=jnp.float32)


def beside(*parts):
    return jnp.concatenate(parts, axis=1)


def below(*parts):
    return jnp.concatenate(parts, axis=0)


def dot_split(a, b):
    (a_high, a_low), (b_high, b_low) = split_two(a), split_two(b)
    row = beside(b_high, b_low)
    both = dot(beside(a_high, a_low), below(row, row), ((1,), (0,)))
    return both[:, : b.shape[1]] + both[:, b.shape[1] :]


def root_parts(product, vector, total_members):
    count = product.shape[0]
    size = (count, count)
    diagonal = lax.broadcasted_iota(jnp.int32, size, 0) == lax.broadcasted_iota(jnp.int32, size, 1)

    def total(x):
        return jnp.sum(jnp.sum(x, axis=0, keepdims=True), axis=1, keepdims=True)

    def plus(x, scalar):
        return jnp.where(diagonal, x + scalar, x)

    def twice(matrix, column):
        once = jnp.sum(matrix * column, axis=0, keepdims=True)
        return jnp.sum(matrix * once, axis=1, keepdims=True)

    least = total_members - 1.0
    trace = total(jnp.where(diagonal, product, 0.0))
    square = total(product * product) + (2.0 * least) * trace + least * least * total_members
    inverse = lax.rsqrt(square)
    b = product * inverse
    x = least * inverse
    z = jnp.ones_like(x)
    m = 1.5 - 0.5 * x
    middle = plus(-0.5 * b, m)
    y = plus((0.25 * x - m) * b + 0.25 * dot_split(b, b), -x * m)
    near = plus(m * m * b + dot_split(y, b), m * m * x)
    slope = plus(y, m * m)
    x, z = x * m * m, m
    root = middle
    vector = twice(middle, vector)
    root_slope = jnp.where(diagonal, -0.5, 0.0)
    for step in range(1, ROOT_STEPS):
        m = 1.5 - 0.5 * x
        middle = plus(-0.5 * near, 1.5)
        root_slope = m * root_slope - 0.5 * dot_split(slope, root)
        vector = twice(middle, vector)
        z = m * z
        if step < ROOT_STEPS - 1:
            root = dot_split(middle, root)
            rest = plus(near, -x)
            y = dot_split(near, plus(0.25 * rest, -m))
            slope = m * m * slope + dot_split(y, slope)
            near = m * m * near + dot_split(y, rest)
            x = x * m * m
    return inverse, z, root_slope, vector


def analysis_kernel(
    s, total_members, piece0_ref, piece1_ref, piece2_ref, piece3_ref, obs_ref,
    send_ref, perturbation_ref, weights_ref, mean_ref,
):
    mem, side = lax.axis_index("mem"), lax.axis_index("gy")
    pieces = (piece0_ref, piece1_ref, piece2_ref, piece3_ref)
    width = 2 * LANES
    cells_total = s.layers * width
    inverse_count = 1.0 / total_members
    members = beside(
        *(
            below(*(pieces[2 * dx + dy][layer * LANES : (layer + 1) * LANES] for layer in range(s.layers) for dy in range(2)))
            for dx in range(2)
        )
    )
    mean_row = dot(jnp.ones((OCTET, total_members), jnp.bfloat16), members, ((1,), (1,))) * inverse_count
    mean = dot(members, jnp.ones((total_members, LANES), jnp.bfloat16), ((1,), (0,))) * inverse_count
    perturbation = beside(
        *(
            (members[:, i : i + LANES].astype(jnp.float32) - mean).astype(jnp.bfloat16)
            for i in range(0, total_members, LANES)
        )
    )
    perturbation_ref[...] = perturbation
    mean_ref[...] = mean_row

    count = obs_ref.shape[1]
    far = [piece1_ref[pl.ds(s.piece_rows + i * s.obs_rows, s.obs_rows), :].astype(jnp.float32) for i in range(3)]
    mine = lax.rem(mem, 2) == side
    obs = padded_rows(jnp.where(mine, obs_ref[...], far[0] + far[1] + far[2])).T
    cells = obs[:, 0:1].astype(jnp.int32)
    values, errors = obs[:, 1:2], obs[:, 2:3]
    column = jnp.bitwise_and(cells, width - 1)
    layer_of = jnp.right_shift(cells, width.bit_length() - 1)
    half = jnp.bitwise_xor(jnp.right_shift(column, LANES.bit_length() - 1), side)
    index = layer_of * width + half * LANES + jnp.bitwise_and(column, LANES - 1)
    chosen = jnp.where(lax.broadcasted_iota(jnp.int32, (count, cells_total), 1) == index, 1.0, 0.0)
    picked = dot(chosen.astype(jnp.bfloat16), members, ((1,), (0,)))
    base = jnp.sum(picked, axis=1, keepdims=True) * inverse_count
    offset = column.astype(jnp.float32) - 0.5 * (width - 1)
    weight = jnp.zeros_like(values)
    for shift in (-1, 0, 1):
        distance = (shift * width + offset) / width
        weight = weight + jnp.exp(-0.5 * distance * distance) / errors
    scale = jnp.sqrt(weight)
    scaled = (picked - base) * scale
    innovation = (values - base) * scale

    high, low = split_two(scaled)
    quarters = dot(below(high, low), below(high, low), ((1,), (1,)))
    halves = quarters[:count] + quarters[count:]
    inverse, z, slope, twice = root_parts(halves[:, :count] + halves[:, count:], innovation, total_members)
    slope_high, slope_low = split_two(slope * inverse)
    both = beside(slope_high, slope_low)
    carried = dot(both, below(high, high), ((1,), (0,))) + dot(both, below(low, low), ((1,), (0,)))
    carried_high, carried_low = split_two(carried)
    turned = below(high, low)
    spread_part = dot(turned, below(carried_high, carried_high), ((0,), (0,)))
    spread_part = spread_part + dot(turned, below(carried_low, carried_low), ((0,), (0,)))
    mean_weights = jnp.sum(scaled * twice, axis=0, keepdims=True) * inverse
    size = (total_members, total_members)
    diagonal = lax.broadcasted_iota(jnp.int32, size, 0) == lax.broadcasted_iota(jnp.int32, size, 1)
    full = jnp.where(diagonal, spread_part + z, spread_part)
    weights = (full * jnp.sqrt((total_members - 1.0) * inverse) + mean_weights).astype(jnp.bfloat16)
    weights_ref[...] = weights
    for dx in range(2):
        block = answer_rows(s, weights, perturbation, mean_row, dx, 1)
        for dy in range(2):
            for layer in range(s.layers):
                at = (layer * 2 + dy) * LANES
                send_ref[2 * dx + dy, layer] = block[:, at : at + LANES]


def answer_rows(s, weights, perturbation, mean_row, dx, part):
    first = (2 * dx + part) * s.local
    block = dot(weights[first : first + s.local], perturbation, ((1,), (1,))) + mean_row[0:1]
    return block.astype(jnp.bfloat16)


def answer_kernel(s, perturbation_ref, weights_ref, mean_ref, *outs):
    for dx in range(2):
        block = answer_rows(s, weights_ref[...], perturbation_ref[...], mean_ref[...], dx, 0)
        for dy in range(2):
            for layer in range(s.layers):
                at = (layer * 2 + dy) * LANES
                outs[2 * dx + dy][0, layer] = block[:, at : at + LANES]


def join_kernel(received_ref, *refs):
    for d in range(4):
        refs[4 + d][1] = received_ref[d]


def place_rows_kernel(s, *refs):
    pieces, out_ref, rows_ref, packed_ref, sems = refs[:4], refs[4], refs[5], refs[6], refs[7]
    mem = lax.axis_index("mem")
    odd = lax.rem(mem, 2)
    place = (mem // 2) * 2 + lax.axis_index("gy")
    count = 2 * OCTET
    copies = []
    for first in range(0, s.local, count):
        for d in range(4):
            for part, parity in ((0, odd), (1, 1 - odd)):
                row = 4 * parity + jnp.bitwise_xor(place, d)
                for layer in range(s.layers):
                    value = pieces[d][part, layer, first : first + count, :].astype(jnp.float32)
                    start = first * s.per_member + layer * s.rows + row
                    rows_ref[pl.ds(start, count, stride=s.per_member), :] = value
        rows = rows_ref[pl.ds(first * s.per_member, count * s.per_member), :]
        packed_ref[pl.ds(first, count)] = rows.astype(jnp.bfloat16).reshape(count, s.layers, s.rows, LANES)
        copies.append(
            pltpu.make_async_copy(
                packed_ref.at[pl.ds(first, count)], out_ref.at[pl.ds(first, count)], sems.at[first // count]
            )
        )
        copies[-1].start()
    for copy in copies:
        copy.wait()


def vmem_call(kernel, outs, scratch, *args, aliases=None):
    spec = pl.BlockSpec(memory_space=pltpu.VMEM)
    return pl.pallas_call(
        kernel,
        out_shape=outs,
        in_specs=[spec] * len(args),
        out_specs=jax.tree.map(lambda _: spec, outs),
        scratch_shapes=[pltpu.VMEM(shape, dtype) for shape, dtype in scratch],
        input_output_aliases=aliases or {},
        compiler_params=pltpu.CompilerParams(vmem_limit_bytes=VMEM_GRANT),
    )(*args)


def on_device_tile(prior_sample_set, flow_speeds, observed_cells, observed_values, error_variance):
    local, layers, rows, columns = prior_sample_set.shape
    s = Sizes(local, layers, rows)
    n_gx = lax.axis_size("gx")
    f32, bf16 = jnp.float32, jnp.bfloat16
    shaped = jax.ShapeDtypeStruct

    pair = [(m, m ^ 1) for m in range(4)]

    def step(m):
        return 1 if m % 2 == 0 else n_gx - 1

    along = [(m * n_gx + z, m * n_gx + (z + step(m)) % n_gx) for m in range(4) for z in range(n_gx)]
    along_other = [
        (m * n_gx + z, (m ^ 1) * n_gx + (z + step(m ^ 1)) % n_gx) for m in range(4) for z in range(n_gx)
    ]
    across = [(0, 1), (1, 0)]
    diagonal = [
        ((m * n_gx + z) * 2 + y, (m * n_gx + (z + step(m)) % n_gx) * 2 + 1 - y)
        for m in range(4) for z in range(n_gx) for y in range(2)
    ]

    sib = lax.ppermute(prior_sample_set, "mem", pair).reshape(local * layers * rows, columns)
    count = observed_cells.shape[-1]
    vmem, hbm = pl.BlockSpec(memory_space=pltpu.VMEM), pl.BlockSpec(memory_space=pltpu.HBM)
    own, wind, obs, same_out, other_out = pl.pallas_call(
        functools.partial(fetch_kernel, s),
        out_shape=(
            shaped((local * layers * rows, columns), f32),
            shaped((2 * layers * rows, columns), f32),
            shaped((2 * OCTET, count), f32),
            shaped((s.halo_rows + 3 * s.wind_rows, LANES), f32),
            shaped((s.halo_rows, LANES), f32),
        ),
        in_specs=[hbm] * 5,
        out_specs=(vmem, vmem, vmem, vmem, vmem),
        scratch_shapes=[
            pltpu.VMEM((1, count), jnp.int32),
            pltpu.VMEM((1, count), f32),
            pltpu.VMEM((1, count), f32),
            pltpu.VMEM((s.wind_rows, LANES), f32),
            pltpu.SemaphoreType.DMA((4 + PRIOR_COPIES,)),
        ],
        compiler_params=pltpu.CompilerParams(vmem_limit_bytes=VMEM_GRANT),
    )(
        *(
            pltpu.with_memory_space_constraint(x, pltpu.HBM)
            for x in (
                prior_sample_set.reshape(local * layers * rows, columns),
                flow_speeds.reshape(2 * layers * rows, columns),
                observed_cells.reshape(1, count),
                observed_values.reshape(1, count),
                error_variance.reshape(1, count),
            )
        )
    )
    obs_sib = lax.ppermute(obs, "mem", pair)

    field_shape = shaped((layers * DOMAIN * EXTENT, LANES), f32)
    winds_shape = shaped((2 * layers * DOMAIN * EXTENT, LANES), f32)
    same = lax.ppermute(same_out.astype(jnp.float16), ("mem", "gx"), along).astype(f32)
    other = lax.ppermute(other_out.astype(jnp.float16), ("mem", "gx"), along_other).astype(f32)
    field, side_out, corner_out = vmem_call(
        functools.partial(pack_edges_kernel, s),
        (
            field_shape,
            shaped((s.side_rows + 2 * OCTET + layers * 2 * HALO * HALO, LANES), bf16),
            shaped((s.corner_rows + 2 * OCTET, LANES), bf16),
        ),
        [],
        own, sib, wind, same_out,
    )
    winds = vmem_call(functools.partial(spread_winds_kernel, s), winds_shape, [], wind)
    side = lax.ppermute(side_out, "gy", across)
    corner = lax.ppermute(corner_out, ("mem", "gx", "gy"), diagonal)
    first, second = vmem_call(functools.partial(inner_kernel, s), (field_shape, field_shape), [], field, winds)
    field, winds, first, second = vmem_call(
        functools.partial(ends_kernel, s),
        (field_shape, winds_shape, field_shape, field_shape),
        [((layers * DOMAIN * EXTENT, LANES), f32)] * 2,
        field, winds, first, second, side,
        aliases={0: 0, 1: 1, 2: 2, 3: 3},
    )
    piece = shaped((s.piece_rows, s.members), bf16)
    piece_obs = shaped((s.piece_rows + 3 * s.obs_rows, s.members), bf16)
    *pieces, _, _, _, _ = vmem_call(
        functools.partial(forecast_kernel, s),
        (piece, piece_obs, piece, piece, field_shape, winds_shape, field_shape, field_shape),
        [],
        field, winds, first, second, same, other, corner, obs_sib,
        aliases={0: 4, 1: 5, 2: 6, 3: 7},
    )

    def flip(d):
        dx, dy = d // 2, d % 2
        return [((m * 2 + y), ((m ^ (2 * dx)) * 2 + (y ^ dy))) for m in range(4) for y in range(2)]

    def exchange(parts):
        arrived = [parts[0]]
        for d in range(1, 4):
            arrived.append(lax.ppermute(parts[d], ("mem", "gy"), flip(d)))
        return arrived

    total = 4 * local
    send, perturbation, weights, mean = vmem_call(
        functools.partial(analysis_kernel, s, total),
        (
            shaped((4, layers, local, LANES), bf16),
            shaped((layers * 2 * LANES, total), bf16),
            shaped((total, total), bf16),
            shaped((OCTET, layers * 2 * LANES), f32),
        ),
        [],
        *exchange(pieces), obs,
    )
    received = lax.ppermute(send, "mem", pair)
    answer = shaped((2, layers, local, LANES), bf16)
    answers = vmem_call(
        functools.partial(answer_kernel, s), (answer, answer, answer, answer), [], perturbation, weights, mean
    )
    answers = vmem_call(
        join_kernel, (answer, answer, answer, answer), [], received, *answers, aliases={1 + d: d for d in range(4)}
    )
    return pl.pallas_call(
        functools.partial(place_rows_kernel, s),
        out_shape=shaped((local, layers, rows, columns), bf16),
        in_specs=[vmem] * 4,
        out_specs=hbm,
        scratch_shapes=[
            pltpu.VMEM((local * layers * rows, LANES), f32),
            pltpu.VMEM((local, layers, rows, columns), bf16),
            pltpu.SemaphoreType.DMA((local // (2 * OCTET),)),
        ],
        compiler_params=pltpu.CompilerParams(vmem_limit_bytes=VMEM_GRANT),
    )(*exchange(answers))


def on_device(prior_sample_set, flow_speeds, observed_cells, observed_values, error_variance):
    local, _, rows, columns = prior_sample_set.shape
    suits = (
        lax.axis_size("mem") == 4
        and lax.axis_size("gy") == 2
        and rows == 2 * HALO
        and columns == LANES
        and observed_cells.shape[-2] == 1
        and 2 * local == LANES
        and observed_cells.shape[-1] == LANES
    )
    form = on_device_tile if suits else on_device_general
    return form(prior_sample_set, flow_speeds, observed_cells, observed_values, error_variance)


def solution(mesh):
    in_specs = (
        P("mem", None, "gx", "gy"),
        P(None, None, "gx", "gy"),
        P("gx", "gy", "mem", None, None),
        P("gx", "gy", "mem", None, None),
        P("gx", "gy", "mem", None, None),
    )
    out_specs = P("mem", None, "gx", "gy")
    return jax.shard_map(
        on_device, mesh=mesh, in_specs=in_specs, out_specs=out_specs, check_vma=False
    )
```

```python
import functools

import jax
import jax.numpy as jnp
from jax import lax
from jax.experimental import pallas as pl
from jax.experimental.pallas import tpu as pltpu
from jax.sharding import PartitionSpec as P


ROOT_STEPS = 4


diffusion = 0.1
coupling = 0.2


def with_halo(block, sides, width):
    for axis, dim in sides:
        count = lax.axis_size(axis)
        forward = [(i, i + 1) for i in range(count - 1)]
        forward.append((count - 1, 0))
        backward = [(target, source) for source, target in forward]
        low = lax.ppermute(
            lax.slice_in_dim(block, block.shape[dim] - width, None, axis=dim), axis, forward
        )
        high = lax.ppermute(lax.slice_in_dim(block, 0, width, axis=dim), axis, backward)
        block = jnp.concatenate([low, block, high], axis=dim)
    return block


def tendency(model_mesh_field, wind_x, wind_y):
    centre = model_mesh_field[:, :, 1:-1, 1:-1]
    north = model_mesh_field[:, :, 2:, 1:-1]
    south = model_mesh_field[:, :, :-2, 1:-1]
    east = model_mesh_field[:, :, 1:-1, 2:]
    west = model_mesh_field[:, :, 1:-1, :-2]
    layer_mean = jnp.mean(centre, axis=1, keepdims=True)
    return (
        -0.5 * wind_x * (north - south)
        - 0.5 * wind_y * (east - west)
        + diffusion * (north + south + east + west - 4.0 * centre)
        + coupling * (layer_mean - centre)
    )


def crop_margin(array, width):
    return array[:, :, width : array.shape[2] - width, width : array.shape[3] - width]


def deep_step(model_mesh_field, wind_pad):
    padded = with_halo(model_mesh_field, (("gx", 2), ("gy", 3)), 4)
    wind_three = crop_margin(wind_pad, 1)
    wind_two = crop_margin(wind_pad, 2)
    wind_one = crop_margin(wind_pad, 3)
    wind_zero = crop_margin(wind_pad, 4)
    section_one = tendency(padded, wind_three[0], wind_three[1])
    section_two = tendency(crop_margin(padded, 1) + 0.5 * section_one, wind_two[0], wind_two[1])
    section_three = tendency(crop_margin(padded, 2) + 0.5 * section_two, wind_one[0], wind_one[1])
    section_four = tendency(crop_margin(padded, 3) + section_three, wind_zero[0], wind_zero[1])
    return (
        crop_margin(padded, 4)
        + (
            crop_margin(section_one, 3)
            + 2.0 * crop_margin(section_two, 2)
            + 2.0 * crop_margin(section_three, 1)
            + section_four
        )
        / 6.0
    )


def transform_device(weights, rolled):
    return jnp.einsum("qik,ilsqc->klsqc", weights, rolled, preferred_element_type=jnp.float32)


def analyze(strip_block, cells, values, errors, transform):
    realization_vectors, layer_stack, rows, width = strip_block.shape
    patches, count = cells.shape
    patch = width // patches
    highest = lax.Precision.HIGHEST
    mean_field = jnp.mean(strip_block, axis=0, dtype=jnp.float32)
    layer_of = cells // (rows * patch)
    row_of = cells // patch % rows
    column = cells % patch
    starts = (jnp.arange(patches, dtype=jnp.int32) * patch)[:, None]
    flat_index = layer_of * (rows * width) + row_of * width + starts + column
    picked = jnp.take(
        strip_block.reshape(realization_vectors, layer_stack * rows * width),
        flat_index.reshape(-1),
        axis=1,
    )
    base = jnp.take(mean_field.reshape(-1), flat_index.reshape(-1)).reshape(patches, count)
    spread = picked.astype(jnp.float32).reshape(realization_vectors, patches, count) - base[None]
    innovation = values - base
    offset = column.astype(jnp.float32) - 0.5 * (patch - 1)
    spread_parts = []
    innovation_parts = []
    for shift in (-1, 0, 1):
        distance = (shift * patch + jnp.roll(offset, -shift, axis=0)) / patch
        scale = jnp.sqrt(jnp.exp(-0.5 * distance * distance) / jnp.roll(errors, -shift, axis=0))
        spread_parts.append(jnp.roll(spread, -shift, axis=1) * scale[None])
        innovation_parts.append(jnp.roll(innovation, -shift, axis=0) * scale)
    scaled = jnp.concatenate(spread_parts, axis=2)
    scaled_innovation = jnp.concatenate(innovation_parts, axis=1)
    identity = jnp.eye(realization_vectors, dtype=jnp.float32)
    gram = (
        jnp.einsum("kpj,ipj->pki", scaled, scaled, precision=highest)
        + (realization_vectors - 1.0) * identity
    )
    frob = jnp.sqrt(jnp.sum(gram * gram, axis=(1, 2)))
    current = gram / frob[:, None, None]
    root = jnp.broadcast_to(identity, gram.shape)
    for _ in range(ROOT_STEPS):
        middle = 1.5 * identity - 0.5 * jnp.einsum("pab,pbc->pac", root, current, precision=highest)
        current = jnp.einsum("pab,pbc->pac", current, middle, precision=highest)
        root = jnp.einsum("pab,pbc->pac", middle, root, precision=highest)
    projected = jnp.einsum("kpj,pj->pk", scaled, scaled_innovation, precision=highest)
    once = jnp.einsum("pab,pb->pa", root, projected, precision=highest)
    twice = jnp.einsum("pab,pb->pa", root, once, precision=highest)
    mean_weights = twice / frob[:, None]
    weights = (
        jnp.sqrt(realization_vectors - 1.0) * root / jnp.sqrt(frob)[:, None, None]
        + mean_weights[:, :, None]
    ).astype(jnp.bfloat16)
    perturbation = (strip_block - mean_field[None]).astype(jnp.bfloat16)
    rolled = jnp.roll(perturbation, -(patch // 2), axis=3).reshape(
        realization_vectors, layer_stack, rows, patches, patch
    )
    first = transform(weights, rolled)
    second = transform(jnp.roll(weights, -1, axis=0), rolled)
    position = (jnp.arange(patch, dtype=jnp.float32) + 0.5) / patch
    increment = ((1.0 - position) * first + position * second).reshape(
        realization_vectors, layer_stack, rows, width
    )
    return (jnp.roll(increment, patch // 2, axis=3) + mean_field[None]).astype(jnp.bfloat16)


def on_device_general(prior_sample_set, flow_speeds, observed_cells, observed_values, error_variance):
    member_group_count = lax.axis_size("mem")
    northward_group_count = lax.axis_size("gy")
    local_member_states, layer_stack, rows_x, column_count_north = prior_sample_set.shape
    band_row_count = rows_x // (member_group_count * northward_group_count)
    all_members = local_member_states * member_group_count
    model_mesh_field = prior_sample_set
    wind_pad = with_halo(flow_speeds, (("gx", 2), ("gy", 3)), 4)
    model_mesh_field = deep_step(model_mesh_field, wind_pad)
    advance_sample_set = model_mesh_field.astype(jnp.bfloat16)
    flattened_realizations = advance_sample_set.reshape(
        local_member_states,
        layer_stack,
        northward_group_count,
        member_group_count,
        band_row_count,
        column_count_north,
    )
    flattened_realizations = flattened_realizations.transpose(3, 2, 0, 1, 4, 5).reshape(
        member_group_count * northward_group_count,
        local_member_states,
        layer_stack,
        band_row_count,
        column_count_north,
    )
    received = lax.all_to_all(
        flattened_realizations, ("mem", "gy"), split_axis=0, concat_axis=0, tiled=True
    )
    received = received.reshape(
        member_group_count,
        northward_group_count,
        local_member_states,
        layer_stack,
        band_row_count,
        column_count_north,
    )
    columns = received.transpose(0, 2, 3, 4, 1, 5).reshape(
        all_members, layer_stack, band_row_count, northward_group_count * column_count_north
    )
    cells = observed_cells.reshape(observed_cells.shape[-2], observed_cells.shape[-1])
    values = observed_values.reshape(observed_values.shape[-2], observed_values.shape[-1])
    errors = error_variance.reshape(error_variance.shape[-2], error_variance.shape[-1])
    analysed = analyze(columns, cells, values, errors, transform_device)
    outgoing = analysed.reshape(
        member_group_count,
        local_member_states,
        layer_stack,
        band_row_count,
        northward_group_count,
        column_count_north,
    )
    outgoing = outgoing.transpose(0, 4, 1, 2, 3, 5).reshape(
        member_group_count * northward_group_count,
        local_member_states,
        layer_stack,
        band_row_count,
        column_count_north,
    )
    returned = lax.all_to_all(outgoing, ("mem", "gy"), split_axis=0, concat_axis=0, tiled=True)
    returned = returned.reshape(
        member_group_count,
        northward_group_count,
        local_member_states,
        layer_stack,
        band_row_count,
        column_count_north,
    )
    return returned.transpose(2, 3, 1, 0, 4, 5).reshape(
        local_member_states, layer_stack, rows_x, column_count_north
    )


LANES = 128
HALO = 4
OCTET = 8
GROUP = 32
DOMAIN = 3 * HALO
TOGETHER = 6
EXTENT = LANES + 2 * OCTET
VMEM_GRANT = 24 << 20
LARGEST = 6.0
WIDENING = 11.06 / LARGEST
PRIOR_COPIES = 4
STAGE_FACTORS = (1.0 / 4.0, 1.0 / 3.0, 1.0 / 2.0, 1.0)


def split_two(x):
    high = x.astype(jnp.bfloat16)
    return high, (x - high.astype(jnp.float32)).astype(jnp.bfloat16)


def split_three(x):
    high = x.astype(jnp.bfloat16)
    rest = x - high.astype(jnp.float32)
    middle = rest.astype(jnp.bfloat16)
    return high, middle, (rest - middle.astype(jnp.float32)).astype(jnp.bfloat16)


def tile_row(odd, j):
    return jnp.where(odd == 1, DOMAIN - 1 - j, j - HALO)


def domain_row(odd, row):
    return jnp.where(odd == 1, DOMAIN - 1 - row, row + HALO)


class Sizes:
    def __init__(self, local, layers, rows):
        self.local = local
        self.layers = layers
        self.rows = rows
        self.members = 2 * local
        self.per_member = layers * rows
        self.halo_rows = HALO * LANES
        self.wind_rows = 2 * layers * HALO
        self.side_rows = layers * 2 * HALO * OCTET
        self.corner_rows = layers * HALO * OCTET
        self.piece_rows = layers * LANES
        self.obs_rows = 2 * OCTET

    def field_at(self, layer, j):
        return (layer * DOMAIN + j) * EXTENT

    def wind_at(self, part, layer, j):
        return ((part * self.layers + layer) * DOMAIN + j) * EXTENT


def columns_first(s, odd, own_ref, sib_ref, layer, j):
    start = layer * s.rows + tile_row(odd, j)
    parts = [ref[pl.ds(start, s.local, stride=s.per_member), :] for ref in (own_ref, sib_ref)]
    return jnp.concatenate(parts, axis=0).T


def wind_scale(odd, value):
    half = 0.5 / diffusion
    sign = jnp.where(odd == 1, -half, half)
    row = lax.broadcasted_iota(jnp.int32, value.shape, 0)
    return value * jnp.where(row < value.shape[0] // 2, sign, half)


def widened(u):
    v = WIDENING * jnp.abs(u)
    series = v * (1.0 + v * (1.0 / 2.0) * (1.0 + v * (1.0 / 3.0) * (1.0 + v * (1.0 / 4.0))))
    g = jnp.where(v < 0.05, series, jnp.exp(v) - 1.0)
    return jnp.where(u < 0.0, -g, g)


def narrowed(w):
    g = jnp.abs(w)
    series = g * (1.0 - g * (1.0 / 2.0 - g * (1.0 / 3.0 - g * (1.0 / 4.0 - g * (1.0 / 5.0)))))
    u = jnp.where(g < 0.05, series, jnp.log(1.0 + g)) * (1.0 / WIDENING)
    return jnp.where(w < 0.0, -u, u)


def fetch_kernel(
    s, prior_ref, wind_ref, cells_ref, values_ref, errors_ref,
    own_ref, wind_out_ref, obs_ref, same_ref, other_ref,
    cells_vmem, values_vmem, errors_vmem, rows_ref, sems,
):
    odd = lax.rem(lax.axis_index("mem"), 2)
    copies = [
        pltpu.make_async_copy(source, target, sems.at[i])
        for i, (source, target) in enumerate(
            (
                (cells_ref, cells_vmem), (values_ref, values_vmem), (errors_ref, errors_vmem),
                (wind_ref, wind_out_ref),
            )
        )
    ]
    share = own_ref.shape[0] // PRIOR_COPIES
    for i in range(PRIOR_COPIES):
        part = pl.ds(i * share, share)
        copies.append(pltpu.make_async_copy(prior_ref.at[part], own_ref.at[part], sems.at[4 + i]))
    for copy in copies[4:] + copies[:4]:
        copy.start()
    obs_ref[...] = jnp.zeros_like(obs_ref)
    for copy in copies[:4]:
        copy.wait()
    obs_ref[0:1, :] = cells_vmem[...].astype(jnp.float32)
    obs_ref[1:2, :] = values_vmem[...]
    obs_ref[2:3, :] = errors_vmem[...]
    for block in range(2 * s.layers):
        for j in range(HALO):
            row = block * s.rows + tile_row(odd, 2 * HALO + j)
            rows_ref[pl.ds(block * HALO + j, 1), :] = wind_out_ref[pl.ds(row, 1), :]
    for i, part in enumerate(split_three(wind_scale(odd, rows_ref[...]))):
        same_ref[pl.ds(s.halo_rows + i * s.wind_rows, s.wind_rows), :] = part.astype(jnp.float32)
    for copy in copies[4:]:
        copy.wait()
    for parity, out_ref in ((odd, same_ref), (1 - odd, other_ref)):
        for j in range(HALO):
            row = tile_row(parity, 2 * HALO + j)
            parts = [own_ref[pl.ds(layer * s.rows + row, s.local, stride=s.per_member), :] for layer in range(s.layers)]
            value = jnp.concatenate(parts, axis=0).T
            out_ref[pl.ds(j * LANES, LANES), :] = widened(value) if j == HALO - 1 else value


def spread(parts, rows, targets, store):
    stacked = jnp.concatenate(parts, axis=0)
    turned = stacked.T
    source = lax.broadcasted_iota(jnp.int32, (stacked.shape[0], LANES), 0)
    for first, second in zip(targets[::2], targets[1::2], strict=True):
        chosen = [jnp.where(lax.rem(source, rows) == row, 1.0, 0.0) for row in (first, second)]
        both = dot(turned, jnp.concatenate(chosen, axis=1).astype(jnp.bfloat16), ((1,), (0,)))
        store(first, both[:, :LANES])
        store(second, both[:, LANES:])


def column_ends(x):
    turned = padded_rows(x).T
    return jnp.concatenate([turned[LANES - HALO :], turned[:HALO]], axis=0)


def packed_ends(x):
    parts = [part.astype(jnp.float32) for part in split_three(column_ends(x))]
    packed = parts[0] + pltpu.roll(parts[1], GROUP, 1) + pltpu.roll(parts[2], 2 * GROUP, 1)
    return jnp.concatenate([packed, jnp.zeros_like(packed)], axis=0).astype(jnp.bfloat16)


def unpacked_ends(x):
    packed = x.astype(jnp.float32)[: 2 * HALO]
    return packed + pltpu.roll(packed, LANES - GROUP, 1) + pltpu.roll(packed, LANES - 2 * GROUP, 1)


def pack_edges_kernel(s, own_ref, sib_ref, wind_ref, same_ref, field_ref, side_ref, corner_ref):
    odd = lax.rem(lax.axis_index("mem"), 2)
    for layer in range(s.layers):
        rows = []
        for j in range(HALO, DOMAIN):
            value = columns_first(s, odd, own_ref, sib_ref, layer, j)
            field_ref[pl.ds(s.field_at(layer, j) + OCTET, LANES), :] = value
            rows += [value[LANES - HALO :], value[:HALO]]
        count = len(rows) // 2
        high, low = split_two(jnp.concatenate(rows, axis=0))
        side_ref[pl.ds(layer * 2 * HALO * OCTET, 2 * HALO * OCTET), :] = high
        low = low.astype(jnp.float32)
        nearest = [low[i * OCTET + 2 : i * OCTET + 6] for i in range(2 * HALO)]
        at = s.side_rows + 2 * OCTET + layer * 2 * HALO * HALO
        side_ref[pl.ds(at, 2 * HALO * HALO), :] = jnp.concatenate(nearest, axis=0).astype(jnp.bfloat16)
        corner_ref[pl.ds(layer * HALO * OCTET, HALO * OCTET), :] = jnp.concatenate(rows[count:], axis=0).astype(jnp.bfloat16)
    near = [same_ref[pl.ds(s.halo_rows + i * s.wind_rows, s.wind_rows), :] for i in range(3)]
    corner_ref[pl.ds(s.corner_rows, 2 * OCTET), :] = packed_ends(near[0] + near[1] + near[2])
    side_ref[pl.ds(s.side_rows, 2 * OCTET), :] = packed_ends(wind_scale(odd, wind_ref[...]))


def spread_winds_kernel(s, wind_ref, winds_ref):
    odd = lax.rem(lax.axis_index("mem"), 2)
    scaled = wind_scale(odd, wind_ref[...])

    def store(row, value):
        at = s.wind_at(row // s.rows // s.layers, row // s.rows % s.layers, domain_row(odd, row % s.rows))
        winds_ref[pl.ds(pl.multiple_of(at, OCTET) + OCTET, LANES), :] = value

    rows = 2 * s.layers * s.rows
    spread(split_three(scaled), rows, list(range(rows)), store)


def set_wind_edges(winds_ref, ends, row, at):
    value = jnp.broadcast_to(ends[:, row : row + 1], (2 * HALO, LANES))
    winds_ref[pl.ds(at + HALO, HALO), :] = value[:HALO]
    winds_ref[pl.ds(at + OCTET + LANES, HALO), :] = value[HALO:]


def padded_rows(x):
    return jnp.concatenate([x, jnp.zeros((LANES - x.shape[0], LANES), x.dtype)], axis=0)


def set_field_edges(s, field_ref, layer, j, edge):
    at = s.field_at(layer, j)
    field_ref[pl.ds(at + HALO, HALO), :] = edge[:HALO]
    field_ref[pl.ds(at + OCTET + LANES, HALO), :] = edge[HALO:]


def evaluate(s, field_ref, winds_ref, from_ref, stage, start, wanted, emit):
    factor, share = STAGE_FACTORS[stage] * diffusion, coupling / s.layers / diffusion
    own_share = 4.0 + coupling / diffusion - share
    centre = {}
    for j in range(wanted[0] - 1, wanted[1] + 1):
        for layer in range(s.layers):
            centre[layer, j] = from_ref[pl.ds(s.field_at(layer, j) + start, OCTET), :]
    for j in range(*wanted):
        for layer in range(s.layers):
            at = s.field_at(layer, j) + start
            others = sum(centre[k, j] for k in range(s.layers) if k != layer)
            north, south = centre[layer, j + 1], centre[layer, j - 1]
            east, west = from_ref[pl.ds(at + 1, OCTET), :], from_ref[pl.ds(at - 1, OCTET), :]
            along = winds_ref[pl.ds(s.wind_at(0, layer, j) + start, OCTET), :]
            across = winds_ref[pl.ds(s.wind_at(1, layer, j) + start, OCTET), :]
            total = along * (south - north) + across * (west - east)
            total = total + ((north + south) + (east + west))
            total = total + ((others if share == 1.0 else share * others) - own_share * centre[layer, j])
            emit(layer, j, field_ref[pl.ds(at, OCTET), :] + factor * total)


def run_stage(s, field_ref, winds_ref, from_ref, to_ref, stage, wanted):
    def step(i, carry):
        for k in range(TOGETHER):
            start = TOGETHER * OCTET * i + OCTET * k

            def emit(layer, j, value):
                to_ref[pl.ds(s.field_at(layer, j) + start, OCTET), :] = value

            evaluate(s, field_ref, winds_ref, from_ref, stage, start, wanted, emit)
        return carry

    lax.fori_loop(0, EXTENT // (TOGETHER * OCTET), step, 0)


def inner_kernel(s, field_ref, winds_ref, first_ref, second_ref):
    refs = (field_ref, first_ref, second_ref, first_ref)
    for stage in range(3):
        wanted = (HALO + 1 + stage, DOMAIN - 1 - stage)
        run_stage(s, field_ref, winds_ref, refs[stage], refs[stage + 1], stage, wanted)


def run_ends_stage(s, field_ref, winds_ref, from_ref, to_ref, stage, wanted):
    def step(i, carry):
        for k in range(2):
            start = LANES * i + OCTET * k

            def emit(layer, j, value):
                to_ref[pl.ds(s.field_at(layer, j) + start, OCTET), :] = value

            evaluate(s, field_ref, winds_ref, from_ref, stage, start, wanted, emit)
        return carry

    lax.fori_loop(0, 2, step, 0)


def ends_kernel(s, _, __, ___, ____, side_ref, field_ref, winds_ref, first_ref, second_ref, ends1_ref, ends2_ref):
    odd = lax.rem(lax.axis_index("mem"), 2)
    for layer in range(s.layers):
        edges = side_ref[pl.ds(layer * 2 * HALO * OCTET, 2 * HALO * OCTET), :].astype(jnp.float32)
        at = s.side_rows + 2 * OCTET + layer * 2 * HALO * HALO
        low = side_ref[pl.ds(at, 2 * HALO * HALO), :].astype(jnp.float32)
        for j in range(HALO, DOMAIN):
            i = j - HALO
            edge = edges[i * OCTET : (i + 1) * OCTET]
            nearest = edge[2:6] + low[i * HALO : (i + 1) * HALO]
            set_field_edges(s, field_ref, layer, j, jnp.concatenate([edge[:2], nearest, edge[6:]], axis=0))
    beside = unpacked_ends(side_ref[pl.ds(s.side_rows, 2 * OCTET), :])
    for block in range(2 * s.layers):
        for row in range(s.rows):
            at = s.wind_at(block // s.layers, block % s.layers, domain_row(odd, row))
            set_wind_edges(winds_ref, beside, block * s.rows + row, pl.multiple_of(at, OCTET))
    refs = (field_ref, ends1_ref, ends2_ref, ends1_ref)
    for stage in range(3):
        wanted = (HALO + 1 + stage, DOMAIN - 1 - stage)
        run_ends_stage(s, field_ref, winds_ref, refs[stage], refs[stage + 1], stage, wanted)
    near = lax.broadcasted_iota(jnp.int32, (OCTET, LANES), 0) < HALO
    for to_ref, from_ref, wanted in (
        (first_ref, ends1_ref, (HALO + 1, HALO + 5)),
        (second_ref, ends2_ref, (HALO + 2, HALO + 4)),
    ):
        for layer in range(s.layers):
            for j in range(*wanted):
                at = s.field_at(layer, j)
                for start, choose in ((0, None), (OCTET, near), (LANES, ~near), (LANES + OCTET, None)):
                    part = pl.ds(at + start, OCTET)
                    value = from_ref[part, :]
                    to_ref[part, :] = value if choose is None else jnp.where(choose, value, to_ref[part, :])


def forecast_kernel(
    s, _, __, ___, ____, same_ref, other_ref, corner_ref, obs_ref,
    out0_ref, out1_ref, out2_ref, out3_ref, field_ref, winds_ref, first_ref, second_ref,
):
    mem = lax.axis_index("mem")
    odd = lax.rem(mem, 2)
    place = (mem // 2) * 2 + lax.axis_index("gy")

    lower = lax.broadcasted_iota(jnp.int32, (LANES, LANES), 1) < s.local
    for j in range(HALO):
        both = []
        for ref in (same_ref, other_ref):
            value = ref[pl.ds(j * LANES, LANES), :]
            both.append(narrowed(value) if j == HALO - 1 else value)
        same, other = both
        layer_fields = (
            jnp.where(lower, same, pltpu.roll(other, s.local, 1)),
            jnp.where(lower, pltpu.roll(same, s.local, 1), other),
        )
        for layer, value in enumerate(layer_fields):
            field_ref[pl.ds(s.field_at(layer, j) + OCTET, LANES), :] = value
    for layer in range(s.layers):
        corner = corner_ref[pl.ds(layer * HALO * OCTET, HALO * OCTET), :].astype(jnp.float32)
        for j in range(HALO):
            set_field_edges(s, field_ref, layer, j, corner[j * OCTET : (j + 1) * OCTET])
    beyond = unpacked_ends(corner_ref[pl.ds(s.corner_rows, 2 * OCTET), :])
    targets = [block * HALO + j for block in range(2 * s.layers) for j in range(1, HALO)]

    def wind_at(row):
        return s.wind_at(row // HALO // s.layers, row // HALO % s.layers, row % HALO)

    for row in targets:
        set_wind_edges(winds_ref, beyond, row, wind_at(row))

    def store(row, value):
        winds_ref[pl.ds(wind_at(row) + OCTET, LANES), :] = value

    near = [same_ref[pl.ds(s.halo_rows + i * s.wind_rows, s.wind_rows), :].astype(jnp.bfloat16) for i in range(3)]
    spread(near, s.wind_rows, targets, store)

    refs = (field_ref, first_ref, second_ref, first_ref)
    for stage in range(3):
        wanted = (1 + stage, HALO + 1 + stage)
        run_stage(s, field_ref, winds_ref, refs[stage], refs[stage + 1], stage, wanted)

    for i, part in enumerate(split_three(obs_ref[...])):
        out1_ref[pl.ds(s.piece_rows + i * s.obs_rows, s.obs_rows), :] = part
    swap_one = jnp.bitwise_xor(jnp.bitwise_and(place, 1), odd) == 1
    swap_two = jnp.bitwise_xor(place // 2, odd) == 1
    outs = (out0_ref, out1_ref, out2_ref, out3_ref)

    def last_step(i, carry):
        results = [{}, {}]
        for k in range(2):
            start = OCTET + 2 * OCTET * i + OCTET * k
            emit = lambda layer, j, value: results[k].update({(layer, j): value})
            evaluate(s, field_ref, winds_ref, first_ref, 3, start, (HALO, 2 * HALO), emit)
        at = pl.multiple_of(2 * OCTET * i, 2 * OCTET)
        for layer in range(s.layers):
            rows = [
                jnp.concatenate([result[layer, HALO + t] for result in results], axis=0).astype(jnp.bfloat16)
                for t in range(HALO)
            ]
            rows = [jnp.where(swap_one, rows[t ^ 1], rows[t]) for t in range(HALO)]
            rows = [jnp.where(swap_two, rows[t ^ 2], rows[t]) for t in range(HALO)]
            for d, out_ref in enumerate(outs):
                out_ref[pl.ds(layer * LANES + at, 2 * OCTET), :] = rows[d]
        return carry

    lax.fori_loop(0, LANES // (2 * OCTET), last_step, 0)


def dot(a, b, contract):
    return lax.dot_general(a, b, (contract, ((), ())), preferred_element_type=jnp.float32)


def beside(*parts):
    return jnp.concatenate(parts, axis=1)


def below(*parts):
    return jnp.concatenate(parts, axis=0)


def dot_split(a, b):
    (a_high, a_low), (b_high, b_low) = split_two(a), split_two(b)
    row = beside(b_high, b_low)
    both = dot(beside(a_high, a_low), below(row, row), ((1,), (0,)))
    return both[:, : b.shape[1]] + both[:, b.shape[1] :]


def root_parts(product, vector, total_members):
    count = product.shape[0]
    size = (count, count)
    diagonal = lax.broadcasted_iota(jnp.int32, size, 0) == lax.broadcasted_iota(jnp.int32, size, 1)

    def total(x):
        return jnp.sum(jnp.sum(x, axis=0, keepdims=True), axis=1, keepdims=True)

    def plus(x, scalar):
        return jnp.where(diagonal, x + scalar, x)

    def twice(matrix, column):
        once = jnp.sum(matrix * column, axis=0, keepdims=True)
        return jnp.sum(matrix * once, axis=1, keepdims=True)

    least = total_members - 1.0
    trace = total(jnp.where(diagonal, product, 0.0))
    square = total(product * product) + (2.0 * least) * trace + least * least * total_members
    inverse = lax.rsqrt(square)
    b = product * inverse
    x = least * inverse
    z = jnp.ones_like(x)
    m = 1.5 - 0.5 * x
    middle = plus(-0.5 * b, m)
    y = plus((0.25 * x - m) * b + 0.25 * dot_split(b, b), -x * m)
    near = plus(m * m * b + dot_split(y, b), m * m * x)
    slope = plus(y, m * m)
    x, z = x * m * m, m
    root = middle
    vector = twice(middle, vector)
    root_slope = jnp.where(diagonal, -0.5, 0.0)
    for step in range(1, ROOT_STEPS):
        m = 1.5 - 0.5 * x
        middle = plus(-0.5 * near, 1.5)
        root_slope = m * root_slope - 0.5 * dot_split(slope, root)
        vector = twice(middle, vector)
        z = m * z
        if step < ROOT_STEPS - 1:
            root = dot_split(middle, root)
            rest = plus(near, -x)
            y = dot_split(near, plus(0.25 * rest, -m))
            slope = m * m * slope + dot_split(y, slope)
            near = m * m * near + dot_split(y, rest)
            x = x * m * m
    return inverse, z, root_slope, vector


def analysis_kernel(
    s, total_members, piece0_ref, piece1_ref, piece2_ref, piece3_ref, obs_ref,
    send_ref, perturbation_ref, weights_ref, mean_ref,
):
    mem, side = lax.axis_index("mem"), lax.axis_index("gy")
    pieces = (piece0_ref, piece1_ref, piece2_ref, piece3_ref)
    width = 2 * LANES
    cells_total = s.layers * width
    inverse_count = 1.0 / total_members
    members = beside(
        *(
            below(*(pieces[2 * dx + dy][layer * LANES : (layer + 1) * LANES] for layer in range(s.layers) for dy in range(2)))
            for dx in range(2)
        )
    )
    mean_row = dot(jnp.ones((OCTET, total_members), jnp.bfloat16), members, ((1,), (1,))) * inverse_count
    mean = dot(members, jnp.ones((total_members, LANES), jnp.bfloat16), ((1,), (0,))) * inverse_count
    perturbation = beside(
        *(
            (members[:, i : i + LANES].astype(jnp.float32) - mean).astype(jnp.bfloat16)
            for i in range(0, total_members, LANES)
        )
    )
    perturbation_ref[...] = perturbation
    mean_ref[...] = mean_row

    count = obs_ref.shape[1]
    far = [piece1_ref[pl.ds(s.piece_rows + i * s.obs_rows, s.obs_rows), :].astype(jnp.float32) for i in range(3)]
    mine = lax.rem(mem, 2) == side
    obs = padded_rows(jnp.where(mine, obs_ref[...], far[0] + far[1] + far[2])).T
    cells = obs[:, 0:1].astype(jnp.int32)
    values, errors = obs[:, 1:2], obs[:, 2:3]
    column = jnp.bitwise_and(cells, width - 1)
    layer_of = jnp.right_shift(cells, width.bit_length() - 1)
    half = jnp.bitwise_xor(jnp.right_shift(column, LANES.bit_length() - 1), side)
    index = layer_of * width + half * LANES + jnp.bitwise_and(column, LANES - 1)
    chosen = jnp.where(lax.broadcasted_iota(jnp.int32, (count, cells_total), 1) == index, 1.0, 0.0)
    picked = dot(chosen.astype(jnp.bfloat16), members, ((1,), (0,)))
    base = jnp.sum(picked, axis=1, keepdims=True) * inverse_count
    offset = column.astype(jnp.float32) - 0.5 * (width - 1)
    weight = jnp.zeros_like(values)
    for shift in (-1, 0, 1):
        distance = (shift * width + offset) / width
        weight = weight + jnp.exp(-0.5 * distance * distance) / errors
    scale = jnp.sqrt(weight)
    scaled = (picked - base) * scale
    innovation = (values - base) * scale

    high, low = split_two(scaled)
    quarters = dot(below(high, low), below(high, low), ((1,), (1,)))
    halves = quarters[:count] + quarters[count:]
    inverse, z, slope, twice = root_parts(halves[:, :count] + halves[:, count:], innovation, total_members)
    slope_high, slope_low = split_two(slope * inverse)
    both = beside(slope_high, slope_low)
    carried = dot(both, below(high, high), ((1,), (0,))) + dot(both, below(low, low), ((1,), (0,)))
    carried_high, carried_low = split_two(carried)
    turned = below(high, low)
    spread_part = dot(turned, below(carried_high, carried_high), ((0,), (0,)))
    spread_part = spread_part + dot(turned, below(carried_low, carried_low), ((0,), (0,)))
    mean_weights = jnp.sum(scaled * twice, axis=0, keepdims=True) * inverse
    size = (total_members, total_members)
    diagonal = lax.broadcasted_iota(jnp.int32, size, 0) == lax.broadcasted_iota(jnp.int32, size, 1)
    full = jnp.where(diagonal, spread_part + z, spread_part)
    weights = (full * jnp.sqrt((total_members - 1.0) * inverse) + mean_weights).astype(jnp.bfloat16)
    weights_ref[...] = weights
    for dx in range(2):
        block = answer_rows(s, weights, perturbation, mean_row, dx, 1)
        for dy in range(2):
            for layer in range(s.layers):
                at = (layer * 2 + dy) * LANES
                send_ref[2 * dx + dy, layer] = block[:, at : at + LANES]


def answer_rows(s, weights, perturbation, mean_row, dx, part):
    first = (2 * dx + part) * s.local
    block = dot(weights[first : first + s.local], perturbation, ((1,), (1,))) + mean_row[0:1]
    return block.astype(jnp.bfloat16)


def answer_kernel(s, perturbation_ref, weights_ref, mean_ref, *outs):
    for dx in range(2):
        block = answer_rows(s, weights_ref[...], perturbation_ref[...], mean_ref[...], dx, 0)
        for dy in range(2):
            for layer in range(s.layers):
                at = (layer * 2 + dy) * LANES
                outs[2 * dx + dy][0, layer] = block[:, at : at + LANES]


def join_kernel(received_ref, *refs):
    for d in range(4):
        refs[4 + d][1] = received_ref[d]


def place_rows_kernel(s, *refs):
    pieces, out_ref, rows_ref, packed_ref, sems = refs[:4], refs[4], refs[5], refs[6], refs[7]
    mem = lax.axis_index("mem")
    odd = lax.rem(mem, 2)
    place = (mem // 2) * 2 + lax.axis_index("gy")
    count = 2 * OCTET
    copies = []
    for first in range(0, s.local, count):
        for d in range(4):
            for part, parity in ((0, odd), (1, 1 - odd)):
                row = 4 * parity + jnp.bitwise_xor(place, d)
                for layer in range(s.layers):
                    value = pieces[d][part, layer, first : first + count, :].astype(jnp.float32)
                    start = first * s.per_member + layer * s.rows + row
                    rows_ref[pl.ds(start, count, stride=s.per_member), :] = value
        rows = rows_ref[pl.ds(first * s.per_member, count * s.per_member), :]
        packed_ref[pl.ds(first, count)] = rows.astype(jnp.bfloat16).reshape(count, s.layers, s.rows, LANES)
        copies.append(
            pltpu.make_async_copy(
                packed_ref.at[pl.ds(first, count)], out_ref.at[pl.ds(first, count)], sems.at[first // count]
            )
        )
        copies[-1].start()
    for copy in copies:
        copy.wait()


def vmem_call(kernel, outs, scratch, *args, aliases=None):
    spec = pl.BlockSpec(memory_space=pltpu.VMEM)
    return pl.pallas_call(
        kernel,
        out_shape=outs,
        in_specs=[spec] * len(args),
        out_specs=jax.tree.map(lambda _: spec, outs),
        scratch_shapes=[pltpu.VMEM(shape, dtype) for shape, dtype in scratch],
        input_output_aliases=aliases or {},
        compiler_params=pltpu.CompilerParams(vmem_limit_bytes=VMEM_GRANT),
    )(*args)


def on_device_tile(prior_sample_set, flow_speeds, observed_cells, observed_values, error_variance):
    local, layers, rows, columns = prior_sample_set.shape
    s = Sizes(local, layers, rows)
    n_gx = lax.axis_size("gx")
    f32, bf16 = jnp.float32, jnp.bfloat16
    shaped = jax.ShapeDtypeStruct

    pair = [(m, m ^ 1) for m in range(4)]

    def step(m):
        return 1 if m % 2 == 0 else n_gx - 1

    along = [(m * n_gx + z, m * n_gx + (z + step(m)) % n_gx) for m in range(4) for z in range(n_gx)]
    along_other = [
        (m * n_gx + z, (m ^ 1) * n_gx + (z + step(m ^ 1)) % n_gx) for m in range(4) for z in range(n_gx)
    ]
    across = [(0, 1), (1, 0)]
    diagonal = [
        ((m * n_gx + z) * 2 + y, (m * n_gx + (z + step(m)) % n_gx) * 2 + 1 - y)
        for m in range(4) for z in range(n_gx) for y in range(2)
    ]

    sib = lax.ppermute(prior_sample_set, "mem", pair).reshape(local * layers * rows, columns)
    count = observed_cells.shape[-1]
    vmem, hbm = pl.BlockSpec(memory_space=pltpu.VMEM), pl.BlockSpec(memory_space=pltpu.HBM)
    own, wind, obs, same_out, other_out = pl.pallas_call(
        functools.partial(fetch_kernel, s),
        out_shape=(
            shaped((local * layers * rows, columns), f32),
            shaped((2 * layers * rows, columns), f32),
            shaped((2 * OCTET, count), f32),
            shaped((s.halo_rows + 3 * s.wind_rows, LANES), f32),
            shaped((s.halo_rows, LANES), f32),
        ),
        in_specs=[hbm] * 5,
        out_specs=(vmem, vmem, vmem, vmem, vmem),
        scratch_shapes=[
            pltpu.VMEM((1, count), jnp.int32),
            pltpu.VMEM((1, count), f32),
            pltpu.VMEM((1, count), f32),
            pltpu.VMEM((s.wind_rows, LANES), f32),
            pltpu.SemaphoreType.DMA((4 + PRIOR_COPIES,)),
        ],
        compiler_params=pltpu.CompilerParams(vmem_limit_bytes=VMEM_GRANT),
    )(
        *(
            pltpu.with_memory_space_constraint(x, pltpu.HBM)
            for x in (
                prior_sample_set.reshape(local * layers * rows, columns),
                flow_speeds.reshape(2 * layers * rows, columns),
                observed_cells.reshape(1, count),
                observed_values.reshape(1, count),
                error_variance.reshape(1, count),
            )
        )
    )
    obs_sib = lax.ppermute(obs, "mem", pair)

    field_shape = shaped((layers * DOMAIN * EXTENT, LANES), f32)
    winds_shape = shaped((2 * layers * DOMAIN * EXTENT, LANES), f32)
    same = lax.ppermute(same_out.astype(jnp.float16), ("mem", "gx"), along).astype(f32)
    other = lax.ppermute(other_out.astype(jnp.float16), ("mem", "gx"), along_other).astype(f32)
    field, side_out, corner_out = vmem_call(
        functools.partial(pack_edges_kernel, s),
        (
            field_shape,
            shaped((s.side_rows + 2 * OCTET + layers * 2 * HALO * HALO, LANES), bf16),
            shaped((s.corner_rows + 2 * OCTET, LANES), bf16),
        ),
        [],
        own, sib, wind, same_out,
    )
    winds = vmem_call(functools.partial(spread_winds_kernel, s), winds_shape, [], wind)
    side = lax.ppermute(side_out, "gy", across)
    corner = lax.ppermute(corner_out, ("mem", "gx", "gy"), diagonal)
    first, second = vmem_call(functools.partial(inner_kernel, s), (field_shape, field_shape), [], field, winds)
    field, winds, first, second = vmem_call(
        functools.partial(ends_kernel, s),
        (field_shape, winds_shape, field_shape, field_shape),
        [((layers * DOMAIN * EXTENT, LANES), f32)] * 2,
        field, winds, first, second, side,
        aliases={0: 0, 1: 1, 2: 2, 3: 3},
    )
    piece = shaped((s.piece_rows, s.members), bf16)
    piece_obs = shaped((s.piece_rows + 3 * s.obs_rows, s.members), bf16)
    *pieces, _, _, _, _ = vmem_call(
        functools.partial(forecast_kernel, s),
        (piece, piece_obs, piece, piece, field_shape, winds_shape, field_shape, field_shape),
        [],
        field, winds, first, second, same, other, corner, obs_sib,
        aliases={0: 4, 1: 5, 2: 6, 3: 7},
    )

    def flip(d):
        dx, dy = d // 2, d % 2
        return [((m * 2 + y), ((m ^ (2 * dx)) * 2 + (y ^ dy))) for m in range(4) for y in range(2)]

    def exchange(parts):
        arrived = [parts[0]]
        for d in range(1, 4):
            arrived.append(lax.ppermute(parts[d], ("mem", "gy"), flip(d)))
        return arrived

    total = 4 * local
    send, perturbation, weights, mean = vmem_call(
        functools.partial(analysis_kernel, s, total),
        (
            shaped((4, layers, local, LANES), bf16),
            shaped((layers * 2 * LANES, total), bf16),
            shaped((total, total), bf16),
            shaped((OCTET, layers * 2 * LANES), f32),
        ),
        [],
        *exchange(pieces), obs,
    )
    received = lax.ppermute(send, "mem", pair)
    answer = shaped((2, layers, local, LANES), bf16)
    answers = vmem_call(
        functools.partial(answer_kernel, s), (answer, answer, answer, answer), [], perturbation, weights, mean
    )
    answers = vmem_call(
        join_kernel, (answer, answer, answer, answer), [], received, *answers, aliases={1 + d: d for d in range(4)}
    )
    return pl.pallas_call(
        functools.partial(place_rows_kernel, s),
        out_shape=shaped((local, layers, rows, columns), bf16),
        in_specs=[vmem] * 4,
        out_specs=hbm,
        scratch_shapes=[
            pltpu.VMEM((local * layers * rows, LANES), f32),
            pltpu.VMEM((local, layers, rows, columns), bf16),
            pltpu.SemaphoreType.DMA((local // (2 * OCTET),)),
        ],
        compiler_params=pltpu.CompilerParams(vmem_limit_bytes=VMEM_GRANT),
    )(*exchange(answers))


def on_device(prior_sample_set, flow_speeds, observed_cells, observed_values, error_variance):
    local, _, rows, columns = prior_sample_set.shape
    suits = (
        lax.axis_size("mem") == 4
        and lax.axis_size("gy") == 2
        and rows == 2 * HALO
        and columns == LANES
        and observed_cells.shape[-2] == 1
        and 2 * local == LANES
        and observed_cells.shape[-1] == LANES
    )
    form = on_device_tile if suits else on_device_general
    return form(prior_sample_set, flow_speeds, observed_cells, observed_values, error_variance)


def solution(mesh):
    in_specs = (
        P("mem", None, "gx", "gy"),
        P(None, None, "gx", "gy"),
        P("gx", "gy", "mem", None, None),
        P("gx", "gy", "mem", None, None),
        P("gx", "gy", "mem", None, None),
    )
    out_specs = P("mem", None, "gx", "gy")
    return jax.shard_map(
        on_device, mesh=mesh, in_specs=in_specs, out_specs=out_specs, check_vma=False
    )
```

```python
import functools

import jax
import jax.numpy as jnp
from jax import lax
from jax.experimental import pallas as pl
from jax.experimental.pallas import tpu as pltpu
from jax.sharding import PartitionSpec as P


ROOT_STEPS = 4


diffusion = 0.1
coupling = 0.2


def with_halo(block, sides, width):
    for axis, dim in sides:
        count = lax.axis_size(axis)
        forward = [(i, i + 1) for i in range(count - 1)]
        forward.append((count - 1, 0))
        backward = [(target, source) for source, target in forward]
        low = lax.ppermute(
            lax.slice_in_dim(block, block.shape[dim] - width, None, axis=dim), axis, forward
        )
        high = lax.ppermute(lax.slice_in_dim(block, 0, width, axis=dim), axis, backward)
        block = jnp.concatenate([low, block, high], axis=dim)
    return block


def tendency(model_mesh_field, wind_x, wind_y):
    centre = model_mesh_field[:, :, 1:-1, 1:-1]
    north = model_mesh_field[:, :, 2:, 1:-1]
    south = model_mesh_field[:, :, :-2, 1:-1]
    east = model_mesh_field[:, :, 1:-1, 2:]
    west = model_mesh_field[:, :, 1:-1, :-2]
    layer_mean = jnp.mean(centre, axis=1, keepdims=True)
    return (
        -0.5 * wind_x * (north - south)
        - 0.5 * wind_y * (east - west)
        + diffusion * (north + south + east + west - 4.0 * centre)
        + coupling * (layer_mean - centre)
    )


def crop_margin(array, width):
    return array[:, :, width : array.shape[2] - width, width : array.shape[3] - width]


def deep_step(model_mesh_field, wind_pad):
    padded = with_halo(model_mesh_field, (("gx", 2), ("gy", 3)), 4)
    wind_three = crop_margin(wind_pad, 1)
    wind_two = crop_margin(wind_pad, 2)
    wind_one = crop_margin(wind_pad, 3)
    wind_zero = crop_margin(wind_pad, 4)
    section_one = tendency(padded, wind_three[0], wind_three[1])
    section_two = tendency(crop_margin(padded, 1) + 0.5 * section_one, wind_two[0], wind_two[1])
    section_three = tendency(crop_margin(padded, 2) + 0.5 * section_two, wind_one[0], wind_one[1])
    section_four = tendency(crop_margin(padded, 3) + section_three, wind_zero[0], wind_zero[1])
    return (
        crop_margin(padded, 4)
        + (
            crop_margin(section_one, 3)
            + 2.0 * crop_margin(section_two, 2)
            + 2.0 * crop_margin(section_three, 1)
            + section_four
        )
        / 6.0
    )


def transform_device(weights, rolled):
    return jnp.einsum("qik,ilsqc->klsqc", weights, rolled, preferred_element_type=jnp.float32)


def analyze(strip_block, cells, values, errors, transform):
    realization_vectors, layer_stack, rows, width = strip_block.shape
    patches, count = cells.shape
    patch = width // patches
    highest = lax.Precision.HIGHEST
    mean_field = jnp.mean(strip_block, axis=0, dtype=jnp.float32)
    layer_of = cells // (rows * patch)
    row_of = cells // patch % rows
    column = cells % patch
    starts = (jnp.arange(patches, dtype=jnp.int32) * patch)[:, None]
    flat_index = layer_of * (rows * width) + row_of * width + starts + column
    picked = jnp.take(
        strip_block.reshape(realization_vectors, layer_stack * rows * width),
        flat_index.reshape(-1),
        axis=1,
    )
    base = jnp.take(mean_field.reshape(-1), flat_index.reshape(-1)).reshape(patches, count)
    spread = picked.astype(jnp.float32).reshape(realization_vectors, patches, count) - base[None]
    innovation = values - base
    offset = column.astype(jnp.float32) - 0.5 * (patch - 1)
    spread_parts = []
    innovation_parts = []
    for shift in (-1, 0, 1):
        distance = (shift * patch + jnp.roll(offset, -shift, axis=0)) / patch
        scale = jnp.sqrt(jnp.exp(-0.5 * distance * distance) / jnp.roll(errors, -shift, axis=0))
        spread_parts.append(jnp.roll(spread, -shift, axis=1) * scale[None])
        innovation_parts.append(jnp.roll(innovation, -shift, axis=0) * scale)
    scaled = jnp.concatenate(spread_parts, axis=2)
    scaled_innovation = jnp.concatenate(innovation_parts, axis=1)
    identity = jnp.eye(realization_vectors, dtype=jnp.float32)
    gram = (
        jnp.einsum("kpj,ipj->pki", scaled, scaled, precision=highest)
        + (realization_vectors - 1.0) * identity
    )
    frob = jnp.sqrt(jnp.sum(gram * gram, axis=(1, 2)))
    current = gram / frob[:, None, None]
    root = jnp.broadcast_to(identity, gram.shape)
    for _ in range(ROOT_STEPS):
        middle = 1.5 * identity - 0.5 * jnp.einsum("pab,pbc->pac", root, current, precision=highest)
        current = jnp.einsum("pab,pbc->pac", current, middle, precision=highest)
        root = jnp.einsum("pab,pbc->pac", middle, root, precision=highest)
    projected = jnp.einsum("kpj,pj->pk", scaled, scaled_innovation, precision=highest)
    once = jnp.einsum("pab,pb->pa", root, projected, precision=highest)
    twice = jnp.einsum("pab,pb->pa", root, once, precision=highest)
    mean_weights = twice / frob[:, None]
    weights = (
        jnp.sqrt(realization_vectors - 1.0) * root / jnp.sqrt(frob)[:, None, None]
        + mean_weights[:, :, None]
    ).astype(jnp.bfloat16)
    perturbation = (strip_block - mean_field[None]).astype(jnp.bfloat16)
    rolled = jnp.roll(perturbation, -(patch // 2), axis=3).reshape(
        realization_vectors, layer_stack, rows, patches, patch
    )
    first = transform(weights, rolled)
    second = transform(jnp.roll(weights, -1, axis=0), rolled)
    position = (jnp.arange(patch, dtype=jnp.float32) + 0.5) / patch
    increment = ((1.0 - position) * first + position * second).reshape(
        realization_vectors, layer_stack, rows, width
    )
    return (jnp.roll(increment, patch // 2, axis=3) + mean_field[None]).astype(jnp.bfloat16)


def on_device_general(prior_sample_set, flow_speeds, observed_cells, observed_values, error_variance):
    member_group_count = lax.axis_size("mem")
    northward_group_count = lax.axis_size("gy")
    local_member_states, layer_stack, rows_x, column_count_north = prior_sample_set.shape
    band_row_count = rows_x // (member_group_count * northward_group_count)
    all_members = local_member_states * member_group_count
    model_mesh_field = prior_sample_set
    wind_pad = with_halo(flow_speeds, (("gx", 2), ("gy", 3)), 4)
    model_mesh_field = deep_step(model_mesh_field, wind_pad)
    advance_sample_set = model_mesh_field.astype(jnp.bfloat16)
    flattened_realizations = advance_sample_set.reshape(
        local_member_states,
        layer_stack,
        northward_group_count,
        member_group_count,
        band_row_count,
        column_count_north,
    )
    flattened_realizations = flattened_realizations.transpose(3, 2, 0, 1, 4, 5).reshape(
        member_group_count * northward_group_count,
        local_member_states,
        layer_stack,
        band_row_count,
        column_count_north,
    )
    received = lax.all_to_all(
        flattened_realizations, ("mem", "gy"), split_axis=0, concat_axis=0, tiled=True
    )
    received = received.reshape(
        member_group_count,
        northward_group_count,
        local_member_states,
        layer_stack,
        band_row_count,
        column_count_north,
    )
    columns = received.transpose(0, 2, 3, 4, 1, 5).reshape(
        all_members, layer_stack, band_row_count, northward_group_count * column_count_north
    )
    cells = observed_cells.reshape(observed_cells.shape[-2], observed_cells.shape[-1])
    values = observed_values.reshape(observed_values.shape[-2], observed_values.shape[-1])
    errors = error_variance.reshape(error_variance.shape[-2], error_variance.shape[-1])
    analysed = analyze(columns, cells, values, errors, transform_device)
    outgoing = analysed.reshape(
        member_group_count,
        local_member_states,
        layer_stack,
        band_row_count,
        northward_group_count,
        column_count_north,
    )
    outgoing = outgoing.transpose(0, 4, 1, 2, 3, 5).reshape(
        member_group_count * northward_group_count,
        local_member_states,
        layer_stack,
        band_row_count,
        column_count_north,
    )
    returned = lax.all_to_all(outgoing, ("mem", "gy"), split_axis=0, concat_axis=0, tiled=True)
    returned = returned.reshape(
        member_group_count,
        northward_group_count,
        local_member_states,
        layer_stack,
        band_row_count,
        column_count_north,
    )
    return returned.transpose(2, 3, 1, 0, 4, 5).reshape(
        local_member_states, layer_stack, rows_x, column_count_north
    )


LANES = 128
HALO = 4
OCTET = 8
GROUP = 32
DOMAIN = 3 * HALO
TOGETHER = 9
EXTENT = LANES + 2 * OCTET
VMEM_GRANT = 24 << 20
LARGEST = 6.0
WIDENING = 11.06 / LARGEST
PRIOR_COPIES = 4
STAGE_FACTORS = (1.0 / 4.0, 1.0 / 3.0, 1.0 / 2.0, 1.0)


def split_two(x):
    high = x.astype(jnp.bfloat16)
    return high, (x - high.astype(jnp.float32)).astype(jnp.bfloat16)


def split_three(x):
    high = x.astype(jnp.bfloat16)
    rest = x - high.astype(jnp.float32)
    middle = rest.astype(jnp.bfloat16)
    return high, middle, (rest - middle.astype(jnp.float32)).astype(jnp.bfloat16)


def tile_row(odd, j):
    return jnp.where(odd == 1, DOMAIN - 1 - j, j - HALO)


def domain_row(odd, row):
    return jnp.where(odd == 1, DOMAIN - 1 - row, row + HALO)


class Sizes:
    def __init__(self, local, layers, rows):
        self.local = local
        self.layers = layers
        self.rows = rows
        self.members = 2 * local
        self.per_member = layers * rows
        self.halo_rows = HALO * LANES
        self.wind_rows = 2 * layers * HALO
        self.side_rows = layers * 2 * HALO * OCTET
        self.corner_rows = layers * HALO * OCTET
        self.piece_rows = layers * LANES
        self.obs_rows = 2 * OCTET

    def field_at(self, layer, j):
        return (layer * DOMAIN + j) * EXTENT

    def wind_at(self, part, layer, j):
        return ((part * self.layers + layer) * DOMAIN + j) * EXTENT


def columns_first(s, odd, own_ref, sib_ref, layer, j):
    start = layer * s.rows + tile_row(odd, j)
    parts = [ref[pl.ds(start, s.local, stride=s.per_member), :] for ref in (own_ref, sib_ref)]
    return jnp.concatenate(parts, axis=0).T


def wind_scale(odd, value):
    half = 0.5 / diffusion
    sign = jnp.where(odd == 1, -half, half)
    row = lax.broadcasted_iota(jnp.int32, value.shape, 0)
    return value * jnp.where(row < value.shape[0] // 2, sign, half)


def widened(u):
    v = WIDENING * jnp.abs(u)
    series = v * (1.0 + v * (1.0 / 2.0) * (1.0 + v * (1.0 / 3.0) * (1.0 + v * (1.0 / 4.0))))
    g = jnp.where(v < 0.05, series, jnp.exp(v) - 1.0)
    return jnp.where(u < 0.0, -g, g)


def narrowed(w):
    g = jnp.abs(w)
    series = g * (1.0 - g * (1.0 / 2.0 - g * (1.0 / 3.0 - g * (1.0 / 4.0 - g * (1.0 / 5.0)))))
    u = jnp.where(g < 0.05, series, jnp.log(1.0 + g)) * (1.0 / WIDENING)
    return jnp.where(w < 0.0, -u, u)


def fetch_kernel(
    s, prior_ref, wind_ref, cells_ref, values_ref, errors_ref,
    own_ref, wind_out_ref, obs_ref, same_ref, other_ref,
    cells_vmem, values_vmem, errors_vmem, rows_ref, sems,
):
    odd = lax.rem(lax.axis_index("mem"), 2)
    copies = [
        pltpu.make_async_copy(source, target, sems.at[i])
        for i, (source, target) in enumerate(
            (
                (cells_ref, cells_vmem), (values_ref, values_vmem), (errors_ref, errors_vmem),
                (wind_ref, wind_out_ref),
            )
        )
    ]
    share = own_ref.shape[0] // PRIOR_COPIES
    for i in range(PRIOR_COPIES):
        part = pl.ds(i * share, share)
        copies.append(pltpu.make_async_copy(prior_ref.at[part], own_ref.at[part], sems.at[4 + i]))
    for copy in copies[4:] + copies[:4]:
        copy.start()
    obs_ref[...] = jnp.zeros_like(obs_ref)
    for copy in copies[:4]:
        copy.wait()
    obs_ref[0:1, :] = cells_vmem[...].astype(jnp.float32)
    obs_ref[1:2, :] = values_vmem[...]
    obs_ref[2:3, :] = errors_vmem[...]
    for block in range(2 * s.layers):
        for j in range(HALO):
            row = block * s.rows + tile_row(odd, 2 * HALO + j)
            rows_ref[pl.ds(block * HALO + j, 1), :] = wind_out_ref[pl.ds(row, 1), :]
    for i, part in enumerate(split_three(wind_scale(odd, rows_ref[...]))):
        same_ref[pl.ds(s.halo_rows + i * s.wind_rows, s.wind_rows), :] = part.astype(jnp.float32)
    for copy in copies[4:]:
        copy.wait()
    for parity, out_ref in ((odd, same_ref), (1 - odd, other_ref)):
        for j in range(HALO):
            row = tile_row(parity, 2 * HALO + j)
            parts = [own_ref[pl.ds(layer * s.rows + row, s.local, stride=s.per_member), :] for layer in range(s.layers)]
            value = jnp.concatenate(parts, axis=0).T
            out_ref[pl.ds(j * LANES, LANES), :] = widened(value) if j == HALO - 1 else value


def spread(parts, rows, targets, store):
    stacked = jnp.concatenate(parts, axis=0)
    turned = stacked.T
    source = lax.broadcasted_iota(jnp.int32, (stacked.shape[0], LANES), 0)
    for first, second in zip(targets[::2], targets[1::2], strict=True):
        chosen = [jnp.where(lax.rem(source, rows) == row, 1.0, 0.0) for row in (first, second)]
        both = dot(turned, jnp.concatenate(chosen, axis=1).astype(jnp.bfloat16), ((1,), (0,)))
        store(first, both[:, :LANES])
        store(second, both[:, LANES:])


def column_ends(x):
    turned = padded_rows(x).T
    return jnp.concatenate([turned[LANES - HALO :], turned[:HALO]], axis=0)


def packed_ends(x):
    parts = [part.astype(jnp.float32) for part in split_three(column_ends(x))]
    packed = parts[0] + pltpu.roll(parts[1], GROUP, 1) + pltpu.roll(parts[2], 2 * GROUP, 1)
    return jnp.concatenate([packed, jnp.zeros_like(packed)], axis=0).astype(jnp.bfloat16)


def unpacked_ends(x):
    packed = x.astype(jnp.float32)[: 2 * HALO]
    return packed + pltpu.roll(packed, LANES - GROUP, 1) + pltpu.roll(packed, LANES - 2 * GROUP, 1)


def pack_edges_kernel(s, own_ref, sib_ref, wind_ref, same_ref, field_ref, side_ref, corner_ref):
    odd = lax.rem(lax.axis_index("mem"), 2)
    for layer in range(s.layers):
        rows = []
        for j in range(HALO, DOMAIN):
            value = columns_first(s, odd, own_ref, sib_ref, layer, j)
            field_ref[pl.ds(s.field_at(layer, j) + OCTET, LANES), :] = value
            rows += [value[LANES - HALO :], value[:HALO]]
        count = len(rows) // 2
        high, low = split_two(jnp.concatenate(rows, axis=0))
        side_ref[pl.ds(layer * 2 * HALO * OCTET, 2 * HALO * OCTET), :] = high
        low = low.astype(jnp.float32)
        nearest = [low[i * OCTET + 2 : i * OCTET + 6] for i in range(2 * HALO)]
        at = s.side_rows + 2 * OCTET + layer * 2 * HALO * HALO
        side_ref[pl.ds(at, 2 * HALO * HALO), :] = jnp.concatenate(nearest, axis=0).astype(jnp.bfloat16)
        corner_ref[pl.ds(layer * HALO * OCTET, HALO * OCTET), :] = jnp.concatenate(rows[count:], axis=0).astype(jnp.bfloat16)
    near = [same_ref[pl.ds(s.halo_rows + i * s.wind_rows, s.wind_rows), :] for i in range(3)]
    corner_ref[pl.ds(s.corner_rows, 2 * OCTET), :] = packed_ends(near[0] + near[1] + near[2])
    side_ref[pl.ds(s.side_rows, 2 * OCTET), :] = packed_ends(wind_scale(odd, wind_ref[...]))


def spread_winds_kernel(s, wind_ref, winds_ref):
    odd = lax.rem(lax.axis_index("mem"), 2)
    scaled = wind_scale(odd, wind_ref[...])

    def store(row, value):
        at = s.wind_at(row // s.rows // s.layers, row // s.rows % s.layers, domain_row(odd, row % s.rows))
        winds_ref[pl.ds(pl.multiple_of(at, OCTET) + OCTET, LANES), :] = value

    rows = 2 * s.layers * s.rows
    spread(split_three(scaled), rows, list(range(rows)), store)


def set_wind_edges(winds_ref, ends, row, at):
    value = jnp.broadcast_to(ends[:, row : row + 1], (2 * HALO, LANES))
    winds_ref[pl.ds(at + HALO, HALO), :] = value[:HALO]
    winds_ref[pl.ds(at + OCTET + LANES, HALO), :] = value[HALO:]


def padded_rows(x):
    return jnp.concatenate([x, jnp.zeros((LANES - x.shape[0], LANES), x.dtype)], axis=0)


def set_field_edges(s, field_ref, layer, j, edge):
    at = s.field_at(layer, j)
    field_ref[pl.ds(at + HALO, HALO), :] = edge[:HALO]
    field_ref[pl.ds(at + OCTET + LANES, HALO), :] = edge[HALO:]


def evaluate(s, field_ref, winds_ref, from_ref, stage, start, wanted, emit):
    factor, share = STAGE_FACTORS[stage] * diffusion, coupling / s.layers / diffusion
    own_share = 4.0 + coupling / diffusion - share
    centre = {}
    for j in range(wanted[0] - 1, wanted[1] + 1):
        for layer in range(s.layers):
            centre[layer, j] = from_ref[pl.ds(s.field_at(layer, j) + start, OCTET), :]
    for j in range(*wanted):
        for layer in range(s.layers):
            at = s.field_at(layer, j) + start
            others = sum(centre[k, j] for k in range(s.layers) if k != layer)
            north, south = centre[layer, j + 1], centre[layer, j - 1]
            east, west = from_ref[pl.ds(at + 1, OCTET), :], from_ref[pl.ds(at - 1, OCTET), :]
            along = winds_ref[pl.ds(s.wind_at(0, layer, j) + start, OCTET), :]
            across = winds_ref[pl.ds(s.wind_at(1, layer, j) + start, OCTET), :]
            total = along * (south - north) + across * (west - east)
            total = total + ((north + south) + (east + west))
            total = total + ((others if share == 1.0 else share * others) - own_share * centre[layer, j])
            emit(layer, j, field_ref[pl.ds(at, OCTET), :] + factor * total)


def run_stage(s, field_ref, winds_ref, from_ref, to_ref, stage, wanted):
    def step(i, carry):
        for k in range(TOGETHER):
            start = TOGETHER * OCTET * i + OCTET * k

            def emit(layer, j, value):
                to_ref[pl.ds(s.field_at(layer, j) + start, OCTET), :] = value

            evaluate(s, field_ref, winds_ref, from_ref, stage, start, wanted, emit)
        return carry

    lax.fori_loop(0, EXTENT // (TOGETHER * OCTET), step, 0)


def inner_kernel(s, field_ref, winds_ref, first_ref, second_ref):
    refs = (field_ref, first_ref, second_ref, first_ref)
    for stage in range(3):
        wanted = (HALO + 1 + stage, DOMAIN - 1 - stage)
        run_stage(s, field_ref, winds_ref, refs[stage], refs[stage + 1], stage, wanted)


def run_ends_stage(s, field_ref, winds_ref, from_ref, to_ref, stage, wanted):
    def step(i, carry):
        for k in range(2):
            start = LANES * i + OCTET * k

            def emit(layer, j, value):
                to_ref[pl.ds(s.field_at(layer, j) + start, OCTET), :] = value

            evaluate(s, field_ref, winds_ref, from_ref, stage, start, wanted, emit)
        return carry

    lax.fori_loop(0, 2, step, 0)


def ends_kernel(s, _, __, ___, ____, side_ref, field_ref, winds_ref, first_ref, second_ref, ends1_ref, ends2_ref):
    odd = lax.rem(lax.axis_index("mem"), 2)
    for layer in range(s.layers):
        edges = side_ref[pl.ds(layer * 2 * HALO * OCTET, 2 * HALO * OCTET), :].astype(jnp.float32)
        at = s.side_rows + 2 * OCTET + layer * 2 * HALO * HALO
        low = side_ref[pl.ds(at, 2 * HALO * HALO), :].astype(jnp.float32)
        for j in range(HALO, DOMAIN):
            i = j - HALO
            edge = edges[i * OCTET : (i + 1) * OCTET]
            nearest = edge[2:6] + low[i * HALO : (i + 1) * HALO]
            set_field_edges(s, field_ref, layer, j, jnp.concatenate([edge[:2], nearest, edge[6:]], axis=0))
    beside = unpacked_ends(side_ref[pl.ds(s.side_rows, 2 * OCTET), :])
    for block in range(2 * s.layers):
        for row in range(s.rows):
            at = s.wind_at(block // s.layers, block % s.layers, domain_row(odd, row))
            set_wind_edges(winds_ref, beside, block * s.rows + row, pl.multiple_of(at, OCTET))
    refs = (field_ref, ends1_ref, ends2_ref, ends1_ref)
    for stage in range(3):
        wanted = (HALO + 1 + stage, DOMAIN - 1 - stage)
        run_ends_stage(s, field_ref, winds_ref, refs[stage], refs[stage + 1], stage, wanted)
    near = lax.broadcasted_iota(jnp.int32, (OCTET, LANES), 0) < HALO
    for to_ref, from_ref, wanted in (
        (first_ref, ends1_ref, (HALO + 1, HALO + 5)),
        (second_ref, ends2_ref, (HALO + 2, HALO + 4)),
    ):
        for layer in range(s.layers):
            for j in range(*wanted):
                at = s.field_at(layer, j)
                for start, choose in ((0, None), (OCTET, near), (LANES, ~near), (LANES + OCTET, None)):
                    part = pl.ds(at + start, OCTET)
                    value = from_ref[part, :]
                    to_ref[part, :] = value if choose is None else jnp.where(choose, value, to_ref[part, :])


def forecast_kernel(
    s, _, __, ___, ____, same_ref, other_ref, corner_ref, obs_ref,
    out0_ref, out1_ref, out2_ref, out3_ref, field_ref, winds_ref, first_ref, second_ref,
):
    mem = lax.axis_index("mem")
    odd = lax.rem(mem, 2)
    place = (mem // 2) * 2 + lax.axis_index("gy")

    lower = lax.broadcasted_iota(jnp.int32, (LANES, LANES), 1) < s.local
    for j in range(HALO):
        both = []
        for ref in (same_ref, other_ref):
            value = ref[pl.ds(j * LANES, LANES), :]
            both.append(narrowed(value) if j == HALO - 1 else value)
        same, other = both
        layer_fields = (
            jnp.where(lower, same, pltpu.roll(other, s.local, 1)),
            jnp.where(lower, pltpu.roll(same, s.local, 1), other),
        )
        for layer, value in enumerate(layer_fields):
            field_ref[pl.ds(s.field_at(layer, j) + OCTET, LANES), :] = value
    for layer in range(s.layers):
        corner = corner_ref[pl.ds(layer * HALO * OCTET, HALO * OCTET), :].astype(jnp.float32)
        for j in range(HALO):
            set_field_edges(s, field_ref, layer, j, corner[j * OCTET : (j + 1) * OCTET])
    beyond = unpacked_ends(corner_ref[pl.ds(s.corner_rows, 2 * OCTET), :])
    targets = [block * HALO + j for block in range(2 * s.layers) for j in range(1, HALO)]

    def wind_at(row):
        return s.wind_at(row // HALO // s.layers, row // HALO % s.layers, row % HALO)

    for row in targets:
        set_wind_edges(winds_ref, beyond, row, wind_at(row))

    def store(row, value):
        winds_ref[pl.ds(wind_at(row) + OCTET, LANES), :] = value

    near = [same_ref[pl.ds(s.halo_rows + i * s.wind_rows, s.wind_rows), :].astype(jnp.bfloat16) for i in range(3)]
    spread(near, s.wind_rows, targets, store)

    refs = (field_ref, first_ref, second_ref, first_ref)
    for stage in range(3):
        wanted = (1 + stage, HALO + 1 + stage)
        run_stage(s, field_ref, winds_ref, refs[stage], refs[stage + 1], stage, wanted)

    for i, part in enumerate(split_three(obs_ref[...])):
        out1_ref[pl.ds(s.piece_rows + i * s.obs_rows, s.obs_rows), :] = part
    swap_one = jnp.bitwise_xor(jnp.bitwise_and(place, 1), odd) == 1
    swap_two = jnp.bitwise_xor(place // 2, odd) == 1
    outs = (out0_ref, out1_ref, out2_ref, out3_ref)

    def last_group(i):
        results = [{}, {}]
        for k in range(2):
            start = OCTET + 2 * OCTET * i + OCTET * k
            emit = lambda layer, j, value: results[k].update({(layer, j): value})
            evaluate(s, field_ref, winds_ref, first_ref, 3, start, (HALO, 2 * HALO), emit)
        at = pl.multiple_of(2 * OCTET * i, 2 * OCTET)
        for layer in range(s.layers):
            rows = [
                jnp.concatenate([result[layer, HALO + t] for result in results], axis=0).astype(jnp.bfloat16)
                for t in range(HALO)
            ]
            rows = [jnp.where(swap_one, rows[t ^ 1], rows[t]) for t in range(HALO)]
            rows = [jnp.where(swap_two, rows[t ^ 2], rows[t]) for t in range(HALO)]
            for d, out_ref in enumerate(outs):
                out_ref[pl.ds(layer * LANES + at, 2 * OCTET), :] = rows[d]

    def last_step(i, carry):
        for k in range(2):
            last_group(2 * i + k)
        return carry

    lax.fori_loop(0, LANES // (4 * OCTET), last_step, 0)


def dot(a, b, contract):
    return lax.dot_general(a, b, (contract, ((), ())), preferred_element_type=jnp.float32)


def beside(*parts):
    return jnp.concatenate(parts, axis=1)


def below(*parts):
    return jnp.concatenate(parts, axis=0)


def dot_split(a, b):
    (a_high, a_low), (b_high, b_low) = split_two(a), split_two(b)
    row = beside(b_high, b_low)
    both = dot(beside(a_high, a_low), below(row, row), ((1,), (0,)))
    return both[:, : b.shape[1]] + both[:, b.shape[1] :]


def root_parts(product, vector, total_members):
    count = product.shape[0]
    size = (count, count)
    diagonal = lax.broadcasted_iota(jnp.int32, size, 0) == lax.broadcasted_iota(jnp.int32, size, 1)

    def total(x):
        return jnp.sum(jnp.sum(x, axis=0, keepdims=True), axis=1, keepdims=True)

    def plus(x, scalar):
        return jnp.where(diagonal, x + scalar, x)

    def twice(matrix, column):
        once = jnp.sum(matrix * column, axis=0, keepdims=True)
        return jnp.sum(matrix * once, axis=1, keepdims=True)

    least = total_members - 1.0
    trace = total(jnp.where(diagonal, product, 0.0))
    square = total(product * product) + (2.0 * least) * trace + least * least * total_members
    inverse = lax.rsqrt(square)
    b = product * inverse
    x = least * inverse
    z = jnp.ones_like(x)
    m = 1.5 - 0.5 * x
    middle = plus(-0.5 * b, m)
    y = plus((0.25 * x - m) * b + 0.25 * dot_split(b, b), -x * m)
    near = plus(m * m * b + dot_split(y, b), m * m * x)
    slope = plus(y, m * m)
    x, z = x * m * m, m
    root = middle
    vector = twice(middle, vector)
    root_slope = jnp.where(diagonal, -0.5, 0.0)
    for step in range(1, ROOT_STEPS):
        m = 1.5 - 0.5 * x
        middle = plus(-0.5 * near, 1.5)
        root_slope = m * root_slope - 0.5 * dot_split(slope, root)
        vector = twice(middle, vector)
        z = m * z
        if step < ROOT_STEPS - 1:
            root = dot_split(middle, root)
            rest = plus(near, -x)
            y = dot_split(near, plus(0.25 * rest, -m))
            slope = m * m * slope + dot_split(y, slope)
            near = m * m * near + dot_split(y, rest)
            x = x * m * m
    return inverse, z, root_slope, vector


def analysis_kernel(
    s, total_members, piece0_ref, piece1_ref, piece2_ref, piece3_ref, obs_ref,
    send_ref, perturbation_ref, weights_ref, mean_ref,
):
    mem, side = lax.axis_index("mem"), lax.axis_index("gy")
    pieces = (piece0_ref, piece1_ref, piece2_ref, piece3_ref)
    width = 2 * LANES
    cells_total = s.layers * width
    inverse_count = 1.0 / total_members
    members = beside(
        *(
            below(*(pieces[2 * dx + dy][layer * LANES : (layer + 1) * LANES] for layer in range(s.layers) for dy in range(2)))
            for dx in range(2)
        )
    )
    mean_row = dot(jnp.ones((OCTET, total_members), jnp.bfloat16), members, ((1,), (1,))) * inverse_count
    mean = dot(members, jnp.ones((total_members, LANES), jnp.bfloat16), ((1,), (0,))) * inverse_count
    perturbation = beside(
        *(
            (members[:, i : i + LANES].astype(jnp.float32) - mean).astype(jnp.bfloat16)
            for i in range(0, total_members, LANES)
        )
    )
    perturbation_ref[...] = perturbation
    mean_ref[...] = mean_row

    count = obs_ref.shape[1]
    far = [piece1_ref[pl.ds(s.piece_rows + i * s.obs_rows, s.obs_rows), :].astype(jnp.float32) for i in range(3)]
    mine = lax.rem(mem, 2) == side
    obs = padded_rows(jnp.where(mine, obs_ref[...], far[0] + far[1] + far[2])).T
    cells = obs[:, 0:1].astype(jnp.int32)
    values, errors = obs[:, 1:2], obs[:, 2:3]
    column = jnp.bitwise_and(cells, width - 1)
    layer_of = jnp.right_shift(cells, width.bit_length() - 1)
    half = jnp.bitwise_xor(jnp.right_shift(column, LANES.bit_length() - 1), side)
    index = layer_of * width + half * LANES + jnp.bitwise_and(column, LANES - 1)
    chosen = jnp.where(lax.broadcasted_iota(jnp.int32, (count, cells_total), 1) == index, 1.0, 0.0)
    picked = dot(chosen.astype(jnp.bfloat16), members, ((1,), (0,)))
    base = jnp.sum(picked, axis=1, keepdims=True) * inverse_count
    offset = column.astype(jnp.float32) - 0.5 * (width - 1)
    weight = jnp.zeros_like(values)
    for shift in (-1, 0, 1):
        distance = (shift * width + offset) / width
        weight = weight + jnp.exp(-0.5 * distance * distance) / errors
    scale = jnp.sqrt(weight)
    scaled = (picked - base) * scale
    innovation = (values - base) * scale

    high, low = split_two(scaled)
    quarters = dot(below(high, low), below(high, low), ((1,), (1,)))
    halves = quarters[:count] + quarters[count:]
    inverse, z, slope, twice = root_parts(halves[:, :count] + halves[:, count:], innovation, total_members)
    slope_high, slope_low = split_two(slope * inverse)
    both = beside(slope_high, slope_low)
    carried = dot(both, below(high, high), ((1,), (0,))) + dot(both, below(low, low), ((1,), (0,)))
    carried_high, carried_low = split_two(carried)
    turned = below(high, low)
    spread_part = dot(turned, below(carried_high, carried_high), ((0,), (0,)))
    spread_part = spread_part + dot(turned, below(carried_low, carried_low), ((0,), (0,)))
    mean_weights = jnp.sum(scaled * twice, axis=0, keepdims=True) * inverse
    size = (total_members, total_members)
    diagonal = lax.broadcasted_iota(jnp.int32, size, 0) == lax.broadcasted_iota(jnp.int32, size, 1)
    full = jnp.where(diagonal, spread_part + z, spread_part)
    weights = (full * jnp.sqrt((total_members - 1.0) * inverse) + mean_weights).astype(jnp.bfloat16)
    weights_ref[...] = weights
    for dx in range(2):
        block = answer_rows(s, weights, perturbation, mean_row, dx, 1)
        for dy in range(2):
            for layer in range(s.layers):
                at = (layer * 2 + dy) * LANES
                send_ref[2 * dx + dy, layer] = block[:, at : at + LANES]


def answer_rows(s, weights, perturbation, mean_row, dx, part):
    first = (2 * dx + part) * s.local
    block = dot(weights[first : first + s.local], perturbation, ((1,), (1,))) + mean_row[0:1]
    return block.astype(jnp.bfloat16)


def answer_kernel(s, perturbation_ref, weights_ref, mean_ref, *outs):
    for dx in range(2):
        block = answer_rows(s, weights_ref[...], perturbation_ref[...], mean_ref[...], dx, 0)
        for dy in range(2):
            for layer in range(s.layers):
                at = (layer * 2 + dy) * LANES
                outs[2 * dx + dy][0, layer] = block[:, at : at + LANES]


def join_kernel(received_ref, *refs):
    for d in range(4):
        refs[4 + d][1] = received_ref[d]


def place_rows_kernel(s, *refs):
    pieces, out_ref, rows_ref, packed_ref, sems = refs[:4], refs[4], refs[5], refs[6], refs[7]
    mem = lax.axis_index("mem")
    odd = lax.rem(mem, 2)
    place = (mem // 2) * 2 + lax.axis_index("gy")
    count = 2 * OCTET
    copies = []
    for first in range(0, s.local, count):
        for d in range(4):
            for part, parity in ((0, odd), (1, 1 - odd)):
                row = 4 * parity + jnp.bitwise_xor(place, d)
                for layer in range(s.layers):
                    value = pieces[d][part, layer, first : first + count, :].astype(jnp.float32)
                    start = first * s.per_member + layer * s.rows + row
                    rows_ref[pl.ds(start, count, stride=s.per_member), :] = value
        rows = rows_ref[pl.ds(first * s.per_member, count * s.per_member), :]
        packed_ref[pl.ds(first, count)] = rows.astype(jnp.bfloat16).reshape(count, s.layers, s.rows, LANES)
        copies.append(
            pltpu.make_async_copy(
                packed_ref.at[pl.ds(first, count)], out_ref.at[pl.ds(first, count)], sems.at[first // count]
            )
        )
        copies[-1].start()
    for copy in copies:
        copy.wait()


def vmem_call(kernel, outs, scratch, *args, aliases=None):
    spec = pl.BlockSpec(memory_space=pltpu.VMEM)
    return pl.pallas_call(
        kernel,
        out_shape=outs,
        in_specs=[spec] * len(args),
        out_specs=jax.tree.map(lambda _: spec, outs),
        scratch_shapes=[pltpu.VMEM(shape, dtype) for shape, dtype in scratch],
        input_output_aliases=aliases or {},
        compiler_params=pltpu.CompilerParams(vmem_limit_bytes=VMEM_GRANT),
    )(*args)


def on_device_tile(prior_sample_set, flow_speeds, observed_cells, observed_values, error_variance):
    local, layers, rows, columns = prior_sample_set.shape
    s = Sizes(local, layers, rows)
    n_gx = lax.axis_size("gx")
    f32, bf16 = jnp.float32, jnp.bfloat16
    shaped = jax.ShapeDtypeStruct

    pair = [(m, m ^ 1) for m in range(4)]

    def step(m):
        return 1 if m % 2 == 0 else n_gx - 1

    along = [(m * n_gx + z, m * n_gx + (z + step(m)) % n_gx) for m in range(4) for z in range(n_gx)]
    along_other = [
        (m * n_gx + z, (m ^ 1) * n_gx + (z + step(m ^ 1)) % n_gx) for m in range(4) for z in range(n_gx)
    ]
    across = [(0, 1), (1, 0)]
    diagonal = [
        ((m * n_gx + z) * 2 + y, (m * n_gx + (z + step(m)) % n_gx) * 2 + 1 - y)
        for m in range(4) for z in range(n_gx) for y in range(2)
    ]

    sib = lax.ppermute(prior_sample_set, "mem", pair).reshape(local * layers * rows, columns)
    count = observed_cells.shape[-1]
    vmem, hbm = pl.BlockSpec(memory_space=pltpu.VMEM), pl.BlockSpec(memory_space=pltpu.HBM)
    own, wind, obs, same_out, other_out = pl.pallas_call(
        functools.partial(fetch_kernel, s),
        out_shape=(
            shaped((local * layers * rows, columns), f32),
            shaped((2 * layers * rows, columns), f32),
            shaped((2 * OCTET, count), f32),
            shaped((s.halo_rows + 3 * s.wind_rows, LANES), f32),
            shaped((s.halo_rows, LANES), f32),
        ),
        in_specs=[hbm] * 5,
        out_specs=(vmem, vmem, vmem, vmem, vmem),
        scratch_shapes=[
            pltpu.VMEM((1, count), jnp.int32),
            pltpu.VMEM((1, count), f32),
            pltpu.VMEM((1, count), f32),
            pltpu.VMEM((s.wind_rows, LANES), f32),
            pltpu.SemaphoreType.DMA((4 + PRIOR_COPIES,)),
        ],
        compiler_params=pltpu.CompilerParams(vmem_limit_bytes=VMEM_GRANT),
    )(
        *(
            pltpu.with_memory_space_constraint(x, pltpu.HBM)
            for x in (
                prior_sample_set.reshape(local * layers * rows, columns),
                flow_speeds.reshape(2 * layers * rows, columns),
                observed_cells.reshape(1, count),
                observed_values.reshape(1, count),
                error_variance.reshape(1, count),
            )
        )
    )
    obs_sib = lax.ppermute(obs, "mem", pair)

    field_shape = shaped((layers * DOMAIN * EXTENT, LANES), f32)
    winds_shape = shaped((2 * layers * DOMAIN * EXTENT, LANES), f32)
    same = lax.ppermute(same_out.astype(jnp.float16), ("mem", "gx"), along).astype(f32)
    other = lax.ppermute(other_out.astype(jnp.float16), ("mem", "gx"), along_other).astype(f32)
    field, side_out, corner_out = vmem_call(
        functools.partial(pack_edges_kernel, s),
        (
            field_shape,
            shaped((s.side_rows + 2 * OCTET + layers * 2 * HALO * HALO, LANES), bf16),
            shaped((s.corner_rows + 2 * OCTET, LANES), bf16),
        ),
        [],
        own, sib, wind, same_out,
    )
    winds = vmem_call(functools.partial(spread_winds_kernel, s), winds_shape, [], wind)
    side = lax.ppermute(side_out, "gy", across)
    corner = lax.ppermute(corner_out, ("mem", "gx", "gy"), diagonal)
    first, second = vmem_call(functools.partial(inner_kernel, s), (field_shape, field_shape), [], field, winds)
    field, winds, first, second = vmem_call(
        functools.partial(ends_kernel, s),
        (field_shape, winds_shape, field_shape, field_shape),
        [((layers * DOMAIN * EXTENT, LANES), f32)] * 2,
        field, winds, first, second, side,
        aliases={0: 0, 1: 1, 2: 2, 3: 3},
    )
    piece = shaped((s.piece_rows, s.members), bf16)
    piece_obs = shaped((s.piece_rows + 3 * s.obs_rows, s.members), bf16)
    *pieces, _, _, _, _ = vmem_call(
        functools.partial(forecast_kernel, s),
        (piece, piece_obs, piece, piece, field_shape, winds_shape, field_shape, field_shape),
        [],
        field, winds, first, second, same, other, corner, obs_sib,
        aliases={0: 4, 1: 5, 2: 6, 3: 7},
    )

    def flip(d):
        dx, dy = d // 2, d % 2
        return [((m * 2 + y), ((m ^ (2 * dx)) * 2 + (y ^ dy))) for m in range(4) for y in range(2)]

    def exchange(parts):
        arrived = [parts[0]]
        for d in range(1, 4):
            arrived.append(lax.ppermute(parts[d], ("mem", "gy"), flip(d)))
        return arrived

    total = 4 * local
    send, perturbation, weights, mean = vmem_call(
        functools.partial(analysis_kernel, s, total),
        (
            shaped((4, layers, local, LANES), bf16),
            shaped((layers * 2 * LANES, total), bf16),
            shaped((total, total), bf16),
            shaped((OCTET, layers * 2 * LANES), f32),
        ),
        [],
        *exchange(pieces), obs,
    )
    received = lax.ppermute(send, "mem", pair)
    answer = shaped((2, layers, local, LANES), bf16)
    answers = vmem_call(
        functools.partial(answer_kernel, s), (answer, answer, answer, answer), [], perturbation, weights, mean
    )
    answers = vmem_call(
        join_kernel, (answer, answer, answer, answer), [], received, *answers, aliases={1 + d: d for d in range(4)}
    )
    return pl.pallas_call(
        functools.partial(place_rows_kernel, s),
        out_shape=shaped((local, layers, rows, columns), bf16),
        in_specs=[vmem] * 4,
        out_specs=hbm,
        scratch_shapes=[
            pltpu.VMEM((local * layers * rows, LANES), f32),
            pltpu.VMEM((local, layers, rows, columns), bf16),
            pltpu.SemaphoreType.DMA((local // (2 * OCTET),)),
        ],
        compiler_params=pltpu.CompilerParams(vmem_limit_bytes=VMEM_GRANT),
    )(*exchange(answers))


def on_device(prior_sample_set, flow_speeds, observed_cells, observed_values, error_variance):
    local, _, rows, columns = prior_sample_set.shape
    suits = (
        lax.axis_size("mem") == 4
        and lax.axis_size("gy") == 2
        and rows == 2 * HALO
        and columns == LANES
        and observed_cells.shape[-2] == 1
        and 2 * local == LANES
        and observed_cells.shape[-1] == LANES
    )
    form = on_device_tile if suits else on_device_general
    return form(prior_sample_set, flow_speeds, observed_cells, observed_values, error_variance)


def solution(mesh):
    in_specs = (
        P("mem", None, "gx", "gy"),
        P(None, None, "gx", "gy"),
        P("gx", "gy", "mem", None, None),
        P("gx", "gy", "mem", None, None),
        P("gx", "gy", "mem", None, None),
    )
    out_specs = P("mem", None, "gx", "gy")
    return jax.shard_map(
        on_device, mesh=mesh, in_specs=in_specs, out_specs=out_specs, check_vma=False
    )
```
